32 devices in a mesh: dp: 8 (over z, x), fsdp: 4 (over y, core).
Axes of the slice: x: 2, y: 2, z: 4, core: 2. Of those that a mesh axis runs over, the one named last changes fastest.
Arguments:
- tokens: bfloat16 [16384, 768], P(('dp', 'fsdp')), may hold values from -6 to 6
- cotangent: bfloat16 [16384, 768], P(('dp', 'fsdp')), may hold values from -6 to 6
- lengths: int32 [32], P(('dp', 'fsdp')), may hold values from 128 to 512
- rel_1d: int32 [32, 512, 512], P(('dp', 'fsdp')), may hold values from 0 to 31
- rel_x: int32 [32, 512, 512], P(('dp', 'fsdp')), may hold values from 0 to 63
- rel_y: int32 [32, 512, 512], P(('dp', 'fsdp')), may hold values from 0 to 63
- attn_weights: float32 [3072, 768], P(('dp', 'fsdp')), may hold values from -0.25 to 0.25
- attn_m1: float32 [3072, 768], P(('dp', 'fsdp')), may hold values from -0.00061035156 to 0.00061035156
- attn_m2: float32 [3072, 768], P(('dp', 'fsdp')), may hold values from 1.4106315e-10 to 5.642526e-10
- attn_ema: float32 [3072, 768], P(('dp', 'fsdp')), may hold values from -0.25 to 0.25
- ffn_weights: float32 [6144, 768], P(('dp', 'fsdp')), may hold values from -0.0625 to 0.0625
- ffn_m1: float32 [6144, 768], P(('dp', 'fsdp')), may hold values from -0.00061035156 to 0.00061035156
- ffn_m2: float32 [6144, 768], P(('dp', 'fsdp')), may hold values from 1.4106315e-10 to 5.642526e-10
- ffn_ema: float32 [6144, 768], P(('dp', 'fsdp')), may hold values from -0.0625 to 0.0625
- vectors: float32 [12, 768], replicated, may hold values from -0.8 to 1.5, as said below
- vec_m1: float32 [12, 768], replicated, may hold values from -0.0024414062 to 0.0024414062
- vec_m2: float32 [12, 768], replicated, may hold values from 2.2570104e-09 to 9.028041e-09
- vec_ema: float32 [12, 768], replicated, may hold values from -0.8 to 1.5, as said below
- table: float32 [160, 12], replicated, may hold values from -5 to 5
- tab_m1: float32 [160, 12], replicated, may hold values from -0.0007324219 to 0.0007324219
- tab_m2: float32 [160, 12], replicated, may hold values from 1.4106315e-10 to 5.642526e-10
- tab_ema: float32 [160, 12], replicated, may hold values from -5 to 5
Outputs:
- block_out: bfloat16 [16384, 768], P(('dp', 'fsdp'))
- grad_input: float32 [16384, 768], P(('dp', 'fsdp'))
- grad_norm: float32 [], replicated
- new_attn: float32 [3072, 768], P(('dp', 'fsdp'))
- new_attn_m1: float32 [3072, 768], P(('dp', 'fsdp'))
- new_attn_m2: float32 [3072, 768], P(('dp', 'fsdp'))
- new_attn_ema: float32 [3072, 768], P(('dp', 'fsdp'))
- new_ffn: float32 [6144, 768], P(('dp', 'fsdp'))
- new_ffn_m1: float32 [6144, 768], P(('dp', 'fsdp'))
- new_ffn_m2: float32 [6144, 768], P(('dp', 'fsdp'))
- new_ffn_ema: float32 [6144, 768], P(('dp', 'fsdp'))
- new_vectors: float32 [12, 768], replicated
- new_vec_m1: float32 [12, 768], replicated
- new_vec_m2: float32 [12, 768], replicated
- new_vec_ema: float32 [12, 768], replicated
- new_table: float32 [160, 12], replicated
- new_tab_m1: float32 [160, 12], replicated
- new_tab_m2: float32 [160, 12], replicated
- new_tab_ema: float32 [160, 12], replicated
- vec_grad: float32 [12, 768], replicated
The draws below stay inside these ranges and needn't reach their ends.
Inputs may be any that keep to these rules, and one draw needn't show every extreme that they name: `vectors`: rows 0 and 2 lie in 0.5 to 1.5. `vec_ema`: rows 0 and 2 lie in 0.5 to 1.5.
All inputs are finite; a program needn't handle non-finite values.
Results may differ from the reference program's by a relative error of at most 0.017.
Values may be sent and summed in bfloat16 or wider, within the bound.
No kernel may reach another device: no remote copies, remote signals or barrier semaphores. Data moves between devices by JAX's collectives and lax.ppermute only.
A program may use at most 128 MiB of HBM per device.

```python
import math
import jax
import jax.numpy as jnp
from jax import lax

D = 768
H = 12
HD = 64
FF = 3072
B1 = 32
BX = 64
SEQ = 512
STEP = 10
PAGES = 32
TOKENS = 16384
BUCKETS = 160
VROWS = 12


def uniform_rows(key, row_scales):
    spread = jax.random.uniform(key, (row_scales.shape[0], D), jnp.float32, -1.0, 1.0)
    return spread * (jnp.sqrt(3.0) * row_scales)[:, None]


def attn_like(key):
    row_ids = jnp.arange(4 * D)
    row_scales = jnp.where(row_ids < 3 * D, float(D) ** (-0.5), float(D // 16) ** (-0.5)).astype(jnp.float32)
    return uniform_rows(key, row_scales)


def ffn_like(key):
    row_ids = jnp.arange(2 * FF)
    row_scales = jnp.where(row_ids < FF, float(D) ** (-0.5), float(FF) ** (-0.5)).astype(jnp.float32)
    return uniform_rows(key, row_scales)


def vector_like(key):
    spread = jax.random.uniform(key, (VROWS, D), jnp.float32, -1.0, 1.0)
    row_ids = jnp.arange(VROWS)[:, None]
    is_gain = (row_ids == 0) | (row_ids == 2)
    return jnp.where(is_gain, 1.0 + 0.5 * spread, 0.8 * spread)


def draw_attn_weights(key, part):
    return attn_like(jax.random.fold_in(key, 11))


def draw_attn_ema(key, part):
    return attn_like(jax.random.fold_in(key, 12))


def draw_ffn_weights(key, part):
    return ffn_like(jax.random.fold_in(key, 21))


def draw_ffn_ema(key, part):
    return ffn_like(jax.random.fold_in(key, 22))


def draw_vectors(key, part):
    return vector_like(jax.random.fold_in(key, 31))


def draw_vec_ema(key, part):
    return vector_like(jax.random.fold_in(key, 32))


def touch_ends(entries, own_key, least, high):
    extent = entries.shape
    spot = [jax.random.randint(jax.random.fold_in(own_key, axis), (), 0, extent[axis]) for axis in range(len(extent))]
    entries = entries.at[tuple(spot)].set(least)
    longest = extent.index(max(extent))
    spot[longest] = (spot[longest] + 1) % extent[longest]
    return entries.at[tuple(spot)].set(high)


def block_levels(stream_key, extent, shards, smallest, largest):
    loudness, own = 1.0, jax.random.fold_in(stream_key, 6)
    for position, parts in shards:
        heights = jnp.exp(jax.random.uniform(jax.random.fold_in(own, position), (parts,), jnp.float32, smallest / len(shards), largest / len(shards)))
        loudness = loudness * jnp.repeat(heights, extent[position] // parts).reshape([-1 if axis == position else 1 for axis in range(len(extent))])
    return loudness


def bell_draw(stream_key, extent, width, limit, shards=(), held_as=jnp.bfloat16):
    values = jax.random.normal(stream_key, extent, jnp.float32) * width
    if len(shards) > 0:
        values = block_levels(stream_key, extent, shards, -0.22, 0.18) * values
    return jnp.clip(values, min=-limit, max=limit).astype(held_as)


def setup_inputs(seed: int = 0) -> dict:
    splits = jax.random.split(jax.random.key(seed), 23)
    return {
        "tokens": bell_draw(splits[0], (TOKENS, D), 1.0, 6.0, ((0, 32),)),
        "cotangent": bell_draw(splits[1], (TOKENS, D), 1.0, 6.0, ((0, 32),)),
        "lengths": touch_ends(jax.random.randint(splits[2], (PAGES,), SEQ // 4, SEQ + 1), jax.random.fold_in(splits[2], 1), SEQ // 4, SEQ).astype(jnp.int32),
        "rel_1d": touch_ends(jax.random.randint(splits[3], (PAGES, SEQ, SEQ), 0, B1), jax.random.fold_in(splits[3], 1), 0, B1 - 1).astype(jnp.int32),
        "rel_x": touch_ends(jax.random.randint(splits[4], (PAGES, SEQ, SEQ), 0, BX), jax.random.fold_in(splits[4], 1), 0, BX - 1).astype(jnp.int32),
        "rel_y": touch_ends(jax.random.randint(splits[5], (PAGES, SEQ, SEQ), 0, BX), jax.random.fold_in(splits[5], 1), 0, BX - 1).astype(jnp.int32),
        "attn_weights": draw_attn_weights(jax.random.fold_in(splits[22], 71), 0),
        "attn_m1": bell_draw(splits[7], (4 * D, D), (0.11 / (4 * D * D + 2 * FF * D + VROWS * D + BUCKETS * H) ** 0.5), 0.00061035156, ((0, 32),), jnp.float32),
        "attn_m2": jnp.clip(jnp.exp(math.log(5.642525890969807e-10) - 1.3862944 * jax.random.uniform(splits[8], (4 * D, D), jnp.float32) ** block_levels(splits[8], (4 * D, D), ((0, 32),), -0.2, 0.2)), 1.4106314727424518e-10, 5.642525890969807e-10),
        "attn_ema": draw_attn_ema(jax.random.fold_in(splits[22], 71), 0),
        "ffn_weights": draw_ffn_weights(jax.random.fold_in(splits[22], 71), 0),
        "ffn_m1": bell_draw(splits[11], (2 * FF, D), (0.11 / (4 * D * D + 2 * FF * D + VROWS * D + BUCKETS * H) ** 0.5), 0.00061035156, ((0, 32),), jnp.float32),
        "ffn_m2": jnp.clip(jnp.exp(math.log(5.642525890969807e-10) - 1.3862944 * jax.random.uniform(splits[12], (2 * FF, D), jnp.float32) ** block_levels(splits[12], (2 * FF, D), ((0, 32),), -0.2, 0.2)), 1.4106314727424518e-10, 5.642525890969807e-10),
        "ffn_ema": draw_ffn_ema(jax.random.fold_in(splits[22], 71), 0),
        "vectors": draw_vectors(jax.random.fold_in(splits[22], 71), 0),
        "vec_m1": bell_draw(splits[15], (VROWS, D), (0.44 / (4 * D * D + 2 * FF * D + VROWS * D + BUCKETS * H) ** 0.5), 0.0024414062, (), jnp.float32),
        "vec_m2": jnp.clip(jnp.exp(jax.random.uniform(splits[16], (VROWS, D), jnp.float32, math.log(2.257010356387923e-09), math.log(9.028041425551692e-09))), 2.257010356387923e-09, 9.028041425551692e-09),
        "vec_ema": draw_vec_ema(jax.random.fold_in(splits[22], 71), 0),
        "table": bell_draw(splits[18], (BUCKETS, H), 1.0, 5.0, (), jnp.float32),
        "tab_m1": bell_draw(splits[19], (BUCKETS, H), (0.13 / (4 * D * D + 2 * FF * D + VROWS * D + BUCKETS * H) ** 0.5), 0.0007324219, (), jnp.float32),
        "tab_m2": jnp.clip(jnp.exp(jax.random.uniform(splits[20], (BUCKETS, H), jnp.float32, math.log(1.4106314727424518e-10), math.log(5.642525890969807e-10))), 1.4106314727424518e-10, 5.642525890969807e-10),
        "tab_ema": bell_draw(splits[21], (BUCKETS, H), 1.0, 5.0, (), jnp.float32),
    }


NEG_FILL = -1e+30
NORM_EPS = 1e-05
PRECISE = lax.Precision.HIGHEST

@jax.custom_vjp
def low(v):
    return lax.optimization_barrier(v.astype(jnp.bfloat16)).astype(jnp.float32)

@jax.custom_vjp
def low_back(v):
    return v

def low_keep(v):
    return (low(v), None)

def low_pass(kept, grad):
    return (grad,)

def back_keep(v):
    return (v, None)

def back_low(kept, grad):
    return (low(grad),)
low.defvjp(low_keep, low_pass)
low_back.defvjp(back_keep, back_low)

def norm_rows(values, gain_row, shift_row):
    center = values - lax.optimization_barrier(jnp.mean(values, axis=-1, keepdims=True))
    spread = lax.optimization_barrier(jnp.mean(center * center, axis=-1, keepdims=True))
    return center * lax.rsqrt(spread + NORM_EPS) * gain_row + shift_row

def adam_update(weight, moment_one, second, gradient, clip_scale, step_rate, decay_rate, average):
    clipped = gradient * clip_scale
    new_first = 0.9 * moment_one + 0.1 * clipped
    new_second = 0.999 * second + 0.001 * clipped * clipped
    first_hat = new_first / (1.0 - 0.9 ** STEP)
    second_hat = new_second / (1.0 - 0.999 ** STEP)
    new_weight = weight - step_rate * (first_hat / (jnp.sqrt(second_hat) + 1e-08) + decay_rate * weight)
    new_average = 0.8 * average + 0.2 * new_weight
    return (new_weight, new_first, new_second, new_average)

def page_block(x_rows, attn_w, ffn_w, vec_w, tab_w, page_len, one_idx, x_idx, y_idx):
    attn_low = low(attn_w)
    ffn_low = low(ffn_w)
    w_three = attn_low[:3 * D].reshape(3, D, D)
    w_out = attn_low[3 * D:]
    w_first = ffn_low[:FF]
    w_second = ffn_low[FF:]
    projected = jnp.einsum('si,tio->sto', x_rows, w_three, precision=PRECISE)
    queries = low(low_back(projected[:, 0] + vec_w[4])).reshape(SEQ, H, HD)
    key_rows = low(low_back(projected[:, 1])).reshape(SEQ, H, HD)
    value_rows = low(low_back(projected[:, 2] + vec_w[5])).reshape(SEQ, H, HD)
    bias_page = jnp.transpose(tab_w[one_idx] + tab_w[x_idx + B1] + tab_w[y_idx + B1 + BX], (0, 2, 1))
    scores = jnp.einsum('ihd,jhd->ihj', queries, key_rows, precision=PRECISE) * HD ** (-0.5) + bias_page
    scores = low_back(scores)
    scores = jnp.where(jnp.arange(SEQ, dtype=jnp.int32) < page_len, scores, NEG_FILL)
    weights_soft = jax.nn.softmax(scores, axis=-1)
    context = jnp.einsum('ihj,jhd->ihd', low(weights_soft), value_rows, precision=PRECISE).reshape(SEQ, D)
    context = low(low_back(context))
    attn_lin = low_back(jnp.dot(context, w_out, precision=PRECISE) + vec_w[6])
    hidden = norm_rows(x_rows + attn_lin, vec_w[0], vec_w[1])
    pre_act = low_back(jnp.einsum('sd,fd->sf', low(hidden), w_first, precision=PRECISE) + vec_w[8:].reshape(FF))
    act_low = low(jax.nn.gelu(pre_act, approximate=False))
    ffn_out = low_back(jnp.dot(act_low, w_second, precision=PRECISE) + vec_w[7])
    return norm_rows(hidden + ffn_out, vec_w[2], vec_w[3])

def reference(tokens, cotangent, lengths, rel_1d, rel_x, rel_y, attn_weights, attn_m1, attn_m2, attn_ema, ffn_weights, ffn_m1, ffn_m2, ffn_ema, vectors, vec_m1, vec_m2, vec_ema, table, tab_m1, tab_m2, tab_ema):
    x_pages = tokens.astype(jnp.float32).reshape(PAGES, SEQ, D)
    d_pages = cotangent.astype(jnp.float32).reshape(PAGES, SEQ, D)

    def page_step(carry, page_data):
        x_page, d_page, page_len, one_idx, x_idx, y_idx = page_data

        def local_block(x_rows, attn_w, ffn_w, vec_w, tab_w):
            return page_block(x_rows, attn_w, ffn_w, vec_w, tab_w, page_len, one_idx, x_idx, y_idx)
        out_page, pullback = jax.vjp(local_block, x_page, attn_weights, ffn_weights, vectors, table)
        d_x, d_attn, d_ffn, d_vec, d_tab = pullback(d_page)
        sum_attn, sum_ffn, sum_vec, sum_tab = carry
        return ((sum_attn + d_attn, sum_ffn + d_ffn, sum_vec + d_vec, sum_tab + d_tab), (out_page, d_x))
    start = (jnp.zeros((4 * D, D), jnp.float32), jnp.zeros((2 * FF, D), jnp.float32), jnp.zeros((VROWS, D), jnp.float32), jnp.zeros((BUCKETS, H), jnp.float32))
    sums, page_outs = lax.scan(page_step, start, (x_pages, d_pages, lengths, rel_1d, rel_x, rel_y))
    grad_attn, grad_ffn, grad_vec, grad_tab = sums
    out_pages, dx_pages = page_outs
    grad_norm = jnp.sqrt(jnp.sum(grad_attn * grad_attn) + jnp.sum(grad_ffn * grad_ffn) + jnp.sum(grad_vec * grad_vec) + jnp.sum(grad_tab * grad_tab))
    clip_scale = 1.0 / jnp.maximum(grad_norm, 1.0)
    attn_new = adam_update(attn_weights, attn_m1, attn_m2, grad_attn, clip_scale, 0.06, 0.01, attn_ema)
    ffn_new = adam_update(ffn_weights, ffn_m1, ffn_m2, grad_ffn, clip_scale, 0.06, 0.01, ffn_ema)
    vec_new = adam_update(vectors, vec_m1, vec_m2, grad_vec, clip_scale, 0.6, 0.0, vec_ema)
    tab_new = adam_update(table, tab_m1, tab_m2, grad_tab, clip_scale, 0.6, 0.0, tab_ema)
    block_out = out_pages.reshape(TOKENS, D).astype(jnp.bfloat16)
    grad_input = dx_pages.reshape(TOKENS, D)
    return (block_out, grad_input, grad_norm, attn_new[0], attn_new[1], attn_new[2], attn_new[3], ffn_new[0], ffn_new[1], ffn_new[2], ffn_new[3], vec_new[0], vec_new[1], vec_new[2], vec_new[3], tab_new[0], tab_new[1], tab_new[2], tab_new[3], grad_vec * clip_scale)
```

```python
import math

import jax
import jax.numpy as jnp
from jax import lax
from jax.experimental import pallas as pl
from jax.experimental.pallas import tpu as pltpu
from jax.sharding import PartitionSpec as P

D = 768
H = 12
HD = 64
FF = 3072
B1 = 32
BX = 64
SEQ = 512
STEP = 10
BUCKETS = B1 + 2 * BX


NEG_FILL = -1e30
NORM_EPS = 1e-05
BF = jnp.bfloat16
F32 = jnp.float32
NT = (((1,), (1,)), ((), ()))
TN = (((0,), (0,)), ((), ()))
NN = (((1,), (0,)), ((), ()))
ALL = ("dp", "fsdp")


def mm(a, b, dims):
    return lax.dot_general(a, b, dims, preferred_element_type=F32)


def adam_update(weight, moment_one, second, gradient, clip_scale, step_rate, decay_rate, average):
    clipped = gradient * clip_scale
    new_first = 0.9 * moment_one + 0.1 * clipped
    new_second = 0.999 * second + 0.001 * clipped * clipped
    first_hat = new_first / (1.0 - 0.9**STEP)
    second_hat = new_second / (1.0 - 0.999**STEP)
    new_weight = weight - step_rate * (
        first_hat / (jnp.sqrt(second_hat) + 1e-08) + decay_rate * weight
    )
    new_average = 0.8 * average + 0.2 * new_weight
    return (new_weight, new_first, new_second, new_average)


def bias_kernel(len_ref, tab_ref, one_ref, x_ref, y_ref, out_ref):
    length = len_ref[0]
    rows = one_ref.shape[1]
    for r in range(0, rows, 8):
        for c in range(0, SEQ, 128):
            ids = [ref[0, r : r + 8, c : c + 128] for ref in (one_ref, x_ref, y_ref)]
            keep = lax.broadcasted_iota(jnp.int32, (8, 128), 1) + c < length
            for h in range(H):
                total = None
                for t in range(3):
                    line = jnp.broadcast_to(tab_ref[h, t : t + 1, :], (8, 128))
                    got = jnp.take_along_axis(line, ids[t], axis=1, mode="promise_in_bounds")
                    total = got if total is None else total + got
                out_ref[h, r : r + 8, c : c + 128] = jnp.where(keep, total, NEG_FILL)


def page_bias(lengths, table, rel_1d, rel_x, rel_y):
    rows = 64
    lines = table.T
    tab = jnp.stack(
        [
            jnp.pad(lines[:, :B1], ((0, 0), (0, 128 - B1))),
            jnp.pad(lines[:, B1 : B1 + BX], ((0, 0), (0, 128 - BX))),
            jnp.pad(lines[:, B1 + BX :], ((0, 0), (0, 128 - BX))),
        ],
        axis=1,
    )
    ids = pl.BlockSpec((1, rows, SEQ), lambda i, *_: (0, i, 0))
    return pl.pallas_call(
        bias_kernel,
        grid_spec=pltpu.PrefetchScalarGridSpec(
            num_scalar_prefetch=1,
            grid=(SEQ // rows,),
            in_specs=[pl.BlockSpec((H, 3, 128), lambda i, *_: (0, 0, 0)), ids, ids, ids],
            out_specs=pl.BlockSpec((H, rows, SEQ), lambda i, *_: (0, i, 0)),
        ),
        out_shape=jax.ShapeDtypeStruct((H, SEQ, SEQ), F32),
        cost_estimate=pl.CostEstimate(
            flops=20_000_000_000, bytes_accessed=16_000_000, transcendentals=0
        ),
        name="bias",
    )(lengths, tab, rel_1d, rel_x, rel_y)


def head_masks():
    lane = lax.broadcasted_iota(jnp.int32, (1, 2 * HD), 1)
    return (lane < HD, lane >= HD)


def attend_kernel(q_ref, k_ref, v_ref, bias_ref, ctx_ref, p_ref, *, rows):
    zero = jnp.zeros((), BF)
    masks = head_masks()
    keys = [jnp.where(m, k_ref[...], zero) for m in masks]
    vals = [jnp.where(m, v_ref[...], zero) for m in masks]
    for r in range(0, SEQ, rows):
        q = q_ref[r : r + rows, :]
        ctx = None
        for h in range(2):
            scores = mm(q, keys[h], NT) * HD ** (-0.5) + bias_ref[h, r : r + rows, :]
            top = jnp.max(scores, axis=-1, keepdims=True)
            raised = jnp.exp(scores - top)
            total = jnp.sum(raised, axis=-1, keepdims=True)
            soft = (raised * (1.0 / total)).astype(BF)
            p_ref[h, r : r + rows, :] = soft
            part = mm(soft, vals[h], NN)
            ctx = part if ctx is None else ctx + part
        ctx_ref[r : r + rows, :] = ctx.astype(BF)


def lane_block(offset):
    return pl.BlockSpec((SEQ, 2 * HD), lambda i: (0, offset + i))


PAIR_BLOCK = pl.BlockSpec((2, SEQ, SEQ), lambda i: (i, 0, 0))


def attend(qkv, bias):
    n = D // (2 * HD)
    return pl.pallas_call(
        lambda *refs: attend_kernel(*refs, rows=256),
        grid=(n,),
        in_specs=[lane_block(0), lane_block(n), lane_block(2 * n), PAIR_BLOCK],
        out_specs=[lane_block(0), PAIR_BLOCK],
        out_shape=[
            jax.ShapeDtypeStruct((SEQ, D), BF),
            jax.ShapeDtypeStruct((H, SEQ, SEQ), BF),
        ],
        cost_estimate=pl.CostEstimate(
            flops=10_000_000_000, bytes_accessed=22_000_000, transcendentals=3_200_000
        ),
        name="attend",
    )(qkv, qkv, qkv, bias)


def attend_back_kernel(
    q_ref, k_ref, v_ref, p_ref, c_ref, dc_ref, dq_ref, dk_ref, dv_ref, ds_ref, sum_ref, *, rows
):
    zero = jnp.zeros((), BF)
    masks = head_masks()
    keys = [jnp.where(m, k_ref[...], zero) for m in masks]
    vals = [jnp.where(m, v_ref[...], zero) for m in masks]
    scale = HD ** (-0.5)
    q_sum = jnp.zeros((1, 2 * HD), F32)
    for r in range(0, SEQ, rows):
        dc = dc_ref[r : r + rows, :]
        prod = dc.astype(F32) * c_ref[r : r + rows, :].astype(F32)
        dq = None
        for h in range(2):
            soft = p_ref[h, r : r + rows, :]
            inner = jnp.sum(jnp.where(masks[h], prod, 0.0), axis=-1, keepdims=True)
            d_soft = mm(dc, vals[h], NT)
            d_scores = (soft.astype(F32) * (d_soft - inner)).astype(BF)
            ds_ref[h, r : r + rows, :] = d_scores
            part = mm(d_scores, keys[h], NN)
            dq = part if dq is None else dq + part
        dq = (dq * scale).astype(BF)
        dq_ref[r : r + rows, :] = dq
        q_sum = q_sum + jnp.sum(dq.astype(F32), axis=0, keepdims=True)
    flips = (dc_ref[...].astype(F32).T.astype(BF), q_ref[...].astype(F32).T.astype(BF))
    sums = [q_sum]
    for flip, factor, pair_ref, out_ref in (
        (flips[0], 1.0, p_ref, dv_ref),
        (flips[1], scale, ds_ref, dk_ref),
    ):
        parts = [mm(flip[HD * h : HD * h + HD, :], pair_ref[h], NN) for h in range(2)]
        done = (jnp.concatenate(parts, axis=0).T * factor).astype(BF)
        out_ref[...] = done
        sums.append(jnp.sum(done.astype(F32), axis=0, keepdims=True))
    sum_ref[...] = jnp.concatenate(sums[:2] + [jnp.zeros((6, 2 * HD), F32)], axis=0)


def attend_back(qkv, soft, ctx, d_ctx):
    n = D // (2 * HD)
    return pl.pallas_call(
        lambda *refs: attend_back_kernel(*refs, rows=256),
        grid=(n,),
        in_specs=[
            lane_block(0),
            lane_block(n),
            lane_block(2 * n),
            PAIR_BLOCK,
            lane_block(0),
            lane_block(0),
        ],
        out_specs=[
            lane_block(0),
            lane_block(0),
            lane_block(0),
            PAIR_BLOCK,
            pl.BlockSpec((8, 2 * HD), lambda i: (0, i)),
        ],
        out_shape=[jax.ShapeDtypeStruct((SEQ, D), BF)] * 3
        + [jax.ShapeDtypeStruct((H, SEQ, SEQ), BF), jax.ShapeDtypeStruct((8, D), F32)],
        cost_estimate=pl.CostEstimate(
            flops=9_000_000_000, bytes_accessed=16_000_000, transcendentals=0
        ),
        name="attend_back",
    )(qkv, qkv, qkv, soft, ctx, d_ctx)


def table_kernel(one_ref, x_ref, y_ref, ds_ref, out_ref):
    @pl.when(pl.program_id(0) == 0)
    def _():
        out_ref[...] = jnp.zeros_like(out_ref)

    rows = one_ref.shape[1]
    flipped = jnp.swapaxes(ds_ref[...].astype(F32), 0, 1).astype(BF)
    total = None
    for r in range(rows):
        hot = jnp.concatenate(
            [
                (lax.broadcasted_iota(jnp.int32, (size, SEQ), 0) == ref[0, r : r + 1, :])
                .astype(F32)
                .astype(BF)
                for ref, size in ((one_ref, B1), (x_ref, BX), (y_ref, BX))
            ],
            axis=0,
        )
        part = mm(flipped[r], hot, NT)
        total = part if total is None else total + part
    out_ref[...] += total


def table_grad(rel_1d, rel_x, rel_y, d_scores):
    rows = 16
    ids = pl.BlockSpec((1, rows, SEQ), lambda i: (0, i, 0))
    return pl.pallas_call(
        table_kernel,
        grid=(SEQ // rows,),
        in_specs=[ids, ids, ids, pl.BlockSpec((H, rows, SEQ), lambda i: (0, i, 0))],
        out_specs=pl.BlockSpec((H, BUCKETS), lambda i: (0, 0)),
        out_shape=jax.ShapeDtypeStruct((H, BUCKETS), F32),
        cost_estimate=pl.CostEstimate(
            flops=22_000_000_000, bytes_accessed=10_000_000, transcendentals=0
        ),
        name="table_grad",
    )(rel_1d, rel_x, rel_y, d_scores)


def row_mean(values):
    return jnp.mean(values, axis=-1, keepdims=True)


def normal_rows(values):
    center = values - row_mean(values)
    inv = lax.rsqrt(row_mean(center * center) + NORM_EPS)
    return center * inv, inv


def normal_back(normal, inv, grad):
    return inv * (grad - row_mean(grad) - normal * row_mean(grad * normal))


def gelu_parts(u):
    z = jnp.abs(u) * (2.0**-0.5)
    t = 1.0 / (1.0 + 0.3275911 * z)
    tail = jnp.exp(-0.5 * u * u)
    poly = t * (
        0.254829592
        + t * (-0.284496736 + t * (1.421413741 + t * (-1.453152027 + t * 1.061405429)))
    )
    half = 0.5 * poly * tail
    cdf = jnp.where(u < 0, half, 1.0 - half)
    return u * cdf, cdf + u * (tail * (1.0 / math.sqrt(2.0 * math.pi)))


def row_sum(values):
    return jnp.sum(values.astype(F32), axis=0, keepdims=True)


def block_kernel(
    ctx_ref,
    tok_ref,
    cot_ref,
    vec_ref,
    b1_ref,
    wo_ref,
    w1_ref,
    w2_ref,
    out_ref,
    hid_ref,
    act_ref,
    dff_ref,
    du_ref,
    dr_ref,
    dab_ref,
    dctx_ref,
    sum_ref,
    db1_ref,
    slope_ref,
    *,
    wide,
):
    @pl.when(pl.program_id(0) == 0)
    def _():
        sum_ref[...] = jnp.zeros_like(sum_ref)
        db1_ref[...] = jnp.zeros_like(db1_ref)

    vec = [vec_ref[i : i + 1, :] for i in range(8)]
    resid = tok_ref[...].astype(F32) + (mm(ctx_ref[...], wo_ref[...], NN) + vec[6])
    n_one, inv_one = normal_rows(resid)
    hidden = n_one * vec[0] + vec[1]
    hid_low = hidden.astype(BF)
    hid_ref[...] = hid_low
    total = hidden + vec[7]
    for f in range(0, FF, wide):
        part = slice(f, f + wide)
        u = mm(hid_low, w1_ref[part, :], NT) + b1_ref[:, part]
        act, slope = gelu_parts(u)
        act = act.astype(BF)
        act_ref[:, part] = act
        slope_ref[:, part] = slope
        total = total + mm(act, w2_ref[part, :], NN)
    n_two, inv_two = normal_rows(total)
    out_ref[...] = (n_two * vec[2] + vec[3]).astype(BF)
    dy = cot_ref[...].astype(F32)
    d_two = normal_back(n_two, inv_two, dy * vec[2])
    dff = d_two.astype(BF)
    dff_ref[...] = dff
    d_hid = d_two
    for f in range(0, FF, wide):
        part = slice(f, f + wide)
        du = (mm(dff, w2_ref[part, :], NT) * slope_ref[:, part]).astype(BF)
        du_ref[:, part] = du
        db1_ref[:, part] += row_sum(du)
        d_hid = d_hid + mm(du, w1_ref[part, :], NN)
    d_one = normal_back(n_one, inv_one, d_hid * vec[0])
    dr_ref[...] = d_one
    dab = d_one.astype(BF)
    dab_ref[...] = dab
    dctx_ref[...] = mm(dab, wo_ref[...], NT).astype(BF)
    sum_ref[...] += jnp.concatenate(
        [
            row_sum(d_hid * n_one),
            row_sum(d_hid),
            row_sum(dy * n_two),
            row_sum(dy),
            jnp.zeros((2, D), F32),
            row_sum(dab),
            row_sum(dff),
        ],
        axis=0,
    )


def block_pass(ctx, tokens, cotangent, vectors, b_first, w_out, w_first, w_second):
    rows = 128
    by_row = lambda width: pl.BlockSpec((rows, width), lambda i: (i, 0))
    whole = lambda shape: pl.BlockSpec(shape, lambda i: (0, 0), pipeline_mode=pl.Buffered(1))
    count = tokens.shape[0]
    low = lambda width: jax.ShapeDtypeStruct((count, width), BF)
    return pl.pallas_call(
        lambda *refs: block_kernel(*refs, wide=768),
        grid=(count // rows,),
        in_specs=[
            by_row(D),
            by_row(D),
            by_row(D),
            whole((12, D)),
            whole((1, FF)),
            whole((D, D)),
            whole((FF, D)),
            whole((FF, D)),
        ],
        out_specs=[
            by_row(D),
            by_row(D),
            by_row(FF),
            by_row(D),
            by_row(FF),
            by_row(D),
            by_row(D),
            by_row(D),
            pl.BlockSpec((8, D), lambda i: (0, 0)),
            pl.BlockSpec((1, FF), lambda i: (0, 0)),
        ],
        out_shape=[
            low(D),
            low(D),
            low(FF),
            low(D),
            low(FF),
            jax.ShapeDtypeStruct((count, D), F32),
            low(D),
            low(D),
            jax.ShapeDtypeStruct((8, D), F32),
            jax.ShapeDtypeStruct((1, FF), F32),
        ],
        scratch_shapes=[pltpu.VMEM((rows, FF), F32)],
        cost_estimate=pl.CostEstimate(
            flops=20_000_000_000, bytes_accessed=22_000_000, transcendentals=1_600_000
        ),
        name="block_pass",
    )(ctx, tokens, cotangent, vectors, b_first, w_out, w_first, w_second)


def shards(
    tokens,
    cotangent,
    lengths,
    rel_1d,
    rel_x,
    rel_y,
    attn_weights,
    attn_m1,
    attn_m2,
    attn_ema,
    ffn_weights,
    ffn_m1,
    ffn_m2,
    ffn_ema,
    vectors,
    vec_m1,
    vec_m2,
    vec_ema,
    table,
    tab_m1,
    tab_m2,
    tab_ema,
):
    attn_full, ffn_full = (
        lax.all_gather(attn_weights.astype(BF), ALL, axis=0, tiled=True),
        lax.all_gather(ffn_weights.astype(BF), ALL, axis=0, tiled=True),
    )
    w_three, w_out = attn_full[: 3 * D].reshape(3, D, D), attn_full[3 * D :]
    w_first, w_second = ffn_full[:FF], ffn_full[FF:]
    bias = page_bias(lengths, table, rel_1d, rel_x, rel_y)
    add_three = jnp.concatenate([vectors[4], jnp.zeros((D,), F32), vectors[5]])
    qkv = jnp.concatenate([mm(tokens, w_three[t], NN) for t in range(3)], axis=1)
    qkv = (qkv + add_three).astype(BF)
    ctx, soft = attend(qkv, bias)
    (
        block_out,
        hid_low,
        act_low,
        d_ffn,
        d_pre_low,
        d_resid_one,
        d_attn,
        d_context,
        sums,
        grad_bias_first,
    ) = block_pass(
        ctx, tokens, cotangent, vectors, vectors[8:].reshape(1, FF), w_out, w_first, w_second
    )
    grad_ffn = jnp.concatenate(
        [mm(d_pre_low, hid_low, TN).astype(BF), mm(act_low, d_ffn, TN).astype(BF)], axis=0
    )
    dq, dk, dv, d_scores, qv_sums = attend_back(qkv, soft, ctx, d_context)
    d_three = (dq, dk, dv)
    grad_attn = jnp.concatenate(
        [mm(tokens, d, TN).astype(BF) for d in d_three] + [mm(ctx, d_attn, TN).astype(BF)], axis=0
    )
    grad_input = d_resid_one
    for t in range(3):
        grad_input = grad_input + mm(d_three[t], w_three[t], NT)
    grad_table = table_grad(rel_1d, rel_x, rel_y, d_scores).T
    attn_shard, ffn_shard = (
        lax.psum_scatter(grad_attn, ALL, scatter_dimension=0, tiled=True).astype(F32),
        lax.psum_scatter(grad_ffn, ALL, scatter_dimension=0, tiled=True).astype(F32),
    )
    grad_vectors = jnp.concatenate(
        [sums[:4], qv_sums[:2], sums[6:], grad_bias_first.reshape(FF // D, D)], axis=0
    )
    shard_squares = jnp.sum(attn_shard * attn_shard) + jnp.sum(ffn_shard * ffn_shard)
    vec_total, tab_total, square_total = lax.psum(
        (grad_vectors, grad_table, shard_squares), ALL
    )
    grad_norm = jnp.sqrt(
        square_total + jnp.sum(vec_total * vec_total) + jnp.sum(tab_total * tab_total)
    )
    clip_scale = 1.0 / jnp.maximum(grad_norm, 1.0)
    attn_new = adam_update(
        attn_weights, attn_m1, attn_m2, attn_shard, clip_scale, 0.06, 0.01, attn_ema
    )
    ffn_new = adam_update(ffn_weights, ffn_m1, ffn_m2, ffn_shard, clip_scale, 0.06, 0.01, ffn_ema)
    vec_new = adam_update(vectors, vec_m1, vec_m2, vec_total, clip_scale, 0.6, 0.0, vec_ema)
    tab_new = adam_update(table, tab_m1, tab_m2, tab_total, clip_scale, 0.6, 0.0, tab_ema)
    return (
        block_out,
        grad_input,
        grad_norm,
        attn_new[0],
        attn_new[1],
        attn_new[2],
        attn_new[3],
        ffn_new[0],
        ffn_new[1],
        ffn_new[2],
        ffn_new[3],
        vec_new[0],
        vec_new[1],
        vec_new[2],
        vec_new[3],
        tab_new[0],
        tab_new[1],
        tab_new[2],
        tab_new[3],
        vec_total * clip_scale,
    )


def solution(mesh):
    return jax.shard_map(
        shards,
        mesh=mesh,
        in_specs=(
            P(("dp", "fsdp"), None),
            P(("dp", "fsdp"), None),
            P(("dp", "fsdp")),
            P(("dp", "fsdp"), None, None),
            P(("dp", "fsdp"), None, None),
            P(("dp", "fsdp"), None, None),
            P(("dp", "fsdp"), None),
            P(("dp", "fsdp"), None),
            P(("dp", "fsdp"), None),
            P(("dp", "fsdp"), None),
            P(("dp", "fsdp"), None),
            P(("dp", "fsdp"), None),
            P(("dp", "fsdp"), None),
            P(("dp", "fsdp"), None),
            P(),
            P(),
            P(),
            P(),
            P(),
            P(),
            P(),
            P(),
        ),
        out_specs=(
            P(("dp", "fsdp"), None),
            P(("dp", "fsdp"), None),
            P(),
            P(("dp", "fsdp"), None),
            P(("dp", "fsdp"), None),
            P(("dp", "fsdp"), None),
            P(("dp", "fsdp"), None),
            P(("dp", "fsdp"), None),
            P(("dp", "fsdp"), None),
            P(("dp", "fsdp"), None),
            P(("dp", "fsdp"), None),
            P(),
            P(),
            P(),
            P(),
            P(),
            P(),
            P(),
            P(),
            P(),
        ),
        check_vma=False,
    )
```

```python
import math

import jax
import jax.numpy as jnp
from jax import lax
from jax.experimental import pallas as pl
from jax.experimental.pallas import tpu as pltpu
from jax.sharding import PartitionSpec as P

D = 768
H = 12
HD = 64
FF = 3072
B1 = 32
BX = 64
SEQ = 512
STEP = 10
BUCKETS = B1 + 2 * BX


NEG_FILL = -1e30
NORM_EPS = 1e-05
BF = jnp.bfloat16
F32 = jnp.float32
NT = (((1,), (1,)), ((), ()))
TN = (((0,), (0,)), ((), ()))
NN = (((1,), (0,)), ((), ()))
ALL = ("dp", "fsdp")
SPLIT = (4, 2, 2, 2)
BLOCKS = 32
A_ROWS = 4 * D // BLOCKS
F_ROWS = 2 * FF // BLOCKS
HALF = FF // 2
ANY = pl.BlockSpec(memory_space=pl.ANY)


def mm(a, b, dims):
    return lax.dot_general(a, b, dims, preferred_element_type=F32)


def adam_update(weight, moment_one, second, gradient, clip_scale, step_rate, decay_rate, average):
    clipped = gradient * clip_scale
    new_first = 0.9 * moment_one + 0.1 * clipped
    new_second = 0.999 * second + 0.001 * clipped * clipped
    first_hat = new_first / (1.0 - 0.9**STEP)
    second_hat = new_second / (1.0 - 0.999**STEP)
    new_weight = weight - step_rate * (
        first_hat / (jnp.sqrt(second_hat) + 1e-08) + decay_rate * weight
    )
    new_average = 0.8 * average + 0.2 * new_weight
    return (new_weight, new_first, new_second, new_average)


def bias_kernel(len_ref, tab_ref, one_ref, x_ref, y_ref, out_ref):
    length = len_ref[0]
    rows = one_ref.shape[1]
    for r in range(0, rows, 8):
        for c in range(0, SEQ, 128):
            ids = [ref[0, r : r + 8, c : c + 128] for ref in (one_ref, x_ref, y_ref)]
            keep = lax.broadcasted_iota(jnp.int32, (8, 128), 1) + c < length
            for h in range(H):
                total = None
                for t in range(3):
                    line = jnp.broadcast_to(tab_ref[h, t : t + 1, :], (8, 128))
                    got = jnp.take_along_axis(line, ids[t], axis=1, mode="promise_in_bounds")
                    total = got if total is None else total + got
                out_ref[h, r : r + 8, c : c + 128] = jnp.where(keep, total, NEG_FILL)


def page_bias(lengths, table, rel_1d, rel_x, rel_y, parts):
    rows = 64
    lines = table.T
    tab = jnp.stack(
        [
            jnp.pad(lines[:, :B1], ((0, 0), (0, 128 - B1))),
            jnp.pad(lines[:, B1 : B1 + BX], ((0, 0), (0, 128 - BX))),
            jnp.pad(lines[:, B1 + BX :], ((0, 0), (0, 128 - BX))),
        ],
        axis=1,
    )
    count = SEQ // rows // parts
    out = None
    for part in range(parts):
        first = part * count
        ids = pl.BlockSpec((1, rows, SEQ), lambda i, *_, first=first: (0, first + i, 0))
        extra = [] if out is None else [out]
        out = pl.pallas_call(
            lambda *refs: bias_kernel(*refs[:5], refs[-1]),
            grid_spec=pltpu.PrefetchScalarGridSpec(
                num_scalar_prefetch=1,
                grid=(count,),
                in_specs=[pl.BlockSpec((H, 3, 128), lambda i, *_: (0, 0, 0)), ids, ids, ids]
                + [ANY] * len(extra),
                out_specs=pl.BlockSpec(
                    (H, rows, SEQ), lambda i, *_, first=first: (0, first + i, 0)
                ),
            ),
            out_shape=jax.ShapeDtypeStruct((H, SEQ, SEQ), F32),
            input_output_aliases={5: 0} if extra else {},
            cost_estimate=pl.CostEstimate(
                flops=20_000_000_000 // parts,
                bytes_accessed=16_000_000 // parts,
                transcendentals=0,
            ),
            name="bias",
        )(lengths, tab, rel_1d, rel_x, rel_y, *extra)
    return out


def head_masks():
    lane = lax.broadcasted_iota(jnp.int32, (1, 2 * HD), 1)
    return (lane < HD, lane >= HD)


def attend_kernel(q_ref, k_ref, v_ref, bias_ref, ctx_ref, p_ref, *, rows):
    zero = jnp.zeros((), BF)
    masks = head_masks()
    keys = [jnp.where(m, k_ref[...], zero) for m in masks]
    vals = [jnp.where(m, v_ref[...], zero) for m in masks]
    for r in range(0, SEQ, rows):
        q = q_ref[r : r + rows, :]
        ctx = None
        for h in range(2):
            scores = mm(q, keys[h], NT) * HD ** (-0.5) + bias_ref[h, r : r + rows, :]
            top = jnp.max(scores, axis=-1, keepdims=True)
            raised = jnp.exp(scores - top)
            total = jnp.sum(raised, axis=-1, keepdims=True)
            soft = (raised * (1.0 / total)).astype(BF)
            p_ref[h, r : r + rows, :] = soft
            part = mm(soft, vals[h], NN)
            ctx = part if ctx is None else ctx + part
        ctx_ref[r : r + rows, :] = ctx.astype(BF)


def lane_block(offset):
    return pl.BlockSpec((SEQ, 2 * HD), lambda i: (0, offset + i))


PAIR_BLOCK = pl.BlockSpec((2, SEQ, SEQ), lambda i: (i, 0, 0))


def attend(qkv, bias):
    n = D // (2 * HD)
    return pl.pallas_call(
        lambda *refs: attend_kernel(*refs, rows=256),
        grid=(n,),
        in_specs=[lane_block(0), lane_block(n), lane_block(2 * n), PAIR_BLOCK],
        out_specs=[lane_block(0), PAIR_BLOCK],
        out_shape=[
            jax.ShapeDtypeStruct((SEQ, D), BF),
            jax.ShapeDtypeStruct((H, SEQ, SEQ), BF),
        ],
        cost_estimate=pl.CostEstimate(
            flops=10_000_000_000, bytes_accessed=22_000_000, transcendentals=3_200_000
        ),
        name="attend",
    )(qkv, qkv, qkv, bias)


def attend_back_kernel(
    q_ref, k_ref, v_ref, p_ref, c_ref, dc_ref, dq_ref, dk_ref, dv_ref, ds_ref, sum_ref, *, rows
):
    zero = jnp.zeros((), BF)
    masks = head_masks()
    keys = [jnp.where(m, k_ref[...], zero) for m in masks]
    vals = [jnp.where(m, v_ref[...], zero) for m in masks]
    scale = HD ** (-0.5)
    q_sum = jnp.zeros((1, 2 * HD), F32)
    for r in range(0, SEQ, rows):
        dc = dc_ref[r : r + rows, :]
        prod = dc.astype(F32) * c_ref[r : r + rows, :].astype(F32)
        dq = None
        for h in range(2):
            soft = p_ref[h, r : r + rows, :]
            inner = jnp.sum(jnp.where(masks[h], prod, 0.0), axis=-1, keepdims=True)
            d_soft = mm(dc, vals[h], NT)
            d_scores = (soft.astype(F32) * (d_soft - inner)).astype(BF)
            ds_ref[h, r : r + rows, :] = d_scores
            part = mm(d_scores, keys[h], NN)
            dq = part if dq is None else dq + part
        dq = (dq * scale).astype(BF)
        dq_ref[r : r + rows, :] = dq
        q_sum = q_sum + jnp.sum(dq.astype(F32), axis=0, keepdims=True)
    flips = (dc_ref[...].astype(F32).T.astype(BF), q_ref[...].astype(F32).T.astype(BF))
    sums = [q_sum]
    for flip, factor, pair_ref, out_ref in (
        (flips[0], 1.0, p_ref, dv_ref),
        (flips[1], scale, ds_ref, dk_ref),
    ):
        parts = [mm(flip[HD * h : HD * h + HD, :], pair_ref[h], NN) for h in range(2)]
        done = (jnp.concatenate(parts, axis=0).T * factor).astype(BF)
        out_ref[...] = done
        sums.append(jnp.sum(done.astype(F32), axis=0, keepdims=True))
    sum_ref[...] = jnp.concatenate(sums[:2] + [jnp.zeros((6, 2 * HD), F32)], axis=0)


def attend_back(qkv, soft, ctx, d_ctx):
    n = D // (2 * HD)
    return pl.pallas_call(
        lambda *refs: attend_back_kernel(*refs, rows=256),
        grid=(n,),
        in_specs=[
            lane_block(0),
            lane_block(n),
            lane_block(2 * n),
            PAIR_BLOCK,
            lane_block(0),
            lane_block(0),
        ],
        out_specs=[
            lane_block(0),
            lane_block(0),
            lane_block(0),
            PAIR_BLOCK,
            pl.BlockSpec((8, 2 * HD), lambda i: (0, i)),
        ],
        out_shape=[jax.ShapeDtypeStruct((SEQ, D), BF)] * 3
        + [jax.ShapeDtypeStruct((H, SEQ, SEQ), BF), jax.ShapeDtypeStruct((8, D), F32)],
        cost_estimate=pl.CostEstimate(
            flops=9_000_000_000, bytes_accessed=16_000_000, transcendentals=0
        ),
        name="attend_back",
    )(qkv, qkv, qkv, soft, ctx, d_ctx)


def table_kernel(one_ref, x_ref, y_ref, ds_ref, out_ref):
    @pl.when(pl.program_id(0) == 0)
    def _():
        out_ref[...] = jnp.zeros_like(out_ref)

    rows = one_ref.shape[1]
    flipped = jnp.swapaxes(ds_ref[...].astype(F32), 0, 1).astype(BF)
    total = None
    for r in range(rows):
        hot = jnp.concatenate(
            [
                (lax.broadcasted_iota(jnp.int32, (size, SEQ), 0) == ref[0, r : r + 1, :])
                .astype(F32)
                .astype(BF)
                for ref, size in ((one_ref, B1), (x_ref, BX), (y_ref, BX))
            ],
            axis=0,
        )
        part = mm(flipped[r], hot, NT)
        total = part if total is None else total + part
    out_ref[...] += total


def table_grad(rel_1d, rel_x, rel_y, d_scores):
    rows = 16
    ids = pl.BlockSpec((1, rows, SEQ), lambda i: (0, i, 0))
    return pl.pallas_call(
        table_kernel,
        grid=(SEQ // rows,),
        in_specs=[ids, ids, ids, pl.BlockSpec((H, rows, SEQ), lambda i: (0, i, 0))],
        out_specs=pl.BlockSpec((H, BUCKETS), lambda i: (0, 0)),
        out_shape=jax.ShapeDtypeStruct((H, BUCKETS), F32),
        cost_estimate=pl.CostEstimate(
            flops=22_000_000_000, bytes_accessed=10_000_000, transcendentals=0
        ),
        name="table_grad",
    )(rel_1d, rel_x, rel_y, d_scores)


def piece_list(refs):
    found = []
    for core in range(2):
        stack, beside, above, low, high = refs[5 * core : 5 * core + 5]
        for z in range(4):
            found.append((core, z, 0, 0, stack.at[z]))
            found.append((core, z, 1, 0, beside.at[z]))
            found.append((core, z, 0, 1, above.at[z]))
            found.append((core, z, 1, 1, low.at[z] if z < 2 else high.at[z - 2]))
    return found


def qkv_kernel(at_ref, tok_ref, add_ref, *refs):
    pieces, (qkv_ref, all_ref, weight_ref, sems, done) = refs[:10], refs[10:]
    copies = []
    for n, (core, z, x, y, ref) in enumerate(piece_list(pieces)):
        block = (
            ((at_ref[0] ^ z) * 2 + (at_ref[1] ^ x)) * 2 + (at_ref[2] ^ y)
        ) * 2 + (at_ref[3] ^ core)
        spot = pl.ds(pl.multiple_of(block * A_ROWS, A_ROWS), A_ROWS)
        copies.append(pltpu.make_async_copy(ref, weight_ref.at[spot, :], sems.at[n]))
    for copy in copies:
        copy.start()
    for copy in copies:
        copy.wait()
    store = pltpu.make_async_copy(weight_ref, all_ref, done)
    store.start()
    for t in range(3):
        part = slice(D * t, D * t + D)
        qkv_ref[:, part] = (mm(tok_ref[...], weight_ref[part, :], NN) + add_ref[:, part]).astype(BF)
    store.wait()


def project(at, tokens, add_three, pieces):
    count = tokens.shape[0]
    vmem = pl.BlockSpec(memory_space=pltpu.VMEM)
    return pl.pallas_call(
        qkv_kernel,
        in_specs=[pl.BlockSpec(memory_space=pltpu.SMEM), vmem, vmem] + [ANY] * 10,
        out_specs=[vmem, ANY],
        out_shape=[
            jax.ShapeDtypeStruct((count, 3 * D), BF),
            jax.ShapeDtypeStruct((4 * D, D), BF),
        ],
        scratch_shapes=[
            pltpu.VMEM((4 * D, D), BF),
            pltpu.SemaphoreType.DMA((BLOCKS,)),
            pltpu.SemaphoreType.DMA,
        ],
        cost_estimate=pl.CostEstimate(
            flops=5_000_000_000, bytes_accessed=14_000_000, transcendentals=0
        ),
        name="project",
    )(at, tokens, add_three, *pieces)


def grad_ffn_kernel(at_ref, *refs, high):
    wide, slim, outs, (left, right, sems) = refs[:4], refs[4:8], refs[8:12], refs[12:]
    which = (at_ref[0] // 2) ^ high
    for w in range(2):

        @pl.when(which == w)
        def _():
            copies = []
            for i in range(2):
                rows = pl.ds(SEQ * i, SEQ)
                copies.append(
                    pltpu.make_async_copy(wide[2 * w + i], left.at[rows, :], sems.at[2 * i])
                )
                copies.append(
                    pltpu.make_async_copy(slim[2 * w + i], right.at[rows, :], sems.at[2 * i + 1])
                )
            for copy in copies:
                copy.start()
            for copy in copies:
                copy.wait()

    for z in range(2):
        done = mm(left[:, HALF // 2 * z : HALF // 2 * (z + 1)], right[...], TN).astype(BF)
        for q in range(4):
            outs[q][z] = done[F_ROWS * q : F_ROWS * q + F_ROWS, :]


def grad_ffn(at, wide, slim, high):
    shape = jax.ShapeDtypeStruct((2, F_ROWS, D), BF)
    return pl.pallas_call(
        lambda *refs: grad_ffn_kernel(*refs, high=high),
        in_specs=[pl.BlockSpec(memory_space=pltpu.SMEM)] + [ANY] * 8,
        out_specs=[pl.BlockSpec(memory_space=pltpu.VMEM)] * 4,
        out_shape=[shape] * 4,
        scratch_shapes=[
            pltpu.VMEM((2 * SEQ, HALF), BF),
            pltpu.VMEM((2 * SEQ, D), BF),
            pltpu.SemaphoreType.DMA((4,)),
        ],
        cost_estimate=pl.CostEstimate(
            flops=3_500_000_000, bytes_accessed=7_000_000, transcendentals=0
        ),
        name="grad_ffn",
    )(at, *wide, *slim)


def grad_attn_kernel(at_ref, tok_ref, tok_far, ctx_ref, ctx_far, *refs):
    grads, outs, (flip, left, right, sems) = refs[:8], refs[8:15], refs[15:]
    copies = []
    for t in range(4):
        for i in range(2):
            spot = right.at[t, pl.ds(SEQ * i, SEQ), :]
            copies.append(pltpu.make_async_copy(grads[2 * t + i], spot, sems.at[2 * t + i]))
    for copy in copies:
        copy.start()
    for n, (near, far) in enumerate(((tok_ref, tok_far), (ctx_ref, ctx_far))):
        flip[:, :SEQ] = near[...].astype(F32).T.astype(BF)
        flip[:, SEQ:] = far[...].astype(F32).T.astype(BF)
        for q in range(4):
            block = (((at_ref[1] ^ (q // 2)) * 2 + (at_ref[2] ^ (q % 2))) * 2) + at_ref[3]
            spot = pl.ds(pl.multiple_of(block * A_ROWS, A_ROWS), A_ROWS)
            left[n, A_ROWS * q : A_ROWS * q + A_ROWS, :] = flip[spot, :]
    for copy in copies:
        copy.wait()
    own, y_low, y_high, x_low, x_high, far_low, far_high = outs
    for z in range(4):
        which = at_ref[0] ^ z
        done = mm(left[which // 3], right[which], NN).astype(BF)
        rows = [done[A_ROWS * q : A_ROWS * q + A_ROWS, :] for q in range(4)]
        own[z] = rows[0]
        (y_low if z < 2 else y_high)[z % 2] = rows[1]
        (x_low if z < 2 else x_high)[z % 2] = rows[2]
        (far_low if z < 2 else far_high)[z % 2] = rows[3]


def grad_attn(at, tokens, tokens_far, ctx, ctx_far, grads):
    four = jax.ShapeDtypeStruct((4, A_ROWS, D), BF)
    two = jax.ShapeDtypeStruct((2, A_ROWS, D), BF)
    vmem = pl.BlockSpec(memory_space=pltpu.VMEM)
    return pl.pallas_call(
        grad_attn_kernel,
        in_specs=[pl.BlockSpec(memory_space=pltpu.SMEM)] + [vmem] * 4 + [ANY] * 8,
        out_specs=[vmem] * 7,
        out_shape=[four] + [two] * 6,
        scratch_shapes=[
            pltpu.VMEM((D, 2 * SEQ), BF),
            pltpu.VMEM((2, D // 2, 2 * SEQ), BF),
            pltpu.VMEM((4, 2 * SEQ, D), BF),
            pltpu.SemaphoreType.DMA((8,)),
        ],
        cost_estimate=pl.CostEstimate(
            flops=5_000_000_000, bytes_accessed=12_000_000, transcendentals=0
        ),
        name="grad_attn",
    )(at, tokens, tokens_far, ctx, ctx_far, *grads)


def row_mean(values):
    return jnp.mean(values, axis=-1, keepdims=True)


def normal_rows(values):
    center = values - row_mean(values)
    inv = lax.rsqrt(row_mean(center * center) + NORM_EPS)
    return center * inv, inv


def normal_back(normal, inv, grad):
    return inv * (grad - row_mean(grad) - normal * row_mean(grad * normal))


def gelu_parts(u):
    z = jnp.abs(u) * (2.0**-0.5)
    t = 1.0 / (1.0 + 0.3275911 * z)
    tail = jnp.exp(-0.5 * u * u)
    poly = t * (
        0.254829592
        + t * (-0.284496736 + t * (1.421413741 + t * (-1.453152027 + t * 1.061405429)))
    )
    half = 0.5 * poly * tail
    cdf = jnp.where(u < 0, half, 1.0 - half)
    return u * cdf, cdf + u * (tail * (1.0 / math.sqrt(2.0 * math.pi)))


def row_sum(values):
    return jnp.sum(values.astype(F32), axis=0, keepdims=True)


def block_kernel(
    at_ref,
    ctx_ref,
    tok_ref,
    cot_ref,
    vec_ref,
    b1_ref,
    wo_ref,
    *refs,
    wide,
):
    pieces, refs = refs[:10], refs[10:]
    out_ref, hid_ref, act_near, act_far, dff_ref, du_near, du_far = refs[:7]
    dr_ref, dab_ref, dctx_ref, sum_ref, db1_ref, slope_ref, ffn_ref, sems = refs[7:]
    copies = []
    for n, (core, z, x, y, ref) in enumerate(piece_list(pieces)):
        spot = pl.ds(core * HALF + ((z % 2) * 4 + x * 2 + y) * F_ROWS, F_ROWS)
        which = (at_ref[0] // 2) ^ (z // 2)
        copies.append(pltpu.make_async_copy(ref, ffn_ref.at[which, spot, :], sems.at[n]))
    w1_ref, w2_ref = ffn_ref.at[0], ffn_ref.at[1]

    @pl.when(pl.program_id(0) == 0)
    def _():
        for copy in copies:
            copy.start()
        sum_ref[...] = jnp.zeros_like(sum_ref)
        db1_ref[...] = jnp.zeros_like(db1_ref)

    vec = [vec_ref[i : i + 1, :] for i in range(8)]
    resid = tok_ref[...].astype(F32) + (mm(ctx_ref[...], wo_ref[...], NN) + vec[6])
    n_one, inv_one = normal_rows(resid)
    hidden = n_one * vec[0] + vec[1]
    hid_low = hidden.astype(BF)
    hid_ref[...] = hid_low
    total = hidden + vec[7]

    @pl.when(pl.program_id(0) == 0)
    def _():
        for copy in copies:
            copy.wait()

    for f in range(0, FF, wide):
        part = slice(f, f + wide)
        u = mm(hid_low, w1_ref[part, :], NT) + b1_ref[:, part]
        act, slope = gelu_parts(u)
        act = act.astype(BF)
        side = slice(f % HALF, f % HALF + wide)
        (act_near if f < HALF else act_far)[:, side] = act
        slope_ref[:, part] = slope
        total = total + mm(act, w2_ref[part, :], NN)
    n_two, inv_two = normal_rows(total)
    out_ref[...] = (n_two * vec[2] + vec[3]).astype(BF)
    dy = cot_ref[...].astype(F32)
    d_two = normal_back(n_two, inv_two, dy * vec[2])
    dff = d_two.astype(BF)
    dff_ref[...] = dff
    d_hid = d_two
    for f in range(0, FF, wide):
        part = slice(f, f + wide)
        du = (mm(dff, w2_ref[part, :], NT) * slope_ref[:, part]).astype(BF)
        side = slice(f % HALF, f % HALF + wide)
        (du_near if f < HALF else du_far)[:, side] = du
        db1_ref[:, part] += row_sum(du)
        d_hid = d_hid + mm(du, w1_ref[part, :], NN)
    d_one = normal_back(n_one, inv_one, d_hid * vec[0])
    dr_ref[...] = d_one
    dab = d_one.astype(BF)
    dab_ref[...] = dab
    dctx_ref[...] = mm(dab, wo_ref[...], NT).astype(BF)
    sum_ref[...] += jnp.concatenate(
        [
            row_sum(d_hid * n_one),
            row_sum(d_hid),
            row_sum(dy * n_two),
            row_sum(dy),
            jnp.zeros((2, D), F32),
            row_sum(dab),
            row_sum(dff),
        ],
        axis=0,
    )


def block_pass(at, ctx, tokens, cotangent, vectors, b_first, attn_full, pieces):
    rows = 256
    by_row = lambda width: pl.BlockSpec((rows, width), lambda i, *_: (i, 0))
    whole = lambda shape, first=0: pl.BlockSpec(
        shape, lambda i, *_: (first, 0), pipeline_mode=pl.Buffered(1)
    )
    count = tokens.shape[0]
    low = lambda width: jax.ShapeDtypeStruct((count, width), BF)
    return pl.pallas_call(
        lambda *refs: block_kernel(*refs, wide=768),
        grid_spec=pltpu.PrefetchScalarGridSpec(
            num_scalar_prefetch=1,
            grid=(count // rows,),
            in_specs=[
                by_row(D),
                by_row(D),
                by_row(D),
                whole((12, D)),
                whole((1, FF)),
                whole((D, D), 3),
            ]
            + [ANY] * 10,
            out_specs=[
                by_row(D),
                by_row(D),
                by_row(HALF),
                by_row(HALF),
                by_row(D),
                by_row(HALF),
                by_row(HALF),
                by_row(D),
                by_row(D),
                by_row(D),
                pl.BlockSpec((8, D), lambda i, *_: (0, 0)),
                pl.BlockSpec((1, FF), lambda i, *_: (0, 0)),
            ],
            scratch_shapes=[
                pltpu.VMEM((rows, FF), F32),
                pltpu.VMEM((2, FF, D), BF),
                pltpu.SemaphoreType.DMA((BLOCKS,)),
            ],
        ),
        out_shape=[
            low(D),
            low(D),
            low(HALF),
            low(HALF),
            low(D),
            low(HALF),
            low(HALF),
            jax.ShapeDtypeStruct((count, D), F32),
            low(D),
            low(D),
            jax.ShapeDtypeStruct((8, D), F32),
            jax.ShapeDtypeStruct((1, FF), F32),
        ],
        cost_estimate=pl.CostEstimate(
            flops=14_000_000_000, bytes_accessed=22_000_000, transcendentals=1_600_000
        ),
        name="block_pass",
    )(at, ctx, tokens, cotangent, vectors, b_first, attn_full, *pieces)


def swap(array, mask):
    return lax.ppermute(array, ALL, [(i, i ^ mask) for i in range(BLOCKS)])


def tie(array, after):
    return lax.optimization_barrier((array, after))[0]


def plane(stack):
    beside, above = swap(stack, 4), swap(stack, 2)
    low, high = swap(beside[:2], 2), swap(above[2:], 4)
    near = (stack, beside, above, low, high)
    return near + tuple(swap(piece, 1) for piece in near)


def column(shard):
    return jnp.stack([shard] + [swap(shard, 8 * z) for z in (1, 2, 3)])


def gather_full(shard):
    full = lax.all_gather(shard, ALL, axis=0, tiled=True)
    view = full.reshape(*SPLIT, full.shape[0] // BLOCKS, D)
    found = ()
    for core in range(2):
        side = view[:, :, :, core]
        found += (side[:, 0, 0], side[:, 1, 0], side[:, 0, 1], side[:2, 1, 1], side[2:, 1, 1])
    return found


def scatter_blocks(own, y_low, y_high, x_low, x_high, far_low, far_high):
    wide = lambda a: a.astype(F32)
    got_low, got_high = swap(far_low, 2), swap(far_high, 4)
    from_y, from_x = swap(y_low, 2), swap(x_high, 4)
    to_x = (wide(x_low) + wide(got_low)).astype(BF)
    to_y = (wide(y_high) + wide(got_high)).astype(BF)
    low = wide(own[:2]) + wide(from_y) + wide(swap(to_x, 4))
    high = wide(own[2:]) + wide(from_x) + wide(swap(to_y, 2))
    return (
        low[0]
        + wide(swap(low[1].astype(BF), 8))
        + wide(swap(high[0].astype(BF), 16))
        + wide(swap(high[1].astype(BF), 24))
    )


def scatter_full(sides):
    cores = []
    for own, y_low, y_high, x_low, x_high, far_low, far_high in sides:
        join = lambda a, b: jnp.concatenate([a, b], axis=0)
        rows = [own, join(y_low, y_high), join(x_low, x_high), join(far_low, far_high)]
        cores.append(jnp.stack(rows, axis=1))
    full = jnp.stack(cores, axis=2).reshape(-1, D)
    return lax.psum_scatter(full, ALL, scatter_dimension=0, tiled=True).astype(F32)


def flip_bits(array, at):
    for axis, bit in enumerate((at[0] % 2, at[1], at[2], at[3])):
        array = jnp.where(bit == 1, jnp.flip(array, axis), array)
    return array


def sum_small(arrays, direct):
    if not direct:
        return lax.psum(arrays, ALL)
    sizes = [a.size for a in arrays]
    flat = jnp.concatenate([a.reshape(-1) for a in arrays])
    pad = -flat.size % 1024
    flat = jnp.pad(flat, (0, pad)).reshape(-1, 128)
    for mask in (1, 2, 4, 8, 16):
        flat = flat + swap(flat, mask)
    flat = flat.reshape(-1)
    found, start = [], 0
    for a, size in zip(arrays, sizes):
        found.append(flat[start : start + size].reshape(a.shape))
        start += size
    return found


def shards(
    tokens,
    cotangent,
    lengths,
    rel_1d,
    rel_x,
    rel_y,
    attn_weights,
    attn_m1,
    attn_m2,
    attn_ema,
    ffn_weights,
    ffn_m1,
    ffn_m2,
    ffn_ema,
    vectors,
    vec_m1,
    vec_m2,
    vec_ema,
    table,
    tab_m1,
    tab_m2,
    tab_ema,
    *,
    direct,
):
    if direct:
        dp, fsdp = lax.axis_index("dp"), lax.axis_index("fsdp")
        at = jnp.stack([dp // 2, dp % 2, fsdp // 2, fsdp % 2]).astype(jnp.int32)
        attn_column = column(attn_weights.astype(BF))
        attn_pieces = plane(attn_column)
        ffn_column = column(tie(ffn_weights.astype(BF), attn_column))
        ffn_pieces = plane(ffn_column)
        far = lambda a: swap(a, 1)
    else:
        at = jnp.zeros((4,), jnp.int32)
        attn_pieces = gather_full(attn_weights.astype(BF))
        ffn_pieces = gather_full(ffn_weights.astype(BF))
        far = jnp.zeros_like
    bias = page_bias(lengths, table, rel_1d, rel_x, rel_y, 4)
    add_three = jnp.concatenate([vectors[4], jnp.zeros((D,), F32), vectors[5]]).reshape(1, 3 * D)
    b_first = flip_bits(vectors[8:].reshape(2, 2, 2, 2, F_ROWS), at)
    b_first = b_first.transpose(3, 0, 1, 2, 4).reshape(1, FF)
    tokens_far = far(tokens)
    qkv, attn_full = project(at, tokens, add_three, attn_pieces)
    ctx, soft = attend(qkv, bias)
    ctx_far = far(ctx)
    (
        block_out,
        hid,
        act_near,
        act_away,
        d_ffn,
        du_near,
        du_away,
        d_resid_one,
        d_attn,
        d_context,
        sums,
        grad_bias_first,
    ) = block_pass(at, ctx, tokens, cotangent, vectors, b_first, attn_full, ffn_pieces)
    if direct:
        wide = (du_near, far(du_away), act_near, far(act_away))
        slim = (hid, far(hid), d_ffn, far(d_ffn))
        d_attn_far = far(d_attn)
        low, high = (grad_ffn(at, wide, slim, side) for side in range(2))
        pairs = [part for pair in zip(low[1:], high[1:]) for part in pair]
        ffn_shard = scatter_blocks(jnp.concatenate([low[0], high[0]]), *pairs)
    dq, dk, dv, d_scores, qv_sums = attend_back(qkv, soft, ctx, d_context)
    d_three = (dq, dk, dv)
    if direct:
        grads = [g for d in d_three for g in (d, far(d))] + [d_attn, d_attn_far]
        attn_shard = scatter_blocks(*grad_attn(at, tokens, tokens_far, ctx, ctx_far, grads))
    else:
        sides, attn_sides = [], []
        grads = [g for d in (*d_three, d_attn) for g in (d, far(d))]
        for core, (du, act) in enumerate(((du_near, act_near), (du_away, act_away))):
            wide = (du, far(du), act, far(act))
            slim = (hid, far(hid), d_ffn, far(d_ffn))
            low, high = (grad_ffn(at, wide, slim, side) for side in range(2))
            pairs = [part for pair in zip(low[1:], high[1:]) for part in pair]
            sides.append((jnp.concatenate([low[0], high[0]]), *pairs))
            spot = at.at[3].set(core)
            attn_sides.append(grad_attn(spot, tokens, tokens_far, ctx, ctx_far, grads))
        ffn_shard, attn_shard = scatter_full(sides), scatter_full(attn_sides)
    grad_input = d_resid_one
    for t in range(3):
        grad_input = grad_input + mm(d_three[t], attn_full[D * t : D * t + D], NT)
    grad_table = table_grad(rel_1d, rel_x, rel_y, d_scores).T
    grad_bias_first = grad_bias_first.reshape(2, 2, 2, 2, F_ROWS).transpose(1, 2, 3, 0, 4)
    grad_bias_first = flip_bits(grad_bias_first, at).reshape(FF // D, D)
    grad_vectors = jnp.concatenate([sums[:4], qv_sums[:2], sums[6:], grad_bias_first], axis=0)
    shard_squares = jnp.sum(attn_shard * attn_shard) + jnp.sum(ffn_shard * ffn_shard)
    vec_total, tab_total, square_total = sum_small(
        (grad_vectors, grad_table, shard_squares), direct
    )
    grad_norm = jnp.sqrt(
        square_total + jnp.sum(vec_total * vec_total) + jnp.sum(tab_total * tab_total)
    )
    clip_scale = 1.0 / jnp.maximum(grad_norm, 1.0)
    attn_new = adam_update(
        attn_weights, attn_m1, attn_m2, attn_shard, clip_scale, 0.06, 0.01, attn_ema
    )
    ffn_new = adam_update(ffn_weights, ffn_m1, ffn_m2, ffn_shard, clip_scale, 0.06, 0.01, ffn_ema)
    vec_new = adam_update(vectors, vec_m1, vec_m2, vec_total, clip_scale, 0.6, 0.0, vec_ema)
    tab_new = adam_update(table, tab_m1, tab_m2, tab_total, clip_scale, 0.6, 0.0, tab_ema)
    return (
        block_out,
        grad_input,
        grad_norm,
        attn_new[0],
        attn_new[1],
        attn_new[2],
        attn_new[3],
        ffn_new[0],
        ffn_new[1],
        ffn_new[2],
        ffn_new[3],
        vec_new[0],
        vec_new[1],
        vec_new[2],
        vec_new[3],
        tab_new[0],
        tab_new[1],
        tab_new[2],
        tab_new[3],
        vec_total * clip_scale,
    )


def solution(mesh):
    direct = mesh.shape["dp"] == SPLIT[0] * SPLIT[1] and mesh.shape["fsdp"] == SPLIT[2] * SPLIT[3]
    return jax.shard_map(
        lambda *arrays: shards(*arrays, direct=direct),
        mesh=mesh,
        in_specs=(
            P(("dp", "fsdp"), None),
            P(("dp", "fsdp"), None),
            P(("dp", "fsdp")),
            P(("dp", "fsdp"), None, None),
            P(("dp", "fsdp"), None, None),
            P(("dp", "fsdp"), None, None),
            P(("dp", "fsdp"), None),
            P(("dp", "fsdp"), None),
            P(("dp", "fsdp"), None),
            P(("dp", "fsdp"), None),
            P(("dp", "fsdp"), None),
            P(("dp", "fsdp"), None),
            P(("dp", "fsdp"), None),
            P(("dp", "fsdp"), None),
            P(),
            P(),
            P(),
            P(),
            P(),
            P(),
            P(),
            P(),
        ),
        out_specs=(
            P(("dp", "fsdp"), None),
            P(("dp", "fsdp"), None),
            P(),
            P(("dp", "fsdp"), None),
            P(("dp", "fsdp"), None),
            P(("dp", "fsdp"), None),
            P(("dp", "fsdp"), None),
            P(("dp", "fsdp"), None),
            P(("dp", "fsdp"), None),
            P(("dp", "fsdp"), None),
            P(("dp", "fsdp"), None),
            P(),
            P(),
            P(),
            P(),
            P(),
            P(),
            P(),
            P(),
            P(),
        ),
        check_vma=False,
    )
```

```python
import math

import jax
import jax.numpy as jnp
from jax import lax
from jax.experimental import pallas as pl
from jax.experimental.pallas import tpu as pltpu
from jax.sharding import PartitionSpec as P

D = 768
H = 12
HD = 64
FF = 3072
B1 = 32
BX = 64
SEQ = 512
STEP = 10
BUCKETS = B1 + 2 * BX


NEG_FILL = -1e30
NORM_EPS = 1e-05
BF = jnp.bfloat16
F32 = jnp.float32
NT = (((1,), (1,)), ((), ()))
TN = (((0,), (0,)), ((), ()))
NN = (((1,), (0,)), ((), ()))
ALL = ("dp", "fsdp")
COST = 1_000_000
SPLIT = (4, 2, 2, 2)
BLOCKS = 32
A_ROWS = 4 * D // BLOCKS
F_ROWS = 2 * FF // BLOCKS
HALF = FF // 2
ANY = pl.BlockSpec(memory_space=pl.ANY)


def mm(a, b, dims):
    return lax.dot_general(a, b, dims, preferred_element_type=F32)


def adam_update(weight, moment_one, second, gradient, clip_scale, step_rate, decay_rate, average):
    clipped = gradient * clip_scale
    new_first = 0.9 * moment_one + 0.1 * clipped
    new_second = 0.999 * second + 0.001 * clipped * clipped
    first_hat = new_first / (1.0 - 0.9**STEP)
    second_hat = new_second / (1.0 - 0.999**STEP)
    new_weight = weight - step_rate * (
        first_hat / (jnp.sqrt(second_hat) + 1e-08) + decay_rate * weight
    )
    new_average = 0.8 * average + 0.2 * new_weight
    return (new_weight, new_first, new_second, new_average)


def bias_kernel(len_ref, tab_ref, one_ref, x_ref, y_ref, out_ref):
    length = len_ref[0]
    rows = one_ref.shape[1]

    def eight(i, _):
        r = pl.ds(pl.multiple_of(i * 8, 8), 8)
        for c in range(0, SEQ, 128):
            ids = [ref[0, r, c : c + 128] for ref in (one_ref, x_ref, y_ref)]
            keep = lax.broadcasted_iota(jnp.int32, (8, 128), 1) + c < length
            for h in range(H):
                total = None
                for t in range(3):
                    line = jnp.broadcast_to(tab_ref[h, t : t + 1, :], (8, 128))
                    got = jnp.take_along_axis(line, ids[t], axis=1, mode="promise_in_bounds")
                    total = got if total is None else total + got
                out_ref[h, r, c : c + 128] = jnp.where(keep, total, NEG_FILL)
        return 0

    lax.fori_loop(0, rows // 8, eight, 0)


PARTS = 2
BIAS_ROWS = ((0, 192), (192, 256), (448, 64))


def bias_lines(table):
    lines = table.T
    return jnp.stack(
        [
            jnp.pad(lines[:, :B1], ((0, 0), (0, 128 - B1))),
            jnp.pad(lines[:, B1 : B1 + BX], ((0, 0), (0, 128 - BX))),
            jnp.pad(lines[:, B1 + BX :], ((0, 0), (0, 128 - BX))),
        ],
        axis=1,
    )


def page_bias(lengths, tab, rel, part, out):
    rows = 64
    first, count = BIAS_ROWS[part][0] // rows, BIAS_ROWS[part][1] // rows
    ids = pl.BlockSpec((1, rows, SEQ), lambda i, *_: (0, first + i, 0))
    extra = [] if out is None else [out]
    return pl.pallas_call(
        lambda *refs: bias_kernel(*refs[:5], refs[-1]),
        grid_spec=pltpu.PrefetchScalarGridSpec(
            num_scalar_prefetch=1,
            grid=(count,),
            in_specs=[pl.BlockSpec((H, 3, 128), lambda i, *_: (0, 0, 0)), ids, ids, ids]
            + [ANY] * len(extra),
            out_specs=pl.BlockSpec((H, rows, SEQ), lambda i, *_: (0, first + i, 0)),
        ),
        out_shape=jax.ShapeDtypeStruct((H, SEQ, SEQ), F32),
        input_output_aliases={5: 0} if extra else {},
        cost_estimate=pl.CostEstimate(
            flops=COST, bytes_accessed=COST, transcendentals=0
        ),
        name="bias",
    )(lengths, tab, *rel, *extra)


def head_masks():
    lane = lax.broadcasted_iota(jnp.int32, (1, 2 * HD), 1)
    return (lane < HD, lane >= HD)


def attend_kernel(q_ref, k_ref, v_ref, bias_ref, ctx_ref, p_ref, *, rows):
    zero = jnp.zeros((), BF)
    masks = head_masks()
    keys = [jnp.where(m, k_ref[...], zero) for m in masks]
    vals = [jnp.where(m, v_ref[...], zero) for m in masks]
    for r in range(0, SEQ, rows):
        q = q_ref[r : r + rows, :]
        ctx = None
        for h in range(2):
            scores = mm(q, keys[h], NT) * HD ** (-0.5) + bias_ref[h, r : r + rows, :]
            top = jnp.max(scores, axis=-1, keepdims=True)
            raised = jnp.exp(scores - top)
            total = jnp.sum(raised, axis=-1, keepdims=True)
            soft = (raised * (1.0 / total)).astype(BF)
            p_ref[h, r : r + rows, :] = soft
            part = mm(soft, vals[h], NN)
            ctx = part if ctx is None else ctx + part
        ctx_ref[r : r + rows, :] = ctx.astype(BF)


def lane_block(offset):
    return pl.BlockSpec((SEQ, 2 * HD), lambda i: (0, offset + i))


PAIR_BLOCK = pl.BlockSpec((2, SEQ, SEQ), lambda i: (i, 0, 0))


def attend(qkv, bias):
    n = D // (2 * HD)
    return pl.pallas_call(
        lambda *refs: attend_kernel(*refs, rows=256),
        grid=(n,),
        in_specs=[lane_block(0), lane_block(n), lane_block(2 * n), PAIR_BLOCK],
        out_specs=[lane_block(0), PAIR_BLOCK],
        out_shape=[
            jax.ShapeDtypeStruct((SEQ, D), BF),
            jax.ShapeDtypeStruct((H, SEQ, SEQ), BF),
        ],
        cost_estimate=pl.CostEstimate(
            flops=COST, bytes_accessed=COST, transcendentals=0
        ),
        name="attend",
    )(qkv, qkv, qkv, bias)


def attend_back_kernel(
    q_ref, k_ref, v_ref, p_ref, c_ref, dc_ref, dq_ref, dk_ref, dv_ref, ds_ref, sum_ref, *, rows
):
    zero = jnp.zeros((), BF)
    masks = head_masks()
    keys = [jnp.where(m, k_ref[...], zero) for m in masks]
    vals = [jnp.where(m, v_ref[...], zero) for m in masks]
    scale = HD ** (-0.5)
    q_sum = jnp.zeros((1, 2 * HD), F32)
    for r in range(0, SEQ, rows):
        dc = dc_ref[r : r + rows, :]
        prod = dc.astype(F32) * c_ref[r : r + rows, :].astype(F32)
        dq = None
        for h in range(2):
            soft = p_ref[h, r : r + rows, :]
            inner = jnp.sum(jnp.where(masks[h], prod, 0.0), axis=-1, keepdims=True)
            d_soft = mm(dc, vals[h], NT)
            d_scores = (soft.astype(F32) * (d_soft - inner)).astype(BF)
            ds_ref[h, r : r + rows, :] = d_scores
            part = mm(d_scores, keys[h], NN)
            dq = part if dq is None else dq + part
        dq = (dq * scale).astype(BF)
        dq_ref[r : r + rows, :] = dq
        q_sum = q_sum + jnp.sum(dq.astype(F32), axis=0, keepdims=True)
    flips = (dc_ref[...].astype(F32).T.astype(BF), q_ref[...].astype(F32).T.astype(BF))
    sums = [q_sum]
    for flip, factor, pair_ref, out_ref in (
        (flips[0], 1.0, p_ref, dv_ref),
        (flips[1], scale, ds_ref, dk_ref),
    ):
        parts = [mm(flip[HD * h : HD * h + HD, :], pair_ref[h], NN) for h in range(2)]
        done = (jnp.concatenate(parts, axis=0).T * factor).astype(BF)
        out_ref[...] = done
        sums.append(jnp.sum(done.astype(F32), axis=0, keepdims=True))
    sum_ref[...] = jnp.concatenate(sums[:2] + [jnp.zeros((6, 2 * HD), F32)], axis=0)


def attend_back(qkv, soft, ctx, d_ctx):
    n = D // (2 * HD)
    return pl.pallas_call(
        lambda *refs: attend_back_kernel(*refs, rows=256),
        grid=(n,),
        in_specs=[
            lane_block(0),
            lane_block(n),
            lane_block(2 * n),
            PAIR_BLOCK,
            lane_block(0),
            lane_block(0),
        ],
        out_specs=[
            lane_block(0),
            lane_block(0),
            lane_block(0),
            PAIR_BLOCK,
            pl.BlockSpec((8, 2 * HD), lambda i: (0, i)),
        ],
        out_shape=[jax.ShapeDtypeStruct((SEQ, D), BF)] * 3
        + [jax.ShapeDtypeStruct((H, SEQ, SEQ), BF), jax.ShapeDtypeStruct((8, D), F32)],
        cost_estimate=pl.CostEstimate(
            flops=COST, bytes_accessed=COST, transcendentals=0
        ),
        name="attend_back",
    )(qkv, qkv, qkv, soft, ctx, d_ctx)


def table_kernel(one_ref, x_ref, y_ref, ds_ref, out_ref):
    @pl.when(pl.program_id(0) == 0)
    def _():
        out_ref[...] = jnp.zeros_like(out_ref)

    rows = one_ref.shape[1]
    flipped = jnp.swapaxes(ds_ref[...].astype(F32), 0, 1).astype(BF)
    total = None
    for r in range(rows):
        hot = jnp.concatenate(
            [
                (lax.broadcasted_iota(jnp.int32, (size, SEQ), 0) == ref[0, r : r + 1, :])
                .astype(F32)
                .astype(BF)
                for ref, size in ((one_ref, B1), (x_ref, BX), (y_ref, BX))
            ],
            axis=0,
        )
        part = mm(flipped[r], hot, NT)
        total = part if total is None else total + part
    out_ref[...] += total


def table_grad(rel_1d, rel_x, rel_y, d_scores, part):
    rows = 16
    count = SEQ // rows // PARTS
    first = part * count
    ids = pl.BlockSpec((1, rows, SEQ), lambda i: (0, first + i, 0))
    return pl.pallas_call(
        table_kernel,
        grid=(count,),
        in_specs=[ids, ids, ids, pl.BlockSpec((H, rows, SEQ), lambda i: (0, first + i, 0))],
        out_specs=pl.BlockSpec((H, BUCKETS), lambda i: (0, 0)),
        out_shape=jax.ShapeDtypeStruct((H, BUCKETS), F32),
        cost_estimate=pl.CostEstimate(
            flops=COST, bytes_accessed=COST, transcendentals=0
        ),
        name="table_grad",
    )(rel_1d, rel_x, rel_y, d_scores)


def spread(size, plan):
    found = []
    for whole in plan:
        at, pieces = 0, []
        for z, x, y, first, last in whole:
            rows = (last - first) * size // 2
            pieces.append((at, rows, z, x, y, first * size // 2))
            at += rows
        found.append(pieces)
    return found


def blocks(zs, x, y):
    return [(z, x, y, 0, 2) for z in zs]


ATTN_PLAN = spread(
    A_ROWS,
    [
        blocks(range(4), 0, 0),
        blocks(range(4), 1, 0),
        blocks(range(4), 0, 1),
        blocks((0, 1), 1, 1),
        blocks((2, 3), 1, 1),
    ],
)
FFN_PLAN = spread(
    F_ROWS,
    [
        blocks((0,), 0, 0),
        blocks((0,), 1, 0),
        blocks((0,), 0, 1),
        blocks((0,), 1, 1),
        blocks((1, 2, 3), 0, 0),
        blocks((1, 2, 3), 1, 0),
        blocks((1, 2, 3), 0, 1),
        [(1, 1, 1, 0, 2), (2, 1, 1, 0, 1)],
        [(2, 1, 1, 1, 2), (3, 1, 1, 0, 2)],
    ],
)
A_COPIES = 2 * sum(len(pieces) for pieces in ATTN_PLAN)
F_COPIES = 2 * sum(len(pieces) for pieces in FFN_PLAN)

ATTN_FAR, FFN_FAR = ATTN_PLAN, FFN_PLAN


def piece_list(plans, refs):
    found = []
    for core, plan in enumerate(plans):
        for pieces, ref in zip(plan, refs[len(plans[0]) * core :]):
            for start, rows, z, x, y, offset in pieces:
                found.append((core, z, x, y, offset, rows, ref.at[pl.ds(start, rows), :]))
    return found


def qkv_kernel(at_ref, tok_ref, add_ref, *refs):
    qkv_ref, all_ref, weight_ref, sems, done = refs[len(ATTN_PLAN) + len(ATTN_FAR) :]
    copies = []
    for n, (core, z, x, y, offset, rows, ref) in enumerate(piece_list((ATTN_PLAN, ATTN_FAR), refs)):
        block = (
            ((at_ref[0] ^ z) * 2 + (at_ref[1] ^ x)) * 2 + (at_ref[2] ^ y)
        ) * 2 + (at_ref[3] ^ core)
        spot = pl.ds(pl.multiple_of(block * A_ROWS + offset, 16), rows)
        copies.append(pltpu.make_async_copy(ref, weight_ref.at[spot, :], sems.at[n]))
    for copy in copies:
        copy.start()
    for copy in copies:
        copy.wait()
    store = pltpu.make_async_copy(weight_ref, all_ref, done)
    store.start()
    for t in range(3):
        part = slice(D * t, D * t + D)
        qkv_ref[:, part] = (mm(tok_ref[...], weight_ref[part, :], NN) + add_ref[:, part]).astype(BF)
    store.wait()


def project(at, tokens, add_three, pieces):
    count = tokens.shape[0]
    vmem = pl.BlockSpec(memory_space=pltpu.VMEM)
    return pl.pallas_call(
        qkv_kernel,
        in_specs=[pl.BlockSpec(memory_space=pltpu.SMEM), vmem, vmem] + [ANY] * len(pieces),
        out_specs=[vmem, ANY],
        out_shape=[
            jax.ShapeDtypeStruct((count, 3 * D), BF),
            jax.ShapeDtypeStruct((4 * D, D), BF),
        ],
        scratch_shapes=[
            pltpu.VMEM((4 * D, D), BF),
            pltpu.SemaphoreType.DMA((A_COPIES,)),
            pltpu.SemaphoreType.DMA,
        ],
        cost_estimate=pl.CostEstimate(
            flops=COST, bytes_accessed=COST, transcendentals=0
        ),
        name="project",
    )(at, tokens, add_three, *pieces)


def grad_ffn_kernel(at_ref, *refs, high):
    wide, slim, outs, (left, right, sems) = refs[:4], refs[4:8], refs[8:11], refs[11:]
    which = (at_ref[0] // 2) ^ high
    for w in range(2):

        @pl.when(which == w)
        def _():
            copies = []
            for i in range(2):
                rows = pl.ds(SEQ * i, SEQ)
                copies.append(
                    pltpu.make_async_copy(wide[2 * w + i], left.at[rows, :], sems.at[2 * i])
                )
                copies.append(
                    pltpu.make_async_copy(slim[2 * w + i], right.at[rows, :], sems.at[2 * i + 1])
                )
            for copy in copies:
                copy.start()
            for copy in copies:
                copy.wait()

    own, kept, sent = outs
    for z in range(2):
        done = mm(left[:, HALF // 2 * z : HALF // 2 * (z + 1)], right[...], TN).astype(BF)
        rows = [done[F_ROWS * q : F_ROWS * q + F_ROWS, :] for q in range(4)]
        own[z] = rows[0]
        kept[z] = rows[1 if high else 2]
        sent[z] = rows[3]
        sent[2 + z] = rows[2 if high else 1]


def grad_ffn(at, wide, slim, high):
    shape = lambda n: jax.ShapeDtypeStruct((n, F_ROWS, D), BF)
    return pl.pallas_call(
        lambda *refs: grad_ffn_kernel(*refs, high=high),
        in_specs=[pl.BlockSpec(memory_space=pltpu.SMEM)] + [ANY] * 8,
        out_specs=[pl.BlockSpec(memory_space=pltpu.VMEM)] * 3,
        out_shape=[shape(2), shape(2), shape(4)],
        scratch_shapes=[
            pltpu.VMEM((2 * SEQ, HALF), BF),
            pltpu.VMEM((2 * SEQ, D), BF),
            pltpu.SemaphoreType.DMA((4,)),
        ],
        cost_estimate=pl.CostEstimate(
            flops=COST, bytes_accessed=COST, transcendentals=0
        ),
        name="grad_ffn",
    )(at, *wide, *slim)


def grad_attn_kernel(at_ref, tok_ref, tok_far, ctx_ref, ctx_far, *refs):
    grads, outs, (flip, left, right, sems) = refs[:8], refs[8:14], refs[14:]
    copies = []
    for t in range(4):
        for i in range(2):
            spot = right.at[t, pl.ds(SEQ * i, SEQ), :]
            copies.append(pltpu.make_async_copy(grads[2 * t + i], spot, sems.at[2 * t + i]))
    for copy in copies:
        copy.start()
    for n, (near, far) in enumerate(((tok_ref, tok_far), (ctx_ref, ctx_far))):
        flip[:, :SEQ] = near[...].astype(F32).T.astype(BF)
        flip[:, SEQ:] = far[...].astype(F32).T.astype(BF)
        for q in range(4):
            block = (((at_ref[1] ^ (q // 2)) * 2 + (at_ref[2] ^ (q % 2))) * 2) + at_ref[3]
            spot = pl.ds(pl.multiple_of(block * A_ROWS, A_ROWS), A_ROWS)
            left[n, A_ROWS * q : A_ROWS * q + A_ROWS, :] = flip[spot, :]
    for copy in copies:
        copy.wait()
    for z in range(4):
        which = at_ref[0] ^ z
        done = mm(left[which // 3], right[which], NN).astype(BF)
        rows = [done[A_ROWS * q : A_ROWS * q + A_ROWS, :] for q in range(4)]
        own, kept, sent = outs[3 * (z // 2) : 3 * (z // 2) + 3]
        own[z % 2] = rows[0]
        kept[z % 2] = rows[1 if z // 2 else 2]
        sent[z % 2] = rows[3]
        sent[2 + z % 2] = rows[2 if z // 2 else 1]


def grad_attn(at, tokens, tokens_far, ctx, ctx_far, grads):
    shape = lambda n: jax.ShapeDtypeStruct((n, A_ROWS, D), BF)
    vmem = pl.BlockSpec(memory_space=pltpu.VMEM)
    return pl.pallas_call(
        grad_attn_kernel,
        in_specs=[pl.BlockSpec(memory_space=pltpu.SMEM)] + [vmem] * 4 + [ANY] * 8,
        out_specs=[vmem] * 6,
        out_shape=[shape(2), shape(2), shape(4)] * 2,
        scratch_shapes=[
            pltpu.VMEM((D, 2 * SEQ), BF),
            pltpu.VMEM((2, D // 2, 2 * SEQ), BF),
            pltpu.VMEM((4, 2 * SEQ, D), BF),
            pltpu.SemaphoreType.DMA((8,)),
        ],
        cost_estimate=pl.CostEstimate(
            flops=COST, bytes_accessed=COST, transcendentals=0
        ),
        name="grad_attn",
    )(at, tokens, tokens_far, ctx, ctx_far, *grads)


def row_mean(values):
    return jnp.mean(values, axis=-1, keepdims=True)


def normal_rows(values):
    center = values - row_mean(values)
    inv = lax.rsqrt(row_mean(center * center) + NORM_EPS)
    return center * inv, inv


def normal_back(normal, inv, grad):
    return inv * (grad - row_mean(grad) - normal * row_mean(grad * normal))


def gelu_parts(u):
    z = jnp.abs(u) * (2.0**-0.5)
    t = 1.0 / (1.0 + 0.3275911 * z)
    tail = jnp.exp(-0.5 * u * u)
    poly = t * (
        0.254829592
        + t * (-0.284496736 + t * (1.421413741 + t * (-1.453152027 + t * 1.061405429)))
    )
    half = 0.5 * poly * tail
    cdf = jnp.where(u < 0, half, 1.0 - half)
    return u * cdf, cdf + u * (tail * (1.0 / math.sqrt(2.0 * math.pi)))


def row_sum(values):
    return jnp.sum(values.astype(F32), axis=0, keepdims=True)


def block_kernel(
    at_ref,
    ctx_ref,
    tok_ref,
    cot_ref,
    vec_ref,
    b1_ref,
    wo_ref,
    *refs,
    wide,
):
    split = len(FFN_PLAN) + len(FFN_FAR)
    pieces, refs = refs[:split], refs[split:]
    out_ref, hid_ref, act_near, act_far, dff_ref, du_near, du_far = refs[:7]
    dr_ref, dab_ref, dctx_ref, sum_ref, db1_ref, slope_ref, ffn_ref, sems = refs[7:]
    copies = []
    for n, (core, z, x, y, offset, rows, ref) in enumerate(piece_list((FFN_PLAN, FFN_FAR), pieces)):
        spot = pl.ds(core * HALF + ((z % 2) * 4 + x * 2 + y) * F_ROWS + offset, rows)
        which = (at_ref[0] // 2) ^ (z // 2)
        copies.append(pltpu.make_async_copy(ref, ffn_ref.at[which, spot, :], sems.at[n]))
    w1_ref, w2_ref = ffn_ref.at[0], ffn_ref.at[1]

    @pl.when(pl.program_id(0) == 0)
    def _():
        for copy in copies:
            copy.start()
        sum_ref[...] = jnp.zeros_like(sum_ref)
        db1_ref[...] = jnp.zeros_like(db1_ref)

    vec = [vec_ref[i : i + 1, :] for i in range(8)]
    resid = tok_ref[...].astype(F32) + (mm(ctx_ref[...], wo_ref[...], NN) + vec[6])
    n_one, inv_one = normal_rows(resid)
    hidden = n_one * vec[0] + vec[1]
    hid_low = hidden.astype(BF)
    hid_ref[...] = hid_low
    total = hidden + vec[7]

    @pl.when(pl.program_id(0) == 0)
    def _():
        for copy in copies:
            copy.wait()

    for f in range(0, FF, wide):
        part = slice(f, f + wide)
        u = mm(hid_low, w1_ref[part, :], NT) + b1_ref[:, part]
        act, slope = gelu_parts(u)
        act = act.astype(BF)
        side = slice(f % HALF, f % HALF + wide)
        (act_near if f < HALF else act_far)[:, side] = act
        slope_ref[:, part] = slope
        total = total + mm(act, w2_ref[part, :], NN)
    n_two, inv_two = normal_rows(total)
    out_ref[...] = (n_two * vec[2] + vec[3]).astype(BF)
    dy = cot_ref[...].astype(F32)
    d_two = normal_back(n_two, inv_two, dy * vec[2])
    dff = d_two.astype(BF)
    dff_ref[...] = dff
    d_hid = d_two
    for f in range(0, FF, wide):
        part = slice(f, f + wide)
        du = (mm(dff, w2_ref[part, :], NT) * slope_ref[:, part]).astype(BF)
        side = slice(f % HALF, f % HALF + wide)
        (du_near if f < HALF else du_far)[:, side] = du
        db1_ref[:, part] += row_sum(du)
        d_hid = d_hid + mm(du, w1_ref[part, :], NN)
    d_one = normal_back(n_one, inv_one, d_hid * vec[0])
    dr_ref[...] = d_one
    dab = d_one.astype(BF)
    dab_ref[...] = dab
    dctx_ref[...] = mm(dab, wo_ref[...], NT).astype(BF)
    sum_ref[...] += jnp.concatenate(
        [
            row_sum(d_hid * n_one),
            row_sum(d_hid),
            row_sum(dy * n_two),
            row_sum(dy),
            jnp.zeros((2, D), F32),
            row_sum(dab),
            row_sum(dff),
        ],
        axis=0,
    )


def block_pass(at, ctx, tokens, cotangent, vectors, b_first, attn_full, pieces):
    rows = 256
    by_row = lambda width: pl.BlockSpec((rows, width), lambda i, *_: (i, 0))
    whole = lambda shape, first=0: pl.BlockSpec(
        shape, lambda i, *_: (first, 0), pipeline_mode=pl.Buffered(1)
    )
    count = tokens.shape[0]
    low = lambda width: jax.ShapeDtypeStruct((count, width), BF)
    return pl.pallas_call(
        lambda *refs: block_kernel(*refs, wide=768),
        grid_spec=pltpu.PrefetchScalarGridSpec(
            num_scalar_prefetch=1,
            grid=(count // rows,),
            in_specs=[
                by_row(D),
                by_row(D),
                by_row(D),
                whole((12, D)),
                whole((1, FF)),
                whole((D, D), 3),
            ]
            + [ANY] * len(pieces),
            out_specs=[
                by_row(D),
                by_row(D),
                by_row(HALF),
                by_row(HALF),
                by_row(D),
                by_row(HALF),
                by_row(HALF),
                by_row(D),
                by_row(D),
                by_row(D),
                pl.BlockSpec((8, D), lambda i, *_: (0, 0)),
                pl.BlockSpec((1, FF), lambda i, *_: (0, 0)),
            ],
            scratch_shapes=[
                pltpu.VMEM((rows, FF), F32),
                pltpu.VMEM((2, FF, D), BF),
                pltpu.SemaphoreType.DMA((F_COPIES,)),
            ],
        ),
        out_shape=[
            low(D),
            low(D),
            low(HALF),
            low(HALF),
            low(D),
            low(HALF),
            low(HALF),
            jax.ShapeDtypeStruct((count, D), F32),
            low(D),
            low(D),
            jax.ShapeDtypeStruct((8, D), F32),
            jax.ShapeDtypeStruct((1, FF), F32),
        ],
        cost_estimate=pl.CostEstimate(
            flops=COST, bytes_accessed=COST, transcendentals=0
        ),
        name="block_pass",
    )(at, ctx, tokens, cotangent, vectors, b_first, attn_full, *pieces)


def swap(array, mask):
    return lax.ppermute(array, ALL, [(i, i ^ mask) for i in range(BLOCKS)])


def together(*groups):
    return lax.optimization_barrier(groups)


def tie(arrays, after):
    return lax.optimization_barrier((arrays, after))[0]


def column(shard, zs):
    return jnp.concatenate([shard if z == 0 else swap(shard, 8 * z) for z in zs])


def gather_full(shard, plans):
    full = lax.all_gather(shard, ALL, axis=0, tiled=True)
    view = full.reshape(*SPLIT, full.shape[0] // BLOCKS, D)
    return tuple(
        jnp.concatenate([view[z, x, y, core, off : off + n] for _, n, z, x, y, off in pieces])
        for core, plan in enumerate(plans)
        for pieces in plan
    )


def wide(array):
    return array.astype(F32)


def scatter_first(low, high):
    return swap(low[2], 2), swap(high[2], 4)


def scatter_second(low, high, from_y, from_x):
    to_x = (wide(low[1]) + wide(from_y[:2])).astype(BF)
    to_y = (wide(high[1]) + wide(from_x[:2])).astype(BF)
    return swap(to_x, 4), swap(to_y, 2)


def scatter_third(low, high, from_y, from_x, last_x, last_y):
    low = wide(low[0]) + wide(from_y[2:]) + wide(last_x)
    high = wide(high[0]) + wide(from_x[2:]) + wide(last_y)
    send = (low[1].astype(BF), high[0].astype(BF), high[1].astype(BF))
    return low[0], tuple(swap(a, 8 * z) for z, a in zip((1, 2, 3), send))


def scatter_full(sides):
    cores = []
    for low, high in sides:
        rows = [(low[0], high[0]), (low[2][2:], high[1]), (low[1], high[2][2:])]
        rows.append((low[2][:2], high[2][:2]))
        cores.append(jnp.stack([jnp.concatenate(pair) for pair in rows], axis=1))
    full = jnp.stack(cores, axis=2).reshape(-1, D)
    return lax.psum_scatter(full, ALL, scatter_dimension=0, tiled=True).astype(F32)


def flip_bits(array, at):
    for axis, bit in enumerate((at[0] % 2, at[1], at[2], at[3])):
        array = jnp.where(bit == 1, jnp.flip(array, axis), array)
    return array


LANES = 256


def pack_table(grad):
    return jnp.pad(grad, ((0, 0), (0, LANES - BUCKETS))).reshape(H * LANES // D, D)


def update_kernel(total_ref, attn_sum, ffn_sum, *refs):
    states, outs = [refs[4 * i : 4 * i + 4] for i in range(4)], refs[16:]
    per = D // LANES
    vec_total = total_ref[:H, :]
    heads = jnp.concatenate(
        [
            total_ref[H + h // per : H + h // per + 1, LANES * (h % per) : LANES * (h % per + 1)]
            for h in range(H)
        ],
        axis=0,
    )
    square = total_ref[H : H + 1, LANES - 1 : LANES]
    lane = lax.broadcasted_iota(jnp.int32, heads.shape, 1)
    tab_total = jnp.where(lane < BUCKETS, heads, 0.0)
    rows = jnp.sum(tab_total * tab_total, axis=0, keepdims=True)
    square = square + jnp.sum(rows, axis=1, keepdims=True)
    rows = jnp.sum(vec_total * vec_total, axis=0, keepdims=True)
    norm = jnp.sqrt(square + jnp.sum(rows, axis=1, keepdims=True))
    scale = 1.0 / jnp.maximum(norm, 1.0)
    outs[0][...] = norm
    outs[1][...] = vec_total * scale
    totals = (attn_sum[...], ffn_sum[...], vec_total, heads[:H, :BUCKETS])
    for i, (state, total) in enumerate(zip(states, totals)):
        rate, decay = (0.06, 0.01) if i < 2 else (0.6, 0.0)
        weight, first, second, average = (ref[...] for ref in state)
        new = adam_update(weight, first, second, total, scale, rate, decay, average)
        for out, value in zip(outs[2 + 4 * i :], new):
            out[...] = value


def update(total, attn_sum, ffn_sum, states):
    vmem = pl.BlockSpec(memory_space=pltpu.VMEM)
    like = lambda a: jax.ShapeDtypeStruct(a.shape, F32)
    one = jax.ShapeDtypeStruct((1, 1), F32)
    return pl.pallas_call(
        update_kernel,
        in_specs=[vmem] * 19,
        out_specs=[vmem] * 18,
        out_shape=[one, like(states[8])] + [like(a) for a in states],
        name="update",
    )(total, attn_sum, ffn_sum, *states)


def input_grad(start, d_three, attn_full):
    for t in range(3):
        start = start + mm(d_three[t], attn_full[D * t : D * t + D], NT)
    return start


def shards(
    tokens,
    cotangent,
    lengths,
    rel_1d,
    rel_x,
    rel_y,
    attn_weights,
    attn_m1,
    attn_m2,
    attn_ema,
    ffn_weights,
    ffn_m1,
    ffn_m2,
    ffn_ema,
    vectors,
    vec_m1,
    vec_m2,
    vec_ema,
    table,
    tab_m1,
    tab_m2,
    tab_ema,
    *,
    direct,
):
    attn_low, ffn_low = attn_weights.astype(BF), ffn_weights.astype(BF)
    rel = (rel_1d, rel_x, rel_y)
    tab = bias_lines(table)
    add_three = jnp.concatenate([vectors[4], jnp.zeros((D,), F32), vectors[5]]).reshape(1, 3 * D)
    if direct:
        dp, fsdp = lax.axis_index("dp"), lax.axis_index("fsdp")
        at = jnp.stack([dp // 2, dp % 2, fsdp // 2, fsdp % 2]).astype(jnp.int32)
        far = lambda a: swap(a, 1)
        attn_column = column(attn_low, range(4))
        ffn_x, ffn_y = swap(ffn_low, 4), swap(ffn_low, 2)
        bias = page_bias(lengths, tab, rel, 0, None)
        attn_column, ffn_x, ffn_y, later, bias = together(
            attn_column, ffn_x, ffn_y, ffn_low, bias
        )
        beside, above = swap(attn_column, 4), swap(attn_column, 2)
        ffn_column = column(later, (1, 2, 3))
        bias = page_bias(lengths, tab, rel, 1, bias)
        beside, above, bias = together(beside, above, bias)
        side = 2 * A_ROWS
        low, high = swap(beside[:side], 2), swap(above[side:], 4)
        near, ffn_column, bias = together((attn_column, beside, above), ffn_column, bias)
        away = tuple(swap(piece, 1) for piece in near)
        bias = page_bias(lengths, tab, rel, 2, bias)
        last, ffn_column, ffn_x, away, bias = together((low, high), ffn_column, ffn_x, away, bias)
        attn_pieces = near + last + away + tuple(swap(piece, 1) for piece in last)
        ffn_low = tie(ffn_low, ffn_column)
        beside, above, corner = swap(ffn_column, 4), swap(ffn_column, 2), swap(ffn_x, 2)
        qkv, attn_full = project(at, tokens, add_three, attn_pieces)
        ctx, soft = attend(qkv, bias)
        near = (ffn_low, ffn_x, ffn_y, corner, ffn_column, beside, above)
        first = (swap(ffn_low, 1), swap(ffn_x, 1))
        near, first, ctx = together(near, first, ctx)
        side = 3 * F_ROWS // 2
        last = (swap(near[5][:side], 2), swap(near[6][side:], 4))
        away = first + tuple(swap(piece, 1) for piece in near[2:])
        last, away = together(last, away)
        ffn_pieces = near + last + away + tuple(swap(piece, 1) for piece in last)
    else:
        at = jnp.zeros((4,), jnp.int32)
        far = jnp.zeros_like
        bias = None
        for part in range(len(BIAS_ROWS)):
            bias = page_bias(lengths, tab, rel, part, bias)
        attn_pieces = gather_full(attn_low, (ATTN_PLAN, ATTN_FAR))
        ffn_pieces = gather_full(ffn_low, (FFN_PLAN, FFN_FAR))
        qkv, attn_full = project(at, tokens, add_three, attn_pieces)
        ctx, soft = attend(qkv, bias)
        tokens_far, ctx_far = far(tokens), far(ctx)
    b_first = flip_bits(vectors[8:].reshape(2, 2, 2, 2, F_ROWS), at)
    b_first = b_first.transpose(3, 0, 1, 2, 4).reshape(1, FF)
    (
        block_out,
        hid,
        act_near,
        act_away,
        d_ffn,
        du_near,
        du_away,
        d_resid_one,
        d_attn,
        d_context,
        sums,
        grad_bias_first,
    ) = block_pass(at, ctx, tokens, cotangent, vectors, b_first, attn_full, ffn_pieces)
    away = (far(du_away), far(act_away), far(hid), far(d_ffn), far(d_attn))
    dq, dk, dv, d_scores, qv_sums = attend_back(qkv, soft, ctx, d_context)
    d_three = (dq, dk, dv)
    if direct:
        away, d_three, d_scores, rows = together(away, d_three, d_scores, (tokens, ctx))
        du_far, act_far, hid_far, d_ffn_far, d_attn_far = away
        wide_ones, slim = (du_near, du_far, act_near, act_far), (hid, hid_far, d_ffn, d_ffn_far)
        low = grad_ffn(at, wide_ones, slim, 0)
        three_far = tuple(far(d) for d in d_three + rows)
        low, three_far, wide_ones = together(low, three_far, wide_ones)
        high = grad_ffn(at, wide_ones, slim, 1)
        grads = [g for pair in zip(d_three, three_far[:3]) for g in pair] + [d_attn, d_attn_far]
        high, grads = together(high, grads)
        ffn_first = scatter_first(low, high)
        parts = grad_attn(at, tokens, three_far[3], ctx, three_far[4], grads)
        parts, d_scores = together(parts, d_scores)
        attn_first = scatter_first(parts[:3], parts[3:])
        tables = [table_grad(*rel, d_scores, 0)]
        ffn_first, d_scores, tables[0] = together(ffn_first, d_scores, tables[0])
        ffn_second = scatter_second(low, high, *ffn_first)
        tables.append(table_grad(*rel, d_scores, 1))
        attn_first, ffn_second, d_three, tables[1] = together(
            attn_first, ffn_second, d_three, tables[1]
        )
        ffn_own, ffn_three = scatter_third(low, high, *ffn_first, *ffn_second)
        attn_second = scatter_second(parts[:3], parts[3:], *attn_first)
        grad_input = input_grad(d_resid_one, d_three, attn_full)
        attn_second, grad_input = together(attn_second, grad_input)
        attn_own, attn_three = scatter_third(parts[:3], parts[3:], *attn_first, *attn_second)
        ffn_shard = sum((wide(a) for a in ffn_three), ffn_own)
        attn_shard = sum((wide(a) for a in attn_three), attn_own)
    else:
        sides, attn_sides = [], []
        grads = [g for d in (*d_three, d_attn) for g in (d, far(d))]
        slim = (hid, far(hid), d_ffn, far(d_ffn))
        for core, (du, act) in enumerate(((du_near, act_near), (du_away, act_away))):
            wide_ones = (du, far(du), act, far(act))
            sides.append([grad_ffn(at, wide_ones, slim, side) for side in range(2)])
            spot = at.at[3].set(core)
            parts = grad_attn(spot, tokens, tokens_far, ctx, ctx_far, grads)
            attn_sides.append((parts[:3], parts[3:]))
        ffn_shard, attn_shard = scatter_full(sides), scatter_full(attn_sides)
        tables = [table_grad(*rel, d_scores, part) for part in range(PARTS)]
        grad_input = input_grad(d_resid_one, d_three, attn_full)
    grad_table = pack_table(sum(tables[1:], tables[0]))
    grad_bias_first = grad_bias_first.reshape(2, 2, 2, 2, F_ROWS).transpose(1, 2, 3, 0, 4)
    grad_bias_first = flip_bits(grad_bias_first, at).reshape(FF // D, D)
    small = jnp.concatenate([sums[:4], qv_sums[:2], sums[6:], grad_bias_first, grad_table], axis=0)
    squares = jnp.sum(attn_shard * attn_shard) + jnp.sum(ffn_shard * ffn_shard)
    row = lax.broadcasted_iota(jnp.int32, small.shape, 0)
    lane = lax.broadcasted_iota(jnp.int32, small.shape, 1)
    small = jnp.where((row == H) & (lane == LANES - 1), squares, small)
    if direct:
        for mask in (1, 2, 4, 8, 16):
            small = small + swap(small, mask)
    else:
        small = lax.psum(small, ALL)
    states = (attn_weights, attn_m1, attn_m2, attn_ema, ffn_weights, ffn_m1, ffn_m2, ffn_ema)
    states += (vectors, vec_m1, vec_m2, vec_ema, table.T, tab_m1.T, tab_m2.T, tab_ema.T)
    grad_norm, vec_grad, *new = update(small, attn_shard, ffn_shard, states)
    new = new[:12] + [array.T for array in new[12:]]
    return (block_out, grad_input, grad_norm.reshape(()), *new, vec_grad)


def solution(mesh):
    direct = mesh.shape["dp"] == SPLIT[0] * SPLIT[1] and mesh.shape["fsdp"] == SPLIT[2] * SPLIT[3]
    return jax.shard_map(
        lambda *arrays: shards(*arrays, direct=direct),
        mesh=mesh,
        in_specs=(
            P(("dp", "fsdp"), None),
            P(("dp", "fsdp"), None),
            P(("dp", "fsdp")),
            P(("dp", "fsdp"), None, None),
            P(("dp", "fsdp"), None, None),
            P(("dp", "fsdp"), None, None),
            P(("dp", "fsdp"), None),
            P(("dp", "fsdp"), None),
            P(("dp", "fsdp"), None),
            P(("dp", "fsdp"), None),
            P(("dp", "fsdp"), None),
            P(("dp", "fsdp"), None),
            P(("dp", "fsdp"), None),
            P(("dp", "fsdp"), None),
            P(),
            P(),
            P(),
            P(),
            P(),
            P(),
            P(),
            P(),
        ),
        out_specs=(
            P(("dp", "fsdp"), None),
            P(("dp", "fsdp"), None),
            P(),
            P(("dp", "fsdp"), None),
            P(("dp", "fsdp"), None),
            P(("dp", "fsdp"), None),
            P(("dp", "fsdp"), None),
            P(("dp", "fsdp"), None),
            P(("dp", "fsdp"), None),
            P(("dp", "fsdp"), None),
            P(("dp", "fsdp"), None),
            P(),
            P(),
            P(),
            P(),
            P(),
            P(),
            P(),
            P(),
            P(),
        ),
        check_vma=False,
    )
```

```python
import math

import jax
import jax.numpy as jnp
from jax import lax
from jax.experimental import pallas as pl
from jax.experimental.pallas import tpu as pltpu
from jax.sharding import PartitionSpec as P

D = 768
H = 12
HD = 64
FF = 3072
B1 = 32
BX = 64
SEQ = 512
STEP = 10
BUCKETS = B1 + 2 * BX


NEG_FILL = -1e30
NORM_EPS = 1e-05
BF = jnp.bfloat16
F32 = jnp.float32
NT = (((1,), (1,)), ((), ()))
TN = (((0,), (0,)), ((), ()))
NN = (((1,), (0,)), ((), ()))
ALL = ("dp", "fsdp")
COST = 1_000_000
SPLIT = (4, 2, 2, 2)
BLOCKS = 32
A_ROWS = 4 * D // BLOCKS
F_ROWS = 2 * FF // BLOCKS
HALF = FF // 2
ANY = pl.BlockSpec(memory_space=pl.ANY)


def mm(a, b, dims):
    return lax.dot_general(a, b, dims, preferred_element_type=F32)


def adam_update(weight, moment_one, second, gradient, clip_scale, step_rate, decay_rate, average):
    clipped = gradient * clip_scale
    new_first = 0.9 * moment_one + 0.1 * clipped
    new_second = 0.999 * second + 0.001 * clipped * clipped
    first_hat = new_first / (1.0 - 0.9**STEP)
    second_hat = new_second / (1.0 - 0.999**STEP)
    new_weight = weight - step_rate * (
        first_hat / (jnp.sqrt(second_hat) + 1e-08) + decay_rate * weight
    )
    new_average = 0.8 * average + 0.2 * new_weight
    return (new_weight, new_first, new_second, new_average)


def bias_kernel(len_ref, tab_ref, one_ref, x_ref, y_ref, out_ref):
    length = len_ref[0]
    rows = one_ref.shape[1]

    def eight(i, _):
        r = pl.ds(pl.multiple_of(i * 8, 8), 8)
        for c in range(0, SEQ, 128):
            ids = [ref[0, r, c : c + 128] for ref in (one_ref, x_ref, y_ref)]
            keep = lax.broadcasted_iota(jnp.int32, (8, 128), 1) + c < length
            for h in range(H):
                total = None
                for t in range(3):
                    line = jnp.broadcast_to(tab_ref[h, t : t + 1, :], (8, 128))
                    got = jnp.take_along_axis(line, ids[t], axis=1, mode="promise_in_bounds")
                    total = got if total is None else total + got
                out_ref[h, r, c : c + 128] = jnp.where(keep, total, NEG_FILL)
        return 0

    lax.fori_loop(0, rows // 8, eight, 0)


PARTS = 2
BIAS_ROWS = ((0, 128), (128, 320), (448, 64))


def bias_lines(table):
    lines = table.T
    return jnp.stack(
        [
            jnp.pad(lines[:, :B1], ((0, 0), (0, 128 - B1))),
            jnp.pad(lines[:, B1 : B1 + BX], ((0, 0), (0, 128 - BX))),
            jnp.pad(lines[:, B1 + BX :], ((0, 0), (0, 128 - BX))),
        ],
        axis=1,
    )


def page_bias(lengths, tab, rel, part, out):
    rows = 64
    first, count = BIAS_ROWS[part][0] // rows, BIAS_ROWS[part][1] // rows
    ids = pl.BlockSpec((1, rows, SEQ), lambda i, *_: (0, first + i, 0))
    extra = [] if out is None else [out]
    return pl.pallas_call(
        lambda *refs: bias_kernel(*refs[:5], refs[-1]),
        grid_spec=pltpu.PrefetchScalarGridSpec(
            num_scalar_prefetch=1,
            grid=(count,),
            in_specs=[pl.BlockSpec((H, 3, 128), lambda i, *_: (0, 0, 0)), ids, ids, ids]
            + [ANY] * len(extra),
            out_specs=pl.BlockSpec((H, rows, SEQ), lambda i, *_: (0, first + i, 0)),
        ),
        out_shape=jax.ShapeDtypeStruct((H, SEQ, SEQ), F32),
        input_output_aliases={5: 0} if extra else {},
        cost_estimate=pl.CostEstimate(
            flops=COST, bytes_accessed=COST, transcendentals=0
        ),
        name="bias",
    )(lengths, tab, *rel, *extra)


def head_masks():
    lane = lax.broadcasted_iota(jnp.int32, (1, 2 * HD), 1)
    return (lane < HD, lane >= HD)


def attend_kernel(q_ref, k_ref, v_ref, bias_ref, ctx_ref, p_ref, *, rows):
    zero = jnp.zeros((), BF)
    masks = head_masks()
    keys = [jnp.where(m, k_ref[...], zero) for m in masks]
    vals = [jnp.where(m, v_ref[...], zero) for m in masks]
    for r in range(0, SEQ, rows):
        q = q_ref[r : r + rows, :]
        ctx = None
        for h in range(2):
            scores = mm(q, keys[h], NT) * HD ** (-0.5) + bias_ref[h, r : r + rows, :]
            top = jnp.max(scores, axis=-1, keepdims=True)
            raised = jnp.exp(scores - top)
            total = jnp.sum(raised, axis=-1, keepdims=True)
            soft = (raised * (1.0 / total)).astype(BF)
            p_ref[h, r : r + rows, :] = soft
            part = mm(soft, vals[h], NN)
            ctx = part if ctx is None else ctx + part
        ctx_ref[r : r + rows, :] = ctx.astype(BF)


def lane_block(offset):
    return pl.BlockSpec((SEQ, 2 * HD), lambda i: (0, offset + i))


PAIR_BLOCK = pl.BlockSpec((2, SEQ, SEQ), lambda i: (i, 0, 0))


def attend(qkv, bias):
    n = D // (2 * HD)
    return pl.pallas_call(
        lambda *refs: attend_kernel(*refs, rows=256),
        grid=(n,),
        in_specs=[lane_block(0), lane_block(n), lane_block(2 * n), PAIR_BLOCK],
        out_specs=[lane_block(0), PAIR_BLOCK],
        out_shape=[
            jax.ShapeDtypeStruct((SEQ, D), BF),
            jax.ShapeDtypeStruct((H, SEQ, SEQ), BF),
        ],
        cost_estimate=pl.CostEstimate(
            flops=COST, bytes_accessed=COST, transcendentals=0
        ),
        name="attend",
    )(qkv, qkv, qkv, bias)


def attend_back_kernel(
    q_ref, k_ref, v_ref, p_ref, c_ref, dc_ref, dq_ref, dk_ref, dv_ref, ds_ref, sum_ref, *, rows
):
    zero = jnp.zeros((), BF)
    masks = head_masks()
    keys = [jnp.where(m, k_ref[...], zero) for m in masks]
    vals = [jnp.where(m, v_ref[...], zero) for m in masks]
    scale = HD ** (-0.5)
    q_sum = jnp.zeros((1, 2 * HD), F32)
    for r in range(0, SEQ, rows):
        dc = dc_ref[r : r + rows, :]
        prod = dc.astype(F32) * c_ref[r : r + rows, :].astype(F32)
        dq = None
        for h in range(2):
            soft = p_ref[h, r : r + rows, :]
            inner = jnp.sum(jnp.where(masks[h], prod, 0.0), axis=-1, keepdims=True)
            d_soft = mm(dc, vals[h], NT)
            d_scores = (soft.astype(F32) * (d_soft - inner)).astype(BF)
            ds_ref[h, r : r + rows, :] = d_scores
            part = mm(d_scores, keys[h], NN)
            dq = part if dq is None else dq + part
        dq = (dq * scale).astype(BF)
        dq_ref[r : r + rows, :] = dq
        q_sum = q_sum + jnp.sum(dq.astype(F32), axis=0, keepdims=True)
    flips = (dc_ref[...].astype(F32).T.astype(BF), q_ref[...].astype(F32).T.astype(BF))
    sums = [q_sum]
    for flip, factor, pair_ref, out_ref in (
        (flips[0], 1.0, p_ref, dv_ref),
        (flips[1], scale, ds_ref, dk_ref),
    ):
        parts = [mm(flip[HD * h : HD * h + HD, :], pair_ref[h], NN) for h in range(2)]
        done = (jnp.concatenate(parts, axis=0).T * factor).astype(BF)
        out_ref[...] = done
        sums.append(jnp.sum(done.astype(F32), axis=0, keepdims=True))
    sum_ref[...] = jnp.concatenate(sums[:2] + [jnp.zeros((6, 2 * HD), F32)], axis=0)


def attend_back(qkv, soft, ctx, d_ctx):
    n = D // (2 * HD)
    return pl.pallas_call(
        lambda *refs: attend_back_kernel(*refs, rows=256),
        grid=(n,),
        in_specs=[
            lane_block(0),
            lane_block(n),
            lane_block(2 * n),
            PAIR_BLOCK,
            lane_block(0),
            lane_block(0),
        ],
        out_specs=[
            lane_block(0),
            lane_block(0),
            lane_block(0),
            PAIR_BLOCK,
            pl.BlockSpec((8, 2 * HD), lambda i: (0, i)),
        ],
        out_shape=[jax.ShapeDtypeStruct((SEQ, D), BF)] * 3
        + [jax.ShapeDtypeStruct((H, SEQ, SEQ), BF), jax.ShapeDtypeStruct((8, D), F32)],
        cost_estimate=pl.CostEstimate(
            flops=COST, bytes_accessed=COST, transcendentals=0
        ),
        name="attend_back",
    )(qkv, qkv, qkv, soft, ctx, d_ctx)


def table_kernel(one_ref, x_ref, y_ref, ds_ref, out_ref):
    @pl.when(pl.program_id(0) == 0)
    def _():
        out_ref[...] = jnp.zeros_like(out_ref)

    rows = one_ref.shape[1]
    flipped = jnp.swapaxes(ds_ref[...].astype(F32), 0, 1).astype(BF)
    total = None
    for r in range(rows):
        hot = jnp.concatenate(
            [
                (lax.broadcasted_iota(jnp.int32, (size, SEQ), 0) == ref[0, r : r + 1, :])
                .astype(F32)
                .astype(BF)
                for ref, size in ((one_ref, B1), (x_ref, BX), (y_ref, BX))
            ],
            axis=0,
        )
        part = mm(flipped[r], hot, NT)
        total = part if total is None else total + part
    out_ref[...] += total


def table_grad(rel_1d, rel_x, rel_y, d_scores, part):
    rows = 16
    count = SEQ // rows // PARTS
    first = part * count
    ids = pl.BlockSpec((1, rows, SEQ), lambda i: (0, first + i, 0))
    return pl.pallas_call(
        table_kernel,
        grid=(count,),
        in_specs=[ids, ids, ids, pl.BlockSpec((H, rows, SEQ), lambda i: (0, first + i, 0))],
        out_specs=pl.BlockSpec((H, BUCKETS), lambda i: (0, 0)),
        out_shape=jax.ShapeDtypeStruct((H, BUCKETS), F32),
        cost_estimate=pl.CostEstimate(
            flops=COST, bytes_accessed=COST, transcendentals=0
        ),
        name="table_grad",
    )(rel_1d, rel_x, rel_y, d_scores)


def spread(size, plan):
    found = []
    for whole in plan:
        at, pieces = 0, []
        for z, x, y, first, last in whole:
            rows = (last - first) * size // 2
            pieces.append((at, rows, z, x, y, first * size // 2))
            at += rows
        found.append(pieces)
    return found


def blocks(zs, x, y):
    return [(z, x, y, 0, 2) for z in zs]


ATTN_PLAN = spread(
    A_ROWS,
    [
        blocks(range(4), 0, 0),
        blocks(range(4), 1, 0),
        blocks(range(4), 0, 1),
        blocks((0, 1), 1, 1),
        blocks((2, 3), 1, 1),
    ],
)
FFN_PLAN = spread(
    F_ROWS,
    [
        blocks((0,), 0, 0),
        blocks((0,), 1, 0),
        blocks((0,), 0, 1),
        blocks((1, 2, 3), 0, 0),
        blocks((1, 2, 3), 1, 0),
        blocks((1, 2, 3), 0, 1),
        blocks((0, 1), 1, 1),
        blocks((2, 3), 1, 1),
    ],
)
A_COPIES = 2 * sum(len(pieces) for pieces in ATTN_PLAN)
F_COPIES = 2 * sum(len(pieces) for pieces in FFN_PLAN)


def joined(plan):
    start, found = 0, []
    for pieces in plan:
        found += [(start + first, *rest) for first, *rest in pieces]
        start += sum(piece[1] for piece in pieces)
    return [found]


ATTN_FAR, FFN_FAR = joined(ATTN_PLAN[:3]) + ATTN_PLAN[3:], FFN_PLAN


def piece_list(plans, refs):
    found = []
    for core, plan in enumerate(plans):
        for pieces, ref in zip(plan, refs[len(plans[0]) * core :]):
            for start, rows, z, x, y, offset in pieces:
                found.append((core, z, x, y, offset, rows, ref.at[pl.ds(start, rows), :]))
    return found


def qkv_kernel(at_ref, tok_ref, add_ref, *refs):
    qkv_ref, all_ref, weight_ref, sems, done = refs[len(ATTN_PLAN) + len(ATTN_FAR) :]
    copies = []
    for n, (core, z, x, y, offset, rows, ref) in enumerate(piece_list((ATTN_PLAN, ATTN_FAR), refs)):
        block = (
            ((at_ref[0] ^ z) * 2 + (at_ref[1] ^ x)) * 2 + (at_ref[2] ^ y)
        ) * 2 + (at_ref[3] ^ core)
        spot = pl.ds(pl.multiple_of(block * A_ROWS + offset, 16), rows)
        copies.append(pltpu.make_async_copy(ref, weight_ref.at[spot, :], sems.at[n]))
    for copy in copies:
        copy.start()
    for copy in copies:
        copy.wait()
    store = pltpu.make_async_copy(weight_ref, all_ref, done)
    store.start()
    for t in range(3):
        part = slice(D * t, D * t + D)
        qkv_ref[:, part] = (mm(tok_ref[...], weight_ref[part, :], NN) + add_ref[:, part]).astype(BF)
    store.wait()


def project(at, tokens, add_three, pieces):
    count = tokens.shape[0]
    vmem = pl.BlockSpec(memory_space=pltpu.VMEM)
    return pl.pallas_call(
        qkv_kernel,
        in_specs=[pl.BlockSpec(memory_space=pltpu.SMEM), vmem, vmem] + [ANY] * len(pieces),
        out_specs=[vmem, ANY],
        out_shape=[
            jax.ShapeDtypeStruct((count, 3 * D), BF),
            jax.ShapeDtypeStruct((4 * D, D), BF),
        ],
        scratch_shapes=[
            pltpu.VMEM((4 * D, D), BF),
            pltpu.SemaphoreType.DMA((A_COPIES,)),
            pltpu.SemaphoreType.DMA,
        ],
        cost_estimate=pl.CostEstimate(
            flops=COST, bytes_accessed=COST, transcendentals=0
        ),
        name="project",
    )(at, tokens, add_three, *pieces)


def grad_ffn_kernel(at_ref, *refs, high):
    wide, slim, outs, (left, right, sems) = refs[:4], refs[4:8], refs[8:11], refs[11:]
    which = (at_ref[0] // 2) ^ high
    for w in range(2):

        @pl.when(which == w)
        def _():
            copies = []
            for i in range(2):
                rows = pl.ds(SEQ * i, SEQ)
                copies.append(
                    pltpu.make_async_copy(wide[2 * w + i], left.at[rows, :], sems.at[2 * i])
                )
                copies.append(
                    pltpu.make_async_copy(slim[2 * w + i], right.at[rows, :], sems.at[2 * i + 1])
                )
            for copy in copies:
                copy.start()
            for copy in copies:
                copy.wait()

    own, kept, sent = outs
    for z in range(2):
        done = mm(left[:, HALF // 2 * z : HALF // 2 * (z + 1)], right[...], TN).astype(BF)
        rows = [done[F_ROWS * q : F_ROWS * q + F_ROWS, :] for q in range(4)]
        own[z] = rows[0]
        kept[z] = rows[1 if high else 2]
        sent[z] = rows[3]
        sent[2 + z] = rows[2 if high else 1]


def grad_ffn(at, wide, slim, high):
    shape = lambda n: jax.ShapeDtypeStruct((n, F_ROWS, D), BF)
    return pl.pallas_call(
        lambda *refs: grad_ffn_kernel(*refs, high=high),
        in_specs=[pl.BlockSpec(memory_space=pltpu.SMEM)] + [ANY] * 8,
        out_specs=[pl.BlockSpec(memory_space=pltpu.VMEM)] * 3,
        out_shape=[shape(2), shape(2), shape(4)],
        scratch_shapes=[
            pltpu.VMEM((2 * SEQ, HALF), BF),
            pltpu.VMEM((2 * SEQ, D), BF),
            pltpu.SemaphoreType.DMA((4,)),
        ],
        cost_estimate=pl.CostEstimate(
            flops=COST, bytes_accessed=COST, transcendentals=0
        ),
        name="grad_ffn",
    )(at, *wide, *slim)


def grad_attn_kernel(at_ref, tok_ref, tok_far, ctx_ref, ctx_far, *refs):
    grads, outs, (flip, left, right, sems) = refs[:8], refs[8:14], refs[14:]
    copies = []
    for t in range(4):
        for i in range(2):
            spot = right.at[t, pl.ds(SEQ * i, SEQ), :]
            copies.append(pltpu.make_async_copy(grads[2 * t + i], spot, sems.at[2 * t + i]))
    for copy in copies:
        copy.start()
    for n, (near, far) in enumerate(((tok_ref, tok_far), (ctx_ref, ctx_far))):
        flip[:, :SEQ] = near[...].astype(F32).T.astype(BF)
        flip[:, SEQ:] = far[...].astype(F32).T.astype(BF)
        for q in range(4):
            block = (((at_ref[1] ^ (q // 2)) * 2 + (at_ref[2] ^ (q % 2))) * 2) + at_ref[3]
            spot = pl.ds(pl.multiple_of(block * A_ROWS, A_ROWS), A_ROWS)
            left[n, A_ROWS * q : A_ROWS * q + A_ROWS, :] = flip[spot, :]
    for copy in copies:
        copy.wait()
    for z in range(4):
        which = at_ref[0] ^ z
        done = mm(left[which // 3], right[which], NN).astype(BF)
        rows = [done[A_ROWS * q : A_ROWS * q + A_ROWS, :] for q in range(4)]
        own, kept, sent = outs[3 * (z // 2) : 3 * (z // 2) + 3]
        own[z % 2] = rows[0]
        kept[z % 2] = rows[1 if z // 2 else 2]
        sent[z % 2] = rows[3]
        sent[2 + z % 2] = rows[2 if z // 2 else 1]


def grad_attn(at, tokens, tokens_far, ctx, ctx_far, grads):
    shape = lambda n: jax.ShapeDtypeStruct((n, A_ROWS, D), BF)
    vmem = pl.BlockSpec(memory_space=pltpu.VMEM)
    return pl.pallas_call(
        grad_attn_kernel,
        in_specs=[pl.BlockSpec(memory_space=pltpu.SMEM)] + [vmem] * 4 + [ANY] * 8,
        out_specs=[vmem] * 6,
        out_shape=[shape(2), shape(2), shape(4)] * 2,
        scratch_shapes=[
            pltpu.VMEM((D, 2 * SEQ), BF),
            pltpu.VMEM((2, D // 2, 2 * SEQ), BF),
            pltpu.VMEM((4, 2 * SEQ, D), BF),
            pltpu.SemaphoreType.DMA((8,)),
        ],
        cost_estimate=pl.CostEstimate(
            flops=COST, bytes_accessed=COST, transcendentals=0
        ),
        name="grad_attn",
    )(at, tokens, tokens_far, ctx, ctx_far, *grads)


def row_mean(values):
    return jnp.mean(values, axis=-1, keepdims=True)


def normal_rows(values):
    center = values - row_mean(values)
    inv = lax.rsqrt(row_mean(center * center) + NORM_EPS)
    return center * inv, inv


def normal_back(normal, inv, grad):
    return inv * (grad - row_mean(grad) - normal * row_mean(grad * normal))


def gelu_parts(u):
    z = jnp.abs(u) * (2.0**-0.5)
    t = 1.0 / (1.0 + 0.3275911 * z)
    tail = jnp.exp(-0.5 * u * u)
    poly = t * (
        0.254829592
        + t * (-0.284496736 + t * (1.421413741 + t * (-1.453152027 + t * 1.061405429)))
    )
    half = 0.5 * poly * tail
    cdf = jnp.where(u < 0, half, 1.0 - half)
    return u * cdf, cdf + u * (tail * (1.0 / math.sqrt(2.0 * math.pi)))


def row_sum(values):
    return jnp.sum(values.astype(F32), axis=0, keepdims=True)


def block_kernel(
    at_ref,
    ctx_ref,
    tok_ref,
    cot_ref,
    vec_ref,
    b1_ref,
    wo_ref,
    *refs,
    wide,
):
    split = len(FFN_PLAN) + len(FFN_FAR)
    pieces, refs = refs[:split], refs[split:]
    out_ref, hid_ref, act_near, act_far, dff_ref, du_near, du_far = refs[:7]
    dr_ref, dab_ref, dctx_ref, sum_ref, db1_ref, slope_ref, ffn_ref, sems = refs[7:]
    copies = []
    for n, (core, z, x, y, offset, rows, ref) in enumerate(piece_list((FFN_PLAN, FFN_FAR), pieces)):
        spot = pl.ds(core * HALF + ((z % 2) * 4 + x * 2 + y) * F_ROWS + offset, rows)
        which = (at_ref[0] // 2) ^ (z // 2)
        copies.append(pltpu.make_async_copy(ref, ffn_ref.at[which, spot, :], sems.at[n]))
    w1_ref, w2_ref = ffn_ref.at[0], ffn_ref.at[1]

    @pl.when(pl.program_id(0) == 0)
    def _():
        for copy in copies:
            copy.start()
        sum_ref[...] = jnp.zeros_like(sum_ref)
        db1_ref[...] = jnp.zeros_like(db1_ref)

    vec = [vec_ref[i : i + 1, :] for i in range(8)]
    resid = tok_ref[...].astype(F32) + (mm(ctx_ref[...], wo_ref[...], NN) + vec[6])
    n_one, inv_one = normal_rows(resid)
    hidden = n_one * vec[0] + vec[1]
    hid_low = hidden.astype(BF)
    hid_ref[...] = hid_low
    total = hidden + vec[7]

    @pl.when(pl.program_id(0) == 0)
    def _():
        for copy in copies:
            copy.wait()

    for f in range(0, FF, wide):
        part = slice(f, f + wide)
        u = mm(hid_low, w1_ref[part, :], NT) + b1_ref[:, part]
        act, slope = gelu_parts(u)
        act = act.astype(BF)
        side = slice(f % HALF, f % HALF + wide)
        (act_near if f < HALF else act_far)[:, side] = act
        slope_ref[:, part] = slope
        total = total + mm(act, w2_ref[part, :], NN)
    n_two, inv_two = normal_rows(total)
    out_ref[...] = (n_two * vec[2] + vec[3]).astype(BF)
    dy = cot_ref[...].astype(F32)
    d_two = normal_back(n_two, inv_two, dy * vec[2])
    dff = d_two.astype(BF)
    dff_ref[...] = dff
    d_hid = d_two
    for f in range(0, FF, wide):
        part = slice(f, f + wide)
        du = (mm(dff, w2_ref[part, :], NT) * slope_ref[:, part]).astype(BF)
        side = slice(f % HALF, f % HALF + wide)
        (du_near if f < HALF else du_far)[:, side] = du
        db1_ref[:, part] += row_sum(du)
        d_hid = d_hid + mm(du, w1_ref[part, :], NN)
    d_one = normal_back(n_one, inv_one, d_hid * vec[0])
    dr_ref[...] = d_one
    dab = d_one.astype(BF)
    dab_ref[...] = dab
    dctx_ref[...] = mm(dab, wo_ref[...], NT).astype(BF)
    sum_ref[...] += jnp.concatenate(
        [
            row_sum(d_hid * n_one),
            row_sum(d_hid),
            row_sum(dy * n_two),
            row_sum(dy),
            jnp.zeros((2, D), F32),
            row_sum(dab),
            row_sum(dff),
        ],
        axis=0,
    )


def block_pass(at, ctx, tokens, cotangent, vectors, b_first, attn_full, pieces):
    rows = 256
    by_row = lambda width: pl.BlockSpec((rows, width), lambda i, *_: (i, 0))
    whole = lambda shape, first=0: pl.BlockSpec(
        shape, lambda i, *_: (first, 0), pipeline_mode=pl.Buffered(1)
    )
    count = tokens.shape[0]
    low = lambda width: jax.ShapeDtypeStruct((count, width), BF)
    return pl.pallas_call(
        lambda *refs: block_kernel(*refs, wide=768),
        grid_spec=pltpu.PrefetchScalarGridSpec(
            num_scalar_prefetch=1,
            grid=(count // rows,),
            in_specs=[
                by_row(D),
                by_row(D),
                by_row(D),
                whole((12, D)),
                whole((1, FF)),
                whole((D, D), 3),
            ]
            + [ANY] * len(pieces),
            out_specs=[
                by_row(D),
                by_row(D),
                by_row(HALF),
                by_row(HALF),
                by_row(D),
                by_row(HALF),
                by_row(HALF),
                by_row(D),
                by_row(D),
                by_row(D),
                pl.BlockSpec((8, D), lambda i, *_: (0, 0)),
                pl.BlockSpec((1, FF), lambda i, *_: (0, 0)),
            ],
            scratch_shapes=[
                pltpu.VMEM((rows, FF), F32),
                pltpu.VMEM((2, FF, D), BF),
                pltpu.SemaphoreType.DMA((F_COPIES,)),
            ],
        ),
        out_shape=[
            low(D),
            low(D),
            low(HALF),
            low(HALF),
            low(D),
            low(HALF),
            low(HALF),
            jax.ShapeDtypeStruct((count, D), F32),
            low(D),
            low(D),
            jax.ShapeDtypeStruct((8, D), F32),
            jax.ShapeDtypeStruct((1, FF), F32),
        ],
        cost_estimate=pl.CostEstimate(
            flops=COST, bytes_accessed=COST, transcendentals=0
        ),
        name="block_pass",
    )(at, ctx, tokens, cotangent, vectors, b_first, attn_full, *pieces)


def swap(array, mask):
    return lax.ppermute(array, ALL, [(i, i ^ mask) for i in range(BLOCKS)])


def together(*groups):
    return lax.optimization_barrier(groups)


def tie(arrays, after):
    return lax.optimization_barrier((arrays, after))[0]


def column(shard, zs):
    return jnp.concatenate([shard if z == 0 else swap(shard, 8 * z) for z in zs])


def gather_full(shard, plans):
    full = lax.all_gather(shard, ALL, axis=0, tiled=True)
    view = full.reshape(*SPLIT, full.shape[0] // BLOCKS, D)
    return tuple(
        jnp.concatenate([view[z, x, y, core, off : off + n] for _, n, z, x, y, off in pieces])
        for core, plan in enumerate(plans)
        for pieces in plan
    )


def wide(array):
    return array.astype(F32)


def scatter_first(low, high):
    return swap(low[2], 2), swap(high[2], 4)


def scatter_sums(low, high, from_y, from_x):
    to_x = (wide(low[1]) + wide(from_y[:2])).astype(BF)
    to_y = (wide(high[1]) + wide(from_x[:2])).astype(BF)
    return to_x, to_y


def scatter_second(to_x, to_y):
    return swap(to_x, 4), swap(to_y, 2)


def scatter_third(low, high, from_y, from_x, last_x, last_y):
    low = wide(low[0]) + wide(from_y[2:]) + wide(last_x)
    high = wide(high[0]) + wide(from_x[2:]) + wide(last_y)
    send = (low[1].astype(BF), high[0].astype(BF), high[1].astype(BF))
    return low[0], tuple(swap(a, 8 * z) for z, a in zip((1, 2, 3), send))


def scatter_full(sides):
    cores = []
    for low, high in sides:
        rows = [(low[0], high[0]), (low[2][2:], high[1]), (low[1], high[2][2:])]
        rows.append((low[2][:2], high[2][:2]))
        cores.append(jnp.stack([jnp.concatenate(pair) for pair in rows], axis=1))
    full = jnp.stack(cores, axis=2).reshape(-1, D)
    return lax.psum_scatter(full, ALL, scatter_dimension=0, tiled=True).astype(F32)


def flip_bits(array, at):
    for axis, bit in enumerate((at[0] % 2, at[1], at[2], at[3])):
        array = jnp.where(bit == 1, jnp.flip(array, axis), array)
    return array


LANES = 256


def pack_table(grad):
    return jnp.pad(grad, ((0, 0), (0, LANES - BUCKETS))).reshape(H * LANES // D, D)


def update_kernel(total_ref, attn_sum, ffn_sum, *refs):
    states, outs = [refs[4 * i : 4 * i + 4] for i in range(4)], refs[16:]
    per = D // LANES
    vec_total = total_ref[:H, :]
    heads = jnp.concatenate(
        [
            total_ref[H + h // per : H + h // per + 1, LANES * (h % per) : LANES * (h % per + 1)]
            for h in range(H)
        ],
        axis=0,
    )
    square = total_ref[H : H + 1, LANES - 1 : LANES]
    lane = lax.broadcasted_iota(jnp.int32, heads.shape, 1)
    tab_total = jnp.where(lane < BUCKETS, heads, 0.0)
    rows = jnp.sum(tab_total * tab_total, axis=0, keepdims=True)
    square = square + jnp.sum(rows, axis=1, keepdims=True)
    rows = jnp.sum(vec_total * vec_total, axis=0, keepdims=True)
    norm = jnp.sqrt(square + jnp.sum(rows, axis=1, keepdims=True))
    scale = 1.0 / jnp.maximum(norm, 1.0)
    outs[0][...] = norm
    outs[1][...] = vec_total * scale
    totals = (attn_sum[...], ffn_sum[...], vec_total, heads[:H, :BUCKETS])
    for i, (state, total) in enumerate(zip(states, totals)):
        rate, decay = (0.06, 0.01) if i < 2 else (0.6, 0.0)
        weight, first, second, average = (ref[...] for ref in state)
        new = adam_update(weight, first, second, total, scale, rate, decay, average)
        for out, value in zip(outs[2 + 4 * i :], new):
            out[...] = value


def update(total, attn_sum, ffn_sum, states):
    like = lambda a: jax.ShapeDtypeStruct(a.shape, F32)
    one = jax.ShapeDtypeStruct((1, 1), F32)
    steps = 4 if attn_sum.shape[0] % 32 == 0 else 1
    whole = lambda shape: pl.BlockSpec(shape, lambda i: (0, 0))
    part = lambda a: pl.BlockSpec((a.shape[0] // steps, D), lambda i: (i, 0))
    states_specs = [part(a) for a in states[:8]] + [whole(a.shape) for a in states[8:]]
    return pl.pallas_call(
        update_kernel,
        grid=(steps,),
        in_specs=[whole(total.shape), part(attn_sum), part(ffn_sum)] + states_specs,
        out_specs=[whole((1, 1)), whole(states[8].shape)] + states_specs,
        out_shape=[one, like(states[8])] + [like(a) for a in states],
        name="update",
    )(total, attn_sum, ffn_sum, *states)


def hidden_bias(vectors, at):
    flipped = flip_bits(vectors[8:].reshape(2, 2, 2, 2, F_ROWS), at)
    return flipped.transpose(3, 0, 1, 2, 4).reshape(1, FF)


def input_grad(start, d_three, attn_full, which=(0, 1, 2)):
    for t in which:
        start = start + mm(d_three[t], attn_full[D * t : D * t + D], NT)
    return start


def shards(
    tokens,
    cotangent,
    lengths,
    rel_1d,
    rel_x,
    rel_y,
    attn_weights,
    attn_m1,
    attn_m2,
    attn_ema,
    ffn_weights,
    ffn_m1,
    ffn_m2,
    ffn_ema,
    vectors,
    vec_m1,
    vec_m2,
    vec_ema,
    table,
    tab_m1,
    tab_m2,
    tab_ema,
    *,
    direct,
):
    attn_low, ffn_low = attn_weights.astype(BF), ffn_weights.astype(BF)
    rel = (rel_1d, rel_x, rel_y)
    tab = bias_lines(table)
    add_three = jnp.concatenate([vectors[4], jnp.zeros((D,), F32), vectors[5]]).reshape(1, 3 * D)
    if direct:
        dp, fsdp = lax.axis_index("dp"), lax.axis_index("fsdp")
        at = jnp.stack([dp // 2, dp % 2, fsdp // 2, fsdp % 2]).astype(jnp.int32)
        far = lambda a: swap(a, 1)
        b_first = hidden_bias(vectors, at)
        attn_column = column(attn_low, range(4))
        ffn_x, ffn_y = swap(ffn_low, 4), swap(ffn_low, 2)
        bias = page_bias(lengths, tab, rel, 0, None)
        attn_column, ffn_x, ffn_y, later, bias, at, b_first, add_three = together(
            attn_column, ffn_x, ffn_y, ffn_low, bias, at, b_first, add_three
        )
        beside, above = swap(attn_column, 4), swap(attn_column, 2)
        ffn_column = column(later, (1, 2, 3))
        bias = page_bias(lengths, tab, rel, 1, bias)
        beside, above, bias = together(beside, above, bias)
        near, ffn_column, bias = together((attn_column, beside, above), ffn_column, bias)
        side = 2 * A_ROWS
        low, high = swap(near[1][:side], 2), swap(near[2][side:], 4)
        beside, above = swap(ffn_column, 4), swap(ffn_column, 2)
        away = swap(jnp.concatenate(near), 1)
        bias = page_bias(lengths, tab, rel, 2, bias)
        last, away, bias, start = together((low, high), away, bias, (ffn_low, ffn_x, ffn_y))
        attn_pieces = near + last + (away,) + tuple(swap(piece, 1) for piece in last)
        first = tuple(swap(piece, 1) for piece in start)
        qkv, attn_full = project(at, tokens, add_three, attn_pieces)
        first, beside, above, qkv = together(first, beside, above, qkv)
        low = swap(jnp.concatenate([start[1], beside[:F_ROWS]]), 2)
        high = swap(above[F_ROWS:], 4)
        middle = (ffn_column, beside, above)
        away = tuple(swap(piece, 1) for piece in middle)
        ctx, soft = attend(qkv, bias)
        last, away, ctx = together((low, high), away, ctx)
        ffn_pieces = start + middle + last + first + away + tuple(swap(a, 1) for a in last)
    else:
        at = jnp.zeros((4,), jnp.int32)
        b_first = hidden_bias(vectors, at)
        far = jnp.zeros_like
        bias = None
        for part in range(len(BIAS_ROWS)):
            bias = page_bias(lengths, tab, rel, part, bias)
        attn_pieces = gather_full(attn_low, (ATTN_PLAN, ATTN_FAR))
        ffn_pieces = gather_full(ffn_low, (FFN_PLAN, FFN_FAR))
        qkv, attn_full = project(at, tokens, add_three, attn_pieces)
        ctx, soft = attend(qkv, bias)
        tokens_far, ctx_far = far(tokens), far(ctx)
    (
        block_out,
        hid,
        act_near,
        act_away,
        d_ffn,
        du_near,
        du_away,
        d_resid_one,
        d_attn,
        d_context,
        sums,
        grad_bias_first,
    ) = block_pass(at, ctx, tokens, cotangent, vectors, b_first, attn_full, ffn_pieces)
    away = (far(du_away), far(act_away), far(hid), far(d_ffn), far(d_attn))
    dq, dk, dv, d_scores, qv_sums = attend_back(qkv, soft, ctx, d_context)
    d_three = (dq, dk, dv)
    if direct:
        away, d_three, d_scores, rows = together(away, d_three, d_scores, (tokens, ctx))
        du_far, act_far, hid_far, d_ffn_far, d_attn_far = away
        wide_ones, slim = (du_near, du_far, act_near, act_far), (hid, hid_far, d_ffn, d_ffn_far)
        low = grad_ffn(at, wide_ones, slim, 0)
        three_far = tuple(far(d) for d in d_three + rows)
        low, three_far, wide_ones = together(low, three_far, wide_ones)
        high = grad_ffn(at, wide_ones, slim, 1)
        grads = [g for pair in zip(d_three, three_far[:3]) for g in pair] + [d_attn, d_attn_far]
        high, grads = together(high, grads)
        ffn_first = scatter_first(low, high)
        parts = grad_attn(at, tokens, three_far[3], ctx, three_far[4], grads)
        parts, d_scores = together(parts, d_scores)
        attn_first = scatter_first(parts[:3], parts[3:])
        tables = [table_grad(*rel, d_scores, 0)]
        ffn_first, d_scores, tables[0] = together(ffn_first, d_scores, tables[0])
        ffn_second = scatter_second(*scatter_sums(low, high, *ffn_first))
        tables.append(table_grad(*rel, d_scores, 1))
        attn_first, ffn_second, d_three, tables[1] = together(
            attn_first, ffn_second, d_three, tables[1]
        )
        ffn_own, ffn_three = scatter_third(low, high, *ffn_first, *ffn_second)
        sent, d_three = together(scatter_sums(parts[:3], parts[3:], *attn_first), d_three)
        attn_second = scatter_second(*sent)
        grad_input = input_grad(d_resid_one, d_three, attn_full, (0, 1))
        late = (sums, qv_sums, grad_bias_first, tables, d_three[2])
        attn_second, grad_input, late = together(attn_second, grad_input, late)
        sums, qv_sums, grad_bias_first, tables, last_grad = late
        grad_input = input_grad(grad_input, (last_grad,), attn_full[2 * D :], (0,))
        attn_own, attn_three = scatter_third(parts[:3], parts[3:], *attn_first, *attn_second)
        ffn_shard = sum((wide(a) for a in ffn_three), ffn_own)
        attn_shard = sum((wide(a) for a in attn_three), attn_own)
    else:
        sides, attn_sides = [], []
        grads = [g for d in (*d_three, d_attn) for g in (d, far(d))]
        slim = (hid, far(hid), d_ffn, far(d_ffn))
        for core, (du, act) in enumerate(((du_near, act_near), (du_away, act_away))):
            wide_ones = (du, far(du), act, far(act))
            sides.append([grad_ffn(at, wide_ones, slim, side) for side in range(2)])
            spot = at.at[3].set(core)
            parts = grad_attn(spot, tokens, tokens_far, ctx, ctx_far, grads)
            attn_sides.append((parts[:3], parts[3:]))
        ffn_shard, attn_shard = scatter_full(sides), scatter_full(attn_sides)
        tables = [table_grad(*rel, d_scores, part) for part in range(PARTS)]
        grad_input = input_grad(d_resid_one, d_three, attn_full)
    grad_table = pack_table(sum(tables[1:], tables[0]))
    grad_bias_first = grad_bias_first.reshape(2, 2, 2, 2, F_ROWS).transpose(1, 2, 3, 0, 4)
    grad_bias_first = flip_bits(grad_bias_first, at).reshape(FF // D, D)
    small = jnp.concatenate([sums[:4], qv_sums[:2], sums[6:], grad_bias_first, grad_table], axis=0)
    squares = jnp.sum(attn_shard * attn_shard) + jnp.sum(ffn_shard * ffn_shard)
    row = lax.broadcasted_iota(jnp.int32, small.shape, 0)
    lane = lax.broadcasted_iota(jnp.int32, small.shape, 1)
    small = jnp.where((row == H) & (lane == LANES - 1), squares, small)
    if direct:
        for mask in (1, 2, 4, 8, 16):
            small = small + swap(small, mask)
    else:
        small = lax.psum(small, ALL)
    states = (attn_weights, attn_m1, attn_m2, attn_ema, ffn_weights, ffn_m1, ffn_m2, ffn_ema)
    states += (vectors, vec_m1, vec_m2, vec_ema, table.T, tab_m1.T, tab_m2.T, tab_ema.T)
    grad_norm, vec_grad, *new = update(small, attn_shard, ffn_shard, states)
    new = new[:12] + [array.T for array in new[12:]]
    return (block_out, grad_input, grad_norm.reshape(()), *new, vec_grad)


def solution(mesh):
    direct = mesh.shape["dp"] == SPLIT[0] * SPLIT[1] and mesh.shape["fsdp"] == SPLIT[2] * SPLIT[3]
    return jax.shard_map(
        lambda *arrays: shards(*arrays, direct=direct),
        mesh=mesh,
        in_specs=(
            P(("dp", "fsdp"), None),
            P(("dp", "fsdp"), None),
            P(("dp", "fsdp")),
            P(("dp", "fsdp"), None, None),
            P(("dp", "fsdp"), None, None),
            P(("dp", "fsdp"), None, None),
            P(("dp", "fsdp"), None),
            P(("dp", "fsdp"), None),
            P(("dp", "fsdp"), None),
            P(("dp", "fsdp"), None),
            P(("dp", "fsdp"), None),
            P(("dp", "fsdp"), None),
            P(("dp", "fsdp"), None),
            P(("dp", "fsdp"), None),
            P(),
            P(),
            P(),
            P(),
            P(),
            P(),
            P(),
            P(),
        ),
        out_specs=(
            P(("dp", "fsdp"), None),
            P(("dp", "fsdp"), None),
            P(),
            P(("dp", "fsdp"), None),
            P(("dp", "fsdp"), None),
            P(("dp", "fsdp"), None),
            P(("dp", "fsdp"), None),
            P(("dp", "fsdp"), None),
            P(("dp", "fsdp"), None),
            P(("dp", "fsdp"), None),
            P(("dp", "fsdp"), None),
            P(),
            P(),
            P(),
            P(),
            P(),
            P(),
            P(),
            P(),
            P(),
        ),
        check_vma=False,
    )
```

```python
import math

import jax
import jax.numpy as jnp
from jax import lax
from jax.experimental import pallas as pl
from jax.experimental.pallas import tpu as pltpu
from jax.sharding import PartitionSpec as P

D = 768
H = 12
HD = 64
FF = 3072
B1 = 32
BX = 64
SEQ = 512
STEP = 10
BUCKETS = B1 + 2 * BX


NEG_FILL = -1e30
NORM_EPS = 1e-05
BF = jnp.bfloat16
F32 = jnp.float32
NT = (((1,), (1,)), ((), ()))
TN = (((0,), (0,)), ((), ()))
NN = (((1,), (0,)), ((), ()))
ALL = ("dp", "fsdp")
COST = 1_000_000
SPLIT = (4, 2, 2, 2)
BLOCKS = 32
A_ROWS = 4 * D // BLOCKS
F_ROWS = 2 * FF // BLOCKS
HALF = FF // 2
ANY = pl.BlockSpec(memory_space=pl.ANY)


def mm(a, b, dims):
    return lax.dot_general(a, b, dims, preferred_element_type=F32)


def adam_update(weight, moment_one, second, gradient, clip_scale, step_rate, decay_rate, average):
    clipped = gradient * clip_scale
    new_first = 0.9 * moment_one + 0.1 * clipped
    new_second = 0.999 * second + 0.001 * clipped * clipped
    first_hat = new_first / (1.0 - 0.9**STEP)
    second_hat = new_second / (1.0 - 0.999**STEP)
    new_weight = weight - step_rate * (
        first_hat / (jnp.sqrt(second_hat) + 1e-08) + decay_rate * weight
    )
    new_average = 0.8 * average + 0.2 * new_weight
    return (new_weight, new_first, new_second, new_average)


def bias_kernel(len_ref, tab_ref, one_ref, x_ref, y_ref, out_ref):
    length = len_ref[0]
    rows = one_ref.shape[1]

    def eight(i, _):
        r = pl.ds(pl.multiple_of(i * 8, 8), 8)
        for c in range(0, SEQ, 128):
            ids = [ref[0, r, c : c + 128] for ref in (one_ref, x_ref, y_ref)]
            keep = lax.broadcasted_iota(jnp.int32, (8, 128), 1) + c < length
            for h in range(H):
                total = None
                for t in range(3):
                    line = jnp.broadcast_to(tab_ref[h, t : t + 1, :], (8, 128))
                    got = jnp.take_along_axis(line, ids[t], axis=1, mode="promise_in_bounds")
                    total = got if total is None else total + got
                out_ref[h, r, c : c + 128] = jnp.where(keep, total, NEG_FILL)
        return 0

    lax.fori_loop(0, rows // 8, eight, 0)


TABLE_ROWS = ((0, 256), (256, 160), (416, 96))
BIAS_ROWS = ((0, 128), (128, 320), (448, 64))


def bias_lines(table):
    lines = table.T
    return jnp.stack(
        [
            jnp.pad(lines[:, :B1], ((0, 0), (0, 128 - B1))),
            jnp.pad(lines[:, B1 : B1 + BX], ((0, 0), (0, 128 - BX))),
            jnp.pad(lines[:, B1 + BX :], ((0, 0), (0, 128 - BX))),
        ],
        axis=1,
    )


def page_bias(lengths, tab, rel, part, out):
    rows = 64
    first, count = BIAS_ROWS[part][0] // rows, BIAS_ROWS[part][1] // rows
    ids = pl.BlockSpec((1, rows, SEQ), lambda i, *_: (0, first + i, 0))
    extra = [] if out is None else [out]
    return pl.pallas_call(
        lambda *refs: bias_kernel(*refs[:5], refs[-1]),
        grid_spec=pltpu.PrefetchScalarGridSpec(
            num_scalar_prefetch=1,
            grid=(count,),
            in_specs=[pl.BlockSpec((H, 3, 128), lambda i, *_: (0, 0, 0)), ids, ids, ids]
            + [ANY] * len(extra),
            out_specs=pl.BlockSpec((H, rows, SEQ), lambda i, *_: (0, first + i, 0)),
        ),
        out_shape=jax.ShapeDtypeStruct((H, SEQ, SEQ), F32),
        input_output_aliases={5: 0} if extra else {},
        cost_estimate=pl.CostEstimate(
            flops=COST, bytes_accessed=COST, transcendentals=0
        ),
        name="bias",
    )(lengths, tab, *rel, *extra)


def head_masks():
    lane = lax.broadcasted_iota(jnp.int32, (1, 2 * HD), 1)
    return (lane < HD, lane >= HD)


def attend_kernel(q_ref, k_ref, v_ref, bias_ref, ctx_ref, p_ref, *, rows):
    zero = jnp.zeros((), BF)
    masks = head_masks()
    keys = [jnp.where(m, k_ref[...], zero) for m in masks]
    vals = [jnp.where(m, v_ref[...], zero) for m in masks]
    for r in range(0, SEQ, rows):
        q = q_ref[r : r + rows, :]
        ctx = None
        for h in range(2):
            scores = mm(q, keys[h], NT) * HD ** (-0.5) + bias_ref[h, r : r + rows, :]
            top = jnp.max(scores, axis=-1, keepdims=True)
            raised = jnp.exp(scores - top)
            total = jnp.sum(raised, axis=-1, keepdims=True)
            soft = (raised * (1.0 / total)).astype(BF)
            p_ref[h, r : r + rows, :] = soft
            part = mm(soft, vals[h], NN)
            ctx = part if ctx is None else ctx + part
        ctx_ref[r : r + rows, :] = ctx.astype(BF)


def lane_block(offset):
    return pl.BlockSpec((SEQ, 2 * HD), lambda i: (0, offset + i))


PAIR_BLOCK = pl.BlockSpec((2, SEQ, SEQ), lambda i: (i, 0, 0))


def attend(qkv, bias):
    n = D // (2 * HD)
    return pl.pallas_call(
        lambda *refs: attend_kernel(*refs, rows=256),
        grid=(n,),
        in_specs=[lane_block(0), lane_block(n), lane_block(2 * n), PAIR_BLOCK],
        out_specs=[lane_block(0), PAIR_BLOCK],
        out_shape=[
            jax.ShapeDtypeStruct((SEQ, D), BF),
            jax.ShapeDtypeStruct((H, SEQ, SEQ), BF),
        ],
        cost_estimate=pl.CostEstimate(
            flops=COST, bytes_accessed=COST, transcendentals=0
        ),
        name="attend",
    )(qkv, qkv, qkv, bias)


def attend_back_kernel(
    q_ref, k_ref, v_ref, p_ref, c_ref, dc_ref, dq_ref, dk_ref, dv_ref, ds_ref, sum_ref, *, rows
):
    zero = jnp.zeros((), BF)
    masks = head_masks()
    keys = [jnp.where(m, k_ref[...], zero) for m in masks]
    vals = [jnp.where(m, v_ref[...], zero) for m in masks]
    scale = HD ** (-0.5)
    q_sum = jnp.zeros((1, 2 * HD), F32)
    for r in range(0, SEQ, rows):
        dc = dc_ref[r : r + rows, :]
        prod = dc.astype(F32) * c_ref[r : r + rows, :].astype(F32)
        dq = None
        for h in range(2):
            soft = p_ref[h, r : r + rows, :]
            inner = jnp.sum(jnp.where(masks[h], prod, 0.0), axis=-1, keepdims=True)
            d_soft = mm(dc, vals[h], NT)
            d_scores = (soft.astype(F32) * (d_soft - inner)).astype(BF)
            ds_ref[h, r : r + rows, :] = d_scores
            part = mm(d_scores, keys[h], NN)
            dq = part if dq is None else dq + part
        dq = (dq * scale).astype(BF)
        dq_ref[r : r + rows, :] = dq
        q_sum = q_sum + jnp.sum(dq.astype(F32), axis=0, keepdims=True)
    flips = (dc_ref[...].astype(F32).T.astype(BF), q_ref[...].astype(F32).T.astype(BF))
    sums = [q_sum]
    for flip, factor, pair_ref, out_ref in (
        (flips[0], 1.0, p_ref, dv_ref),
        (flips[1], scale, ds_ref, dk_ref),
    ):
        parts = [mm(flip[HD * h : HD * h + HD, :], pair_ref[h], NN) for h in range(2)]
        done = (jnp.concatenate(parts, axis=0).T * factor).astype(BF)
        out_ref[...] = done
        sums.append(jnp.sum(done.astype(F32), axis=0, keepdims=True))
    sum_ref[...] = jnp.concatenate(sums[:2] + [jnp.zeros((6, 2 * HD), F32)], axis=0)


def attend_back(qkv, soft, ctx, d_ctx):
    n = D // (2 * HD)
    return pl.pallas_call(
        lambda *refs: attend_back_kernel(*refs, rows=256),
        grid=(n,),
        in_specs=[
            lane_block(0),
            lane_block(n),
            lane_block(2 * n),
            PAIR_BLOCK,
            lane_block(0),
            lane_block(0),
        ],
        out_specs=[
            lane_block(0),
            lane_block(0),
            lane_block(0),
            PAIR_BLOCK,
            pl.BlockSpec((8, 2 * HD), lambda i: (0, i)),
        ],
        out_shape=[jax.ShapeDtypeStruct((SEQ, D), BF)] * 3
        + [jax.ShapeDtypeStruct((H, SEQ, SEQ), BF), jax.ShapeDtypeStruct((8, D), F32)],
        cost_estimate=pl.CostEstimate(
            flops=COST, bytes_accessed=COST, transcendentals=0
        ),
        name="attend_back",
    )(qkv, qkv, qkv, soft, ctx, d_ctx)


def table_kernel(one_ref, x_ref, y_ref, ds_ref, out_ref):
    @pl.when(pl.program_id(0) == 0)
    def _():
        out_ref[...] = jnp.zeros_like(out_ref)

    rows = one_ref.shape[1]
    flipped = jnp.swapaxes(ds_ref[...].astype(F32), 0, 1).astype(BF)
    total = None
    for r in range(rows):
        hot = jnp.concatenate(
            [
                (lax.broadcasted_iota(jnp.int32, (size, SEQ), 0) == ref[0, r : r + 1, :])
                .astype(F32)
                .astype(BF)
                for ref, size in ((one_ref, B1), (x_ref, BX), (y_ref, BX))
            ],
            axis=0,
        )
        part = mm(flipped[r], hot, NT)
        total = part if total is None else total + part
    out_ref[...] += total


def table_grad(rel_1d, rel_x, rel_y, d_scores, part):
    rows = 16
    first, count = TABLE_ROWS[part][0] // rows, TABLE_ROWS[part][1] // rows
    ids = pl.BlockSpec((1, rows, SEQ), lambda i: (0, first + i, 0))
    return pl.pallas_call(
        table_kernel,
        grid=(count,),
        in_specs=[ids, ids, ids, pl.BlockSpec((H, rows, SEQ), lambda i: (0, first + i, 0))],
        out_specs=pl.BlockSpec((H, BUCKETS), lambda i: (0, 0)),
        out_shape=jax.ShapeDtypeStruct((H, BUCKETS), F32),
        cost_estimate=pl.CostEstimate(
            flops=COST, bytes_accessed=COST, transcendentals=0
        ),
        name="table_grad",
    )(rel_1d, rel_x, rel_y, d_scores)


def spread(size, plan):
    found = []
    for whole in plan:
        at, pieces = 0, []
        for z, x, y, first, last in whole:
            rows = (last - first) * size // 2
            pieces.append((at, rows, z, x, y, first * size // 2))
            at += rows
        found.append(pieces)
    return found


def blocks(zs, x, y):
    return [(z, x, y, 0, 2) for z in zs]


ATTN_PLAN = spread(
    A_ROWS,
    [
        blocks(range(4), 0, 0),
        blocks(range(4), 1, 0),
        blocks(range(4), 0, 1),
        blocks((0, 1), 1, 1),
        blocks((2, 3), 1, 1),
    ],
)
FFN_PLAN = spread(
    F_ROWS,
    [
        blocks((0,), 0, 0),
        blocks((0,), 1, 0),
        blocks((0,), 0, 1),
        blocks((1, 2, 3), 0, 0),
        blocks((1, 2, 3), 1, 0),
        blocks((1, 2, 3), 0, 1),
        blocks((0, 1), 1, 1),
        blocks((2, 3), 1, 1),
    ],
)
A_COPIES = 2 * sum(len(pieces) for pieces in ATTN_PLAN)
F_COPIES = 2 * sum(len(pieces) for pieces in FFN_PLAN)


def joined(plan):
    start, found = 0, []
    for pieces in plan:
        found += [(start + first, *rest) for first, *rest in pieces]
        start += sum(piece[1] for piece in pieces)
    return [found]


ATTN_FAR, FFN_FAR = joined(ATTN_PLAN[:3]) + ATTN_PLAN[3:], FFN_PLAN


def piece_list(plans, refs):
    found = []
    for core, plan in enumerate(plans):
        for pieces, ref in zip(plan, refs[len(plans[0]) * core :]):
            for start, rows, z, x, y, offset in pieces:
                found.append((core, z, x, y, offset, rows, ref.at[pl.ds(start, rows), :]))
    return found


def qkv_kernel(at_ref, tok_ref, add_ref, *refs):
    qkv_ref, all_ref, weight_ref, sems, done = refs[len(ATTN_PLAN) + len(ATTN_FAR) :]
    copies = []
    for n, (core, z, x, y, offset, rows, ref) in enumerate(piece_list((ATTN_PLAN, ATTN_FAR), refs)):
        block = (
            ((at_ref[0] ^ z) * 2 + (at_ref[1] ^ x)) * 2 + (at_ref[2] ^ y)
        ) * 2 + (at_ref[3] ^ core)
        spot = pl.ds(pl.multiple_of(block * A_ROWS + offset, 16), rows)
        copies.append(pltpu.make_async_copy(ref, weight_ref.at[spot, :], sems.at[n]))
    for copy in copies:
        copy.start()
    for copy in copies:
        copy.wait()
    store = pltpu.make_async_copy(weight_ref, all_ref, done)
    store.start()
    for t in range(3):
        part = slice(D * t, D * t + D)
        qkv_ref[:, part] = (mm(tok_ref[...], weight_ref[part, :], NN) + add_ref[:, part]).astype(BF)
    store.wait()


def project(at, tokens, add_three, pieces):
    count = tokens.shape[0]
    vmem = pl.BlockSpec(memory_space=pltpu.VMEM)
    return pl.pallas_call(
        qkv_kernel,
        in_specs=[pl.BlockSpec(memory_space=pltpu.SMEM), vmem, vmem] + [ANY] * len(pieces),
        out_specs=[vmem, ANY],
        out_shape=[
            jax.ShapeDtypeStruct((count, 3 * D), BF),
            jax.ShapeDtypeStruct((4 * D, D), BF),
        ],
        scratch_shapes=[
            pltpu.VMEM((4 * D, D), BF),
            pltpu.SemaphoreType.DMA((A_COPIES,)),
            pltpu.SemaphoreType.DMA,
        ],
        cost_estimate=pl.CostEstimate(
            flops=COST, bytes_accessed=COST, transcendentals=0
        ),
        name="project",
    )(at, tokens, add_three, *pieces)


def grad_ffn_kernel(at_ref, *refs, high):
    wide, slim, outs, (left, right, sems) = refs[:4], refs[4:8], refs[8:11], refs[11:]
    which = (at_ref[0] // 2) ^ high
    for w in range(2):

        @pl.when(which == w)
        def _():
            copies = []
            for i in range(2):
                rows = pl.ds(SEQ * i, SEQ)
                copies.append(
                    pltpu.make_async_copy(wide[2 * w + i], left.at[rows, :], sems.at[2 * i])
                )
                copies.append(
                    pltpu.make_async_copy(slim[2 * w + i], right.at[rows, :], sems.at[2 * i + 1])
                )
            for copy in copies:
                copy.start()
            for copy in copies:
                copy.wait()

    own, kept, sent = outs
    for z in range(2):
        done = mm(left[:, HALF // 2 * z : HALF // 2 * (z + 1)], right[...], TN).astype(BF)
        rows = [done[F_ROWS * q : F_ROWS * q + F_ROWS, :] for q in range(4)]
        own[z] = rows[0]
        kept[z] = rows[1 if high else 2]
        sent[z] = rows[3]
        sent[2 + z] = rows[2 if high else 1]


def grad_ffn(at, wide, slim, high):
    shape = lambda n: jax.ShapeDtypeStruct((n, F_ROWS, D), BF)
    return pl.pallas_call(
        lambda *refs: grad_ffn_kernel(*refs, high=high),
        in_specs=[pl.BlockSpec(memory_space=pltpu.SMEM)] + [ANY] * 8,
        out_specs=[pl.BlockSpec(memory_space=pltpu.VMEM)] * 3,
        out_shape=[shape(2), shape(2), shape(4)],
        scratch_shapes=[
            pltpu.VMEM((2 * SEQ, HALF), BF),
            pltpu.VMEM((2 * SEQ, D), BF),
            pltpu.SemaphoreType.DMA((4,)),
        ],
        cost_estimate=pl.CostEstimate(
            flops=COST, bytes_accessed=COST, transcendentals=0
        ),
        name="grad_ffn",
    )(at, *wide, *slim)


def grad_attn_kernel(at_ref, tok_ref, tok_far, ctx_ref, ctx_far, *refs):
    grads, outs, (flip, left, right, sems) = refs[:8], refs[8:14], refs[14:]
    copies = []
    for t in range(4):
        for i in range(2):
            spot = right.at[t, pl.ds(SEQ * i, SEQ), :]
            copies.append(pltpu.make_async_copy(grads[2 * t + i], spot, sems.at[2 * t + i]))
    for copy in copies:
        copy.start()
    for n, (near, far) in enumerate(((tok_ref, tok_far), (ctx_ref, ctx_far))):
        flip[:, :SEQ] = near[...].astype(F32).T.astype(BF)
        flip[:, SEQ:] = far[...].astype(F32).T.astype(BF)
        for q in range(4):
            block = (((at_ref[1] ^ (q // 2)) * 2 + (at_ref[2] ^ (q % 2))) * 2) + at_ref[3]
            spot = pl.ds(pl.multiple_of(block * A_ROWS, A_ROWS), A_ROWS)
            left[n, A_ROWS * q : A_ROWS * q + A_ROWS, :] = flip[spot, :]
    for copy in copies:
        copy.wait()
    for z in range(4):
        which = at_ref[0] ^ z
        done = mm(left[which // 3], right[which], NN).astype(BF)
        rows = [done[A_ROWS * q : A_ROWS * q + A_ROWS, :] for q in range(4)]
        own, kept, sent = outs[3 * (z // 2) : 3 * (z // 2) + 3]
        own[z % 2] = rows[0]
        kept[z % 2] = rows[1 if z // 2 else 2]
        sent[z % 2] = rows[3]
        sent[2 + z % 2] = rows[2 if z // 2 else 1]


def grad_attn(at, tokens, tokens_far, ctx, ctx_far, grads):
    shape = lambda n: jax.ShapeDtypeStruct((n, A_ROWS, D), BF)
    vmem = pl.BlockSpec(memory_space=pltpu.VMEM)
    return pl.pallas_call(
        grad_attn_kernel,
        in_specs=[pl.BlockSpec(memory_space=pltpu.SMEM)] + [vmem] * 4 + [ANY] * 8,
        out_specs=[vmem] * 6,
        out_shape=[shape(2), shape(2), shape(4)] * 2,
        scratch_shapes=[
            pltpu.VMEM((D, 2 * SEQ), BF),
            pltpu.VMEM((2, D // 2, 2 * SEQ), BF),
            pltpu.VMEM((4, 2 * SEQ, D), BF),
            pltpu.SemaphoreType.DMA((8,)),
        ],
        cost_estimate=pl.CostEstimate(
            flops=COST, bytes_accessed=COST, transcendentals=0
        ),
        name="grad_attn",
    )(at, tokens, tokens_far, ctx, ctx_far, *grads)


def row_mean(values):
    return jnp.mean(values, axis=-1, keepdims=True)


def normal_rows(values):
    center = values - row_mean(values)
    inv = lax.rsqrt(row_mean(center * center) + NORM_EPS)
    return center * inv, inv


def normal_back(normal, inv, grad):
    return inv * (grad - row_mean(grad) - normal * row_mean(grad * normal))


def gelu_parts(u):
    z = jnp.abs(u) * (2.0**-0.5)
    t = 1.0 / (1.0 + 0.3275911 * z)
    tail = jnp.exp(-0.5 * u * u)
    poly = t * (
        0.254829592
        + t * (-0.284496736 + t * (1.421413741 + t * (-1.453152027 + t * 1.061405429)))
    )
    half = 0.5 * poly * tail
    cdf = jnp.where(u < 0, half, 1.0 - half)
    return u * cdf, cdf + u * (tail * (1.0 / math.sqrt(2.0 * math.pi)))


def row_sum(values):
    return jnp.sum(values.astype(F32), axis=0, keepdims=True)


def block_kernel(
    at_ref,
    ctx_ref,
    tok_ref,
    cot_ref,
    vec_ref,
    b1_ref,
    wo_ref,
    *refs,
    wide,
):
    split = len(FFN_PLAN) + len(FFN_FAR)
    pieces, refs = refs[:split], refs[split:]
    out_ref, hid_ref, act_near, act_far, dff_ref, du_near, du_far = refs[:7]
    dr_ref, dab_ref, dctx_ref, sum_ref, db1_ref, slope_ref, ffn_ref, sems = refs[7:]
    copies = []
    for n, (core, z, x, y, offset, rows, ref) in enumerate(piece_list((FFN_PLAN, FFN_FAR), pieces)):
        spot = pl.ds(core * HALF + ((z % 2) * 4 + x * 2 + y) * F_ROWS + offset, rows)
        which = (at_ref[0] // 2) ^ (z // 2)
        copies.append(pltpu.make_async_copy(ref, ffn_ref.at[which, spot, :], sems.at[n]))
    w1_ref, w2_ref = ffn_ref.at[0], ffn_ref.at[1]

    @pl.when(pl.program_id(0) == 0)
    def _():
        for copy in copies:
            copy.start()
        sum_ref[...] = jnp.zeros_like(sum_ref)
        db1_ref[...] = jnp.zeros_like(db1_ref)

    vec = [vec_ref[i : i + 1, :] for i in range(8)]
    resid = tok_ref[...].astype(F32) + (mm(ctx_ref[...], wo_ref[...], NN) + vec[6])
    n_one, inv_one = normal_rows(resid)
    hidden = n_one * vec[0] + vec[1]
    hid_low = hidden.astype(BF)
    hid_ref[...] = hid_low
    total = hidden + vec[7]

    @pl.when(pl.program_id(0) == 0)
    def _():
        for copy in copies:
            copy.wait()

    for f in range(0, FF, wide):
        part = slice(f, f + wide)
        u = mm(hid_low, w1_ref[part, :], NT) + b1_ref[:, part]
        act, slope = gelu_parts(u)
        act = act.astype(BF)
        side = slice(f % HALF, f % HALF + wide)
        (act_near if f < HALF else act_far)[:, side] = act
        slope_ref[:, part] = slope
        total = total + mm(act, w2_ref[part, :], NN)
    n_two, inv_two = normal_rows(total)
    out_ref[...] = (n_two * vec[2] + vec[3]).astype(BF)
    dy = cot_ref[...].astype(F32)
    d_two = normal_back(n_two, inv_two, dy * vec[2])
    dff = d_two.astype(BF)
    dff_ref[...] = dff
    d_hid = d_two
    for f in range(0, FF, wide):
        part = slice(f, f + wide)
        du = (mm(dff, w2_ref[part, :], NT) * slope_ref[:, part]).astype(BF)
        side = slice(f % HALF, f % HALF + wide)
        (du_near if f < HALF else du_far)[:, side] = du
        db1_ref[:, part] += row_sum(du)
        d_hid = d_hid + mm(du, w1_ref[part, :], NN)
    d_one = normal_back(n_one, inv_one, d_hid * vec[0])
    dr_ref[...] = d_one
    dab = d_one.astype(BF)
    dab_ref[...] = dab
    dctx_ref[...] = mm(dab, wo_ref[...], NT).astype(BF)
    sum_ref[...] += jnp.concatenate(
        [
            row_sum(d_hid * n_one),
            row_sum(d_hid),
            row_sum(dy * n_two),
            row_sum(dy),
            jnp.zeros((2, D), F32),
            row_sum(dab),
            row_sum(dff),
        ],
        axis=0,
    )


def block_pass(at, ctx, tokens, cotangent, vectors, b_first, attn_full, pieces):
    rows = 256
    by_row = lambda width: pl.BlockSpec((rows, width), lambda i, *_: (i, 0))
    whole = lambda shape, first=0: pl.BlockSpec(
        shape, lambda i, *_: (first, 0), pipeline_mode=pl.Buffered(1)
    )
    count = tokens.shape[0]
    low = lambda width: jax.ShapeDtypeStruct((count, width), BF)
    return pl.pallas_call(
        lambda *refs: block_kernel(*refs, wide=768),
        grid_spec=pltpu.PrefetchScalarGridSpec(
            num_scalar_prefetch=1,
            grid=(count // rows,),
            in_specs=[
                by_row(D),
                by_row(D),
                by_row(D),
                whole((12, D)),
                whole((1, FF)),
                whole((D, D), 3),
            ]
            + [ANY] * len(pieces),
            out_specs=[
                by_row(D),
                by_row(D),
                by_row(HALF),
                by_row(HALF),
                by_row(D),
                by_row(HALF),
                by_row(HALF),
                by_row(D),
                by_row(D),
                by_row(D),
                pl.BlockSpec((8, D), lambda i, *_: (0, 0)),
                pl.BlockSpec((1, FF), lambda i, *_: (0, 0)),
            ],
            scratch_shapes=[
                pltpu.VMEM((rows, FF), F32),
                pltpu.VMEM((2, FF, D), BF),
                pltpu.SemaphoreType.DMA((F_COPIES,)),
            ],
        ),
        out_shape=[
            low(D),
            low(D),
            low(HALF),
            low(HALF),
            low(D),
            low(HALF),
            low(HALF),
            jax.ShapeDtypeStruct((count, D), F32),
            low(D),
            low(D),
            jax.ShapeDtypeStruct((8, D), F32),
            jax.ShapeDtypeStruct((1, FF), F32),
        ],
        cost_estimate=pl.CostEstimate(
            flops=COST, bytes_accessed=COST, transcendentals=0
        ),
        name="block_pass",
    )(at, ctx, tokens, cotangent, vectors, b_first, attn_full, *pieces)


def swap(array, mask):
    return lax.ppermute(array, ALL, [(i, i ^ mask) for i in range(BLOCKS)])


def together(*groups):
    return lax.optimization_barrier(groups)


def tie(arrays, after):
    return lax.optimization_barrier((arrays, after))[0]


def column(shard, zs):
    return jnp.concatenate([shard if z == 0 else swap(shard, 8 * z) for z in zs])


def gather_full(shard, plans):
    full = lax.all_gather(shard, ALL, axis=0, tiled=True)
    view = full.reshape(*SPLIT, full.shape[0] // BLOCKS, D)
    return tuple(
        jnp.concatenate([view[z, x, y, core, off : off + n] for _, n, z, x, y, off in pieces])
        for core, plan in enumerate(plans)
        for pieces in plan
    )


def wide(array):
    return array.astype(F32)


def scatter_first(low, high):
    return swap(low[2], 2), swap(high[2], 4)


def scatter_sums(low, high, from_y, from_x):
    to_x = (wide(low[1]) + wide(from_y[:2])).astype(BF)
    to_y = (wide(high[1]) + wide(from_x[:2])).astype(BF)
    return to_x, to_y


def scatter_second(to_x, to_y):
    return swap(to_x, 4), swap(to_y, 2)


def scatter_third(low, high, from_y, from_x, last_x, last_y):
    low = wide(low[0]) + wide(from_y[2:]) + wide(last_x)
    high = wide(high[0]) + wide(from_x[2:]) + wide(last_y)
    send = (low[1].astype(BF), high[0].astype(BF), high[1].astype(BF))
    return low[0], tuple(swap(a, 8 * z) for z, a in zip((1, 2, 3), send))


def scatter_full(sides):
    cores = []
    for low, high in sides:
        rows = [(low[0], high[0]), (low[2][2:], high[1]), (low[1], high[2][2:])]
        rows.append((low[2][:2], high[2][:2]))
        cores.append(jnp.stack([jnp.concatenate(pair) for pair in rows], axis=1))
    full = jnp.stack(cores, axis=2).reshape(-1, D)
    return lax.psum_scatter(full, ALL, scatter_dimension=0, tiled=True).astype(F32)


def flip_bits(array, at):
    for axis, bit in enumerate((at[0] % 2, at[1], at[2], at[3])):
        array = jnp.where(bit == 1, jnp.flip(array, axis), array)
    return array


LANES = 256


def pack_table(grad):
    return jnp.pad(grad, ((0, 0), (0, LANES - BUCKETS))).reshape(H * LANES // D, D)


def update_kernel(total_ref, attn_sum, ffn_sum, *refs):
    states, outs = [refs[4 * i : 4 * i + 4] for i in range(4)], refs[16:]
    per = D // LANES
    vec_total = total_ref[:H, :]
    heads = jnp.concatenate(
        [
            total_ref[H + h // per : H + h // per + 1, LANES * (h % per) : LANES * (h % per + 1)]
            for h in range(H)
        ],
        axis=0,
    )
    square = total_ref[H : H + 1, LANES - 1 : LANES]
    lane = lax.broadcasted_iota(jnp.int32, heads.shape, 1)
    tab_total = jnp.where(lane < BUCKETS, heads, 0.0)
    rows = jnp.sum(tab_total * tab_total, axis=0, keepdims=True)
    square = square + jnp.sum(rows, axis=1, keepdims=True)
    rows = jnp.sum(vec_total * vec_total, axis=0, keepdims=True)
    norm = jnp.sqrt(square + jnp.sum(rows, axis=1, keepdims=True))
    scale = 1.0 / jnp.maximum(norm, 1.0)
    outs[0][...] = norm
    outs[1][...] = vec_total * scale
    totals = (attn_sum[...], ffn_sum[...], vec_total, heads[:H, :BUCKETS])
    for i, (state, total) in enumerate(zip(states, totals)):
        rate, decay = (0.06, 0.01) if i < 2 else (0.6, 0.0)
        weight, first, second, average = (ref[...] for ref in state)
        new = adam_update(weight, first, second, total, scale, rate, decay, average)
        for out, value in zip(outs[2 + 4 * i :], new):
            out[...] = value


def update(total, attn_sum, ffn_sum, states):
    like = lambda a: jax.ShapeDtypeStruct(a.shape, F32)
    one = jax.ShapeDtypeStruct((1, 1), F32)
    steps = 1
    whole = lambda shape: pl.BlockSpec(shape, lambda i: (0, 0))
    part = lambda a: pl.BlockSpec((a.shape[0] // steps, D), lambda i: (i, 0))
    states_specs = [part(a) for a in states[:8]] + [whole(a.shape) for a in states[8:]]
    return pl.pallas_call(
        update_kernel,
        grid=(steps,),
        in_specs=[whole(total.shape), part(attn_sum), part(ffn_sum)] + states_specs,
        out_specs=[whole((1, 1)), whole(states[8].shape)] + states_specs,
        out_shape=[one, like(states[8])] + [like(a) for a in states],
        name="update",
    )(total, attn_sum, ffn_sum, *states)


def hidden_bias(vectors, at):
    flipped = flip_bits(vectors[8:].reshape(2, 2, 2, 2, F_ROWS), at)
    return flipped.transpose(3, 0, 1, 2, 4).reshape(1, FF)


def input_grad(start, d_three, attn_full, which=(0, 1, 2)):
    for t in which:
        start = start + mm(d_three[t], attn_full[D * t : D * t + D], NT)
    return start


def shards(
    tokens,
    cotangent,
    lengths,
    rel_1d,
    rel_x,
    rel_y,
    attn_weights,
    attn_m1,
    attn_m2,
    attn_ema,
    ffn_weights,
    ffn_m1,
    ffn_m2,
    ffn_ema,
    vectors,
    vec_m1,
    vec_m2,
    vec_ema,
    table,
    tab_m1,
    tab_m2,
    tab_ema,
    *,
    direct,
):
    attn_low, ffn_low = attn_weights.astype(BF), ffn_weights.astype(BF)
    rel = (rel_1d, rel_x, rel_y)
    tab = bias_lines(table)
    add_three = jnp.concatenate([vectors[4], jnp.zeros((D,), F32), vectors[5]]).reshape(1, 3 * D)
    if direct:
        dp, fsdp = lax.axis_index("dp"), lax.axis_index("fsdp")
        at = jnp.stack([dp // 2, dp % 2, fsdp // 2, fsdp % 2]).astype(jnp.int32)
        far = lambda a: swap(a, 1)
        b_first = hidden_bias(vectors, at)
        attn_column = column(attn_low, range(4))
        ffn_x, ffn_y = swap(ffn_low, 4), swap(ffn_low, 2)
        bias = page_bias(lengths, tab, rel, 0, None)
        attn_column, ffn_x, ffn_y, later, bias, at, b_first, add_three = together(
            attn_column, ffn_x, ffn_y, ffn_low, bias, at, b_first, add_three
        )
        beside, above = swap(attn_column, 4), swap(attn_column, 2)
        ffn_column = column(later, (1, 2, 3))
        bias = page_bias(lengths, tab, rel, 1, bias)
        beside, above, bias = together(beside, above, bias)
        near, ffn_column, bias = together((attn_column, beside, above), ffn_column, bias)
        side = 2 * A_ROWS
        low, high = swap(near[1][:side], 2), swap(near[2][side:], 4)
        beside, above = swap(ffn_column, 4), swap(ffn_column, 2)
        away = swap(jnp.concatenate(near), 1)
        bias = page_bias(lengths, tab, rel, 2, bias)
        last, away, bias, start = together((low, high), away, bias, (ffn_low, ffn_x, ffn_y))
        attn_pieces = near + last + (away,) + tuple(swap(piece, 1) for piece in last)
        first = tuple(swap(piece, 1) for piece in start)
        qkv, attn_full = project(at, tokens, add_three, attn_pieces)
        first, beside, above, qkv = together(first, beside, above, qkv)
        low = swap(jnp.concatenate([start[1], beside[:F_ROWS]]), 2)
        high = swap(above[F_ROWS:], 4)
        middle = (ffn_column, beside, above)
        away = tuple(swap(piece, 1) for piece in middle)
        ctx, soft = attend(qkv, bias)
        last, away, ctx = together((low, high), away, ctx)
        ffn_pieces = start + middle + last + first + away + tuple(swap(a, 1) for a in last)
    else:
        at = jnp.zeros((4,), jnp.int32)
        b_first = hidden_bias(vectors, at)
        far = jnp.zeros_like
        bias = None
        for part in range(len(BIAS_ROWS)):
            bias = page_bias(lengths, tab, rel, part, bias)
        attn_pieces = gather_full(attn_low, (ATTN_PLAN, ATTN_FAR))
        ffn_pieces = gather_full(ffn_low, (FFN_PLAN, FFN_FAR))
        qkv, attn_full = project(at, tokens, add_three, attn_pieces)
        ctx, soft = attend(qkv, bias)
        tokens_far, ctx_far = far(tokens), far(ctx)
    (
        block_out,
        hid,
        act_near,
        act_away,
        d_ffn,
        du_near,
        du_away,
        d_resid_one,
        d_attn,
        d_context,
        sums,
        grad_bias_first,
    ) = block_pass(at, ctx, tokens, cotangent, vectors, b_first, attn_full, ffn_pieces)
    away = (far(du_away), far(act_away), far(hid), far(d_ffn), far(d_attn))
    dq, dk, dv, d_scores, qv_sums = attend_back(qkv, soft, ctx, d_context)
    d_three = (dq, dk, dv)
    if direct:
        away, d_three, d_scores, rows = together(away, d_three, d_scores, (tokens, ctx))
        du_far, act_far, hid_far, d_ffn_far, d_attn_far = away
        wide_ones, slim = (du_near, du_far, act_near, act_far), (hid, hid_far, d_ffn, d_ffn_far)
        low = grad_ffn(at, wide_ones, slim, 0)
        three_far = tuple(far(d) for d in d_three + rows)
        low, three_far, wide_ones = together(low, three_far, wide_ones)
        high = grad_ffn(at, wide_ones, slim, 1)
        grads = [g for pair in zip(d_three, three_far[:3]) for g in pair] + [d_attn, d_attn_far]
        high, grads = together(high, grads)
        ffn_first = scatter_first(low, high)
        parts = grad_attn(at, tokens, three_far[3], ctx, three_far[4], grads)
        parts, d_scores = together(parts, d_scores)
        attn_first = scatter_first(parts[:3], parts[3:])
        tables = [table_grad(*rel, d_scores, 0)]
        ffn_first, d_scores, tables[0] = together(ffn_first, d_scores, tables[0])
        ffn_second = scatter_second(*scatter_sums(low, high, *ffn_first))
        tables.append(table_grad(*rel, d_scores, 1))
        attn_first, ffn_second, d_three, tables[1] = together(
            attn_first, ffn_second, d_three, tables[1]
        )
        ffn_own, ffn_three = scatter_third(low, high, *ffn_first, *ffn_second)
        sent, d_three = together(scatter_sums(parts[:3], parts[3:], *attn_first), d_three)
        attn_second = scatter_second(*sent)
        grad_input = input_grad(d_resid_one, d_three, attn_full, (0, 1))
        late = (sums, qv_sums, grad_bias_first, tables, d_three[2], d_scores)
        attn_second, grad_input, late = together(attn_second, grad_input, late)
        sums, qv_sums, grad_bias_first, tables, last_grad, d_scores = late
        tables.append(table_grad(*rel, d_scores, 2))
        grad_input = input_grad(grad_input, (last_grad,), attn_full[2 * D :], (0,))
        attn_own, attn_three = scatter_third(parts[:3], parts[3:], *attn_first, *attn_second)
        ffn_shard = sum((wide(a) for a in ffn_three), ffn_own)
        attn_shard = sum((wide(a) for a in attn_three), attn_own)
    else:
        sides, attn_sides = [], []
        grads = [g for d in (*d_three, d_attn) for g in (d, far(d))]
        slim = (hid, far(hid), d_ffn, far(d_ffn))
        for core, (du, act) in enumerate(((du_near, act_near), (du_away, act_away))):
            wide_ones = (du, far(du), act, far(act))
            sides.append([grad_ffn(at, wide_ones, slim, side) for side in range(2)])
            spot = at.at[3].set(core)
            parts = grad_attn(spot, tokens, tokens_far, ctx, ctx_far, grads)
            attn_sides.append((parts[:3], parts[3:]))
        ffn_shard, attn_shard = scatter_full(sides), scatter_full(attn_sides)
        tables = [table_grad(*rel, d_scores, part) for part in range(len(TABLE_ROWS))]
        grad_input = input_grad(d_resid_one, d_three, attn_full)
    grad_table = pack_table(sum(tables[1:], tables[0]))
    grad_bias_first = grad_bias_first.reshape(2, 2, 2, 2, F_ROWS).transpose(1, 2, 3, 0, 4)
    grad_bias_first = flip_bits(grad_bias_first, at).reshape(FF // D, D)
    small = jnp.concatenate([sums[:4], qv_sums[:2], sums[6:], grad_bias_first, grad_table], axis=0)
    squares = jnp.sum(attn_shard * attn_shard) + jnp.sum(ffn_shard * ffn_shard)
    row = lax.broadcasted_iota(jnp.int32, small.shape, 0)
    lane = lax.broadcasted_iota(jnp.int32, small.shape, 1)
    small = jnp.where((row == H) & (lane == LANES - 1), squares, small)
    if direct:
        for mask in (1, 2, 4, 8, 16):
            small = small + swap(small, mask)
    else:
        small = lax.psum(small, ALL)
    states = (attn_weights, attn_m1, attn_m2, attn_ema, ffn_weights, ffn_m1, ffn_m2, ffn_ema)
    states += (vectors, vec_m1, vec_m2, vec_ema, table.T, tab_m1.T, tab_m2.T, tab_ema.T)
    grad_norm, vec_grad, *new = update(small, attn_shard, ffn_shard, states)
    new = new[:12] + [array.T for array in new[12:]]
    return (block_out, grad_input, grad_norm.reshape(()), *new, vec_grad)


def solution(mesh):
    direct = mesh.shape["dp"] == SPLIT[0] * SPLIT[1] and mesh.shape["fsdp"] == SPLIT[2] * SPLIT[3]
    return jax.shard_map(
        lambda *arrays: shards(*arrays, direct=direct),
        mesh=mesh,
        in_specs=(
            P(("dp", "fsdp"), None),
            P(("dp", "fsdp"), None),
            P(("dp", "fsdp")),
            P(("dp", "fsdp"), None, None),
            P(("dp", "fsdp"), None, None),
            P(("dp", "fsdp"), None, None),
            P(("dp", "fsdp"), None),
            P(("dp", "fsdp"), None),
            P(("dp", "fsdp"), None),
            P(("dp", "fsdp"), None),
            P(("dp", "fsdp"), None),
            P(("dp", "fsdp"), None),
            P(("dp", "fsdp"), None),
            P(("dp", "fsdp"), None),
            P(),
            P(),
            P(),
            P(),
            P(),
            P(),
            P(),
            P(),
        ),
        out_specs=(
            P(("dp", "fsdp"), None),
            P(("dp", "fsdp"), None),
            P(),
            P(("dp", "fsdp"), None),
            P(("dp", "fsdp"), None),
            P(("dp", "fsdp"), None),
            P(("dp", "fsdp"), None),
            P(("dp", "fsdp"), None),
            P(("dp", "fsdp"), None),
            P(("dp", "fsdp"), None),
            P(("dp", "fsdp"), None),
            P(),
            P(),
            P(),
            P(),
            P(),
            P(),
            P(),
            P(),
            P(),
        ),
        check_vma=False,
    )
```

```python
import math

import jax
import jax.numpy as jnp
from jax import lax
from jax.experimental import pallas as pl
from jax.experimental.pallas import tpu as pltpu
from jax.sharding import PartitionSpec as P

D = 768
H = 12
HD = 64
FF = 3072
B1 = 32
BX = 64
SEQ = 512
STEP = 10
BUCKETS = B1 + 2 * BX


NEG_FILL = -1e30
NORM_EPS = 1e-05
BF = jnp.bfloat16
F32 = jnp.float32
NT = (((1,), (1,)), ((), ()))
TN = (((0,), (0,)), ((), ()))
NN = (((1,), (0,)), ((), ()))
ALL = ("dp", "fsdp")
COST = 1_000_000
SPLIT = (4, 2, 2, 2)
BLOCKS = 32
A_ROWS = 4 * D // BLOCKS
F_ROWS = 2 * FF // BLOCKS
HALF = FF // 2
ANY = pl.BlockSpec(memory_space=pl.ANY)


def mm(a, b, dims):
    return lax.dot_general(a, b, dims, preferred_element_type=F32)


def adam_update(weight, moment_one, second, gradient, clip_scale, step_rate, decay_rate, average):
    clipped = gradient * clip_scale
    new_first = 0.9 * moment_one + 0.1 * clipped
    new_second = 0.999 * second + 0.001 * clipped * clipped
    first_hat = new_first / (1.0 - 0.9**STEP)
    second_hat = new_second / (1.0 - 0.999**STEP)
    new_weight = weight - step_rate * (
        first_hat / (jnp.sqrt(second_hat) + 1e-08) + decay_rate * weight
    )
    new_average = 0.8 * average + 0.2 * new_weight
    return (new_weight, new_first, new_second, new_average)


def bias_kernel(len_ref, tab_ref, one_ref, x_ref, y_ref, out_ref):
    length = len_ref[0]
    rows = one_ref.shape[1]

    def eight(i, _):
        r = pl.ds(pl.multiple_of(i * 8, 8), 8)
        for c in range(0, SEQ, 128):
            ids = [ref[0, r, c : c + 128] for ref in (one_ref, x_ref, y_ref)]
            keep = lax.broadcasted_iota(jnp.int32, (8, 128), 1) + c < length
            for h in range(H):
                total = None
                for t in range(3):
                    line = jnp.broadcast_to(tab_ref[h, t : t + 1, :], (8, 128))
                    got = jnp.take_along_axis(line, ids[t], axis=1, mode="promise_in_bounds")
                    total = got if total is None else total + got
                out_ref[h, r, c : c + 128] = jnp.where(keep, total, NEG_FILL)
        return 0

    lax.fori_loop(0, rows // 8, eight, 0)


PARTS = 2
BIAS_ROWS = ((0, 128), (128, 320), (448, 64))


def bias_lines(table):
    lines = table.T
    return jnp.stack(
        [
            jnp.pad(lines[:, :B1], ((0, 0), (0, 128 - B1))),
            jnp.pad(lines[:, B1 : B1 + BX], ((0, 0), (0, 128 - BX))),
            jnp.pad(lines[:, B1 + BX :], ((0, 0), (0, 128 - BX))),
        ],
        axis=1,
    )


def page_bias(lengths, tab, rel, part, out):
    rows = 64
    first, count = BIAS_ROWS[part][0] // rows, BIAS_ROWS[part][1] // rows
    ids = pl.BlockSpec((1, rows, SEQ), lambda i, *_: (0, first + i, 0))
    extra = [] if out is None else [out]
    return pl.pallas_call(
        lambda *refs: bias_kernel(*refs[:5], refs[-1]),
        grid_spec=pltpu.PrefetchScalarGridSpec(
            num_scalar_prefetch=1,
            grid=(count,),
            in_specs=[pl.BlockSpec((H, 3, 128), lambda i, *_: (0, 0, 0)), ids, ids, ids]
            + [ANY] * len(extra),
            out_specs=pl.BlockSpec((H, rows, SEQ), lambda i, *_: (0, first + i, 0)),
        ),
        out_shape=jax.ShapeDtypeStruct((H, SEQ, SEQ), F32),
        input_output_aliases={5: 0} if extra else {},
        cost_estimate=pl.CostEstimate(
            flops=COST, bytes_accessed=COST, transcendentals=0
        ),
        name="bias",
    )(lengths, tab, *rel, *extra)


def head_masks():
    lane = lax.broadcasted_iota(jnp.int32, (1, 2 * HD), 1)
    return (lane < HD, lane >= HD)


def attend_kernel(q_ref, k_ref, v_ref, bias_ref, ctx_ref, p_ref, *, rows):
    zero = jnp.zeros((), BF)
    masks = head_masks()
    keys = [jnp.where(m, k_ref[...], zero) for m in masks]
    vals = [jnp.where(m, v_ref[...], zero) for m in masks]
    for r in range(0, SEQ, rows):
        q = q_ref[r : r + rows, :]
        ctx = None
        for h in range(2):
            scores = mm(q, keys[h], NT) * HD ** (-0.5) + bias_ref[h, r : r + rows, :]
            top = jnp.max(scores, axis=-1, keepdims=True)
            raised = jnp.exp(scores - top)
            total = jnp.sum(raised, axis=-1, keepdims=True)
            soft = (raised * (1.0 / total)).astype(BF)
            p_ref[h, r : r + rows, :] = soft
            part = mm(soft, vals[h], NN)
            ctx = part if ctx is None else ctx + part
        ctx_ref[r : r + rows, :] = ctx.astype(BF)


def lane_block(offset):
    return pl.BlockSpec((SEQ, 2 * HD), lambda i: (0, offset + i))


PAIR_BLOCK = pl.BlockSpec((2, SEQ, SEQ), lambda i: (i, 0, 0))


def attend(qkv, bias):
    n = D // (2 * HD)
    return pl.pallas_call(
        lambda *refs: attend_kernel(*refs, rows=256),
        grid=(n,),
        in_specs=[lane_block(0), lane_block(n), lane_block(2 * n), PAIR_BLOCK],
        out_specs=[lane_block(0), PAIR_BLOCK],
        out_shape=[
            jax.ShapeDtypeStruct((SEQ, D), BF),
            jax.ShapeDtypeStruct((H, SEQ, SEQ), BF),
        ],
        cost_estimate=pl.CostEstimate(
            flops=COST, bytes_accessed=COST, transcendentals=0
        ),
        name="attend",
    )(qkv, qkv, qkv, bias)


def attend_back_kernel(
    q_ref, k_ref, v_ref, p_ref, c_ref, dc_ref, dq_ref, dk_ref, dv_ref, ds_ref, sum_ref, *, rows
):
    zero = jnp.zeros((), BF)
    masks = head_masks()
    keys = [jnp.where(m, k_ref[...], zero) for m in masks]
    vals = [jnp.where(m, v_ref[...], zero) for m in masks]
    scale = HD ** (-0.5)
    q_sum = jnp.zeros((1, 2 * HD), F32)
    for r in range(0, SEQ, rows):
        dc = dc_ref[r : r + rows, :]
        prod = dc.astype(F32) * c_ref[r : r + rows, :].astype(F32)
        dq = None
        for h in range(2):
            soft = p_ref[h, r : r + rows, :]
            inner = jnp.sum(jnp.where(masks[h], prod, 0.0), axis=-1, keepdims=True)
            d_soft = mm(dc, vals[h], NT)
            d_scores = (soft.astype(F32) * (d_soft - inner)).astype(BF)
            ds_ref[h, r : r + rows, :] = d_scores
            part = mm(d_scores, keys[h], NN)
            dq = part if dq is None else dq + part
        dq = (dq * scale).astype(BF)
        dq_ref[r : r + rows, :] = dq
        q_sum = q_sum + jnp.sum(dq.astype(F32), axis=0, keepdims=True)
    flips = (dc_ref[...].astype(F32).T.astype(BF), q_ref[...].astype(F32).T.astype(BF))
    sums = [q_sum]
    for flip, factor, pair_ref, out_ref in (
        (flips[0], 1.0, p_ref, dv_ref),
        (flips[1], scale, ds_ref, dk_ref),
    ):
        parts = [mm(flip[HD * h : HD * h + HD, :], pair_ref[h], NN) for h in range(2)]
        done = (jnp.concatenate(parts, axis=0).T * factor).astype(BF)
        out_ref[...] = done
        sums.append(jnp.sum(done.astype(F32), axis=0, keepdims=True))
    sum_ref[...] = jnp.concatenate(sums[:2] + [jnp.zeros((6, 2 * HD), F32)], axis=0)


def attend_back(qkv, soft, ctx, d_ctx):
    n = D // (2 * HD)
    return pl.pallas_call(
        lambda *refs: attend_back_kernel(*refs, rows=256),
        grid=(n,),
        in_specs=[
            lane_block(0),
            lane_block(n),
            lane_block(2 * n),
            PAIR_BLOCK,
            lane_block(0),
            lane_block(0),
        ],
        out_specs=[
            lane_block(0),
            lane_block(0),
            lane_block(0),
            PAIR_BLOCK,
            pl.BlockSpec((8, 2 * HD), lambda i: (0, i)),
        ],
        out_shape=[jax.ShapeDtypeStruct((SEQ, D), BF)] * 3
        + [jax.ShapeDtypeStruct((H, SEQ, SEQ), BF), jax.ShapeDtypeStruct((8, D), F32)],
        cost_estimate=pl.CostEstimate(
            flops=COST, bytes_accessed=COST, transcendentals=0
        ),
        name="attend_back",
    )(qkv, qkv, qkv, soft, ctx, d_ctx)


def table_kernel(one_ref, x_ref, y_ref, ds_ref, out_ref):
    @pl.when(pl.program_id(0) == 0)
    def _():
        out_ref[...] = jnp.zeros_like(out_ref)

    rows = one_ref.shape[1]
    flipped = jnp.swapaxes(ds_ref[...].astype(F32), 0, 1).astype(BF)
    total = None
    for r in range(rows):
        hot = jnp.concatenate(
            [
                (lax.broadcasted_iota(jnp.int32, (size, SEQ), 0) == ref[0, r : r + 1, :])
                .astype(F32)
                .astype(BF)
                for ref, size in ((one_ref, B1), (x_ref, BX), (y_ref, BX))
            ],
            axis=0,
        )
        part = mm(flipped[r], hot, NT)
        total = part if total is None else total + part
    out_ref[...] += total


def table_grad(rel_1d, rel_x, rel_y, d_scores, part):
    rows = 16
    count = SEQ // rows // PARTS
    first = part * count
    ids = pl.BlockSpec((1, rows, SEQ), lambda i: (0, first + i, 0))
    return pl.pallas_call(
        table_kernel,
        grid=(count,),
        in_specs=[ids, ids, ids, pl.BlockSpec((H, rows, SEQ), lambda i: (0, first + i, 0))],
        out_specs=pl.BlockSpec((H, BUCKETS), lambda i: (0, 0)),
        out_shape=jax.ShapeDtypeStruct((H, BUCKETS), F32),
        cost_estimate=pl.CostEstimate(
            flops=COST, bytes_accessed=COST, transcendentals=0
        ),
        name="table_grad",
    )(rel_1d, rel_x, rel_y, d_scores)


def spread(size, plan):
    found = []
    for whole in plan:
        at, pieces = 0, []
        for z, x, y, first, last in whole:
            rows = (last - first) * size // 2
            pieces.append((at, rows, z, x, y, first * size // 2))
            at += rows
        found.append(pieces)
    return found


def blocks(zs, x, y):
    return [(z, x, y, 0, 2) for z in zs]


ATTN_PLAN = spread(
    A_ROWS,
    [
        blocks(range(4), 0, 0),
        blocks(range(4), 1, 0),
        blocks(range(4), 0, 1),
        blocks((0, 1), 1, 1),
        blocks((2, 3), 1, 1),
    ],
)
FFN_PLAN = spread(
    F_ROWS,
    [
        blocks((0,), 0, 0),
        blocks((0,), 1, 0),
        blocks((0,), 0, 1),
        blocks((1, 2, 3), 0, 0),
        blocks((1, 2, 3), 1, 0),
        blocks((1, 2, 3), 0, 1),
        blocks((0, 1), 1, 1),
        blocks((2, 3), 1, 1),
    ],
)
A_COPIES = 2 * sum(len(pieces) for pieces in ATTN_PLAN)
F_COPIES = 2 * sum(len(pieces) for pieces in FFN_PLAN)


def joined(plan):
    start, found = 0, []
    for pieces in plan:
        found += [(start + first, *rest) for first, *rest in pieces]
        start += sum(piece[1] for piece in pieces)
    return [found]


ATTN_FAR, FFN_FAR = joined(ATTN_PLAN[:3]) + ATTN_PLAN[3:], FFN_PLAN


def piece_list(plans, refs):
    found = []
    for core, plan in enumerate(plans):
        for pieces, ref in zip(plan, refs[len(plans[0]) * core :]):
            for start, rows, z, x, y, offset in pieces:
                found.append((core, z, x, y, offset, rows, ref.at[pl.ds(start, rows), :]))
    return found


def qkv_kernel(at_ref, tok_ref, add_ref, *refs):
    qkv_ref, all_ref, weight_ref, sems, done = refs[len(ATTN_PLAN) + len(ATTN_FAR) :]
    copies = []
    for n, (core, z, x, y, offset, rows, ref) in enumerate(piece_list((ATTN_PLAN, ATTN_FAR), refs)):
        block = (
            ((at_ref[0] ^ z) * 2 + (at_ref[1] ^ x)) * 2 + (at_ref[2] ^ y)
        ) * 2 + (at_ref[3] ^ core)
        spot = pl.ds(pl.multiple_of(block * A_ROWS + offset, 16), rows)
        copies.append(pltpu.make_async_copy(ref, weight_ref.at[spot, :], sems.at[n]))
    for copy in copies:
        copy.start()
    for copy in copies:
        copy.wait()
    store = pltpu.make_async_copy(weight_ref, all_ref, done)
    store.start()
    for t in range(3):
        part = slice(D * t, D * t + D)
        qkv_ref[:, part] = (mm(tok_ref[...], weight_ref[part, :], NN) + add_ref[:, part]).astype(BF)
    store.wait()


def project(at, tokens, add_three, pieces):
    count = tokens.shape[0]
    vmem = pl.BlockSpec(memory_space=pltpu.VMEM)
    return pl.pallas_call(
        qkv_kernel,
        in_specs=[pl.BlockSpec(memory_space=pltpu.SMEM), vmem, vmem] + [ANY] * len(pieces),
        out_specs=[vmem, ANY],
        out_shape=[
            jax.ShapeDtypeStruct((count, 3 * D), BF),
            jax.ShapeDtypeStruct((4 * D, D), BF),
        ],
        scratch_shapes=[
            pltpu.VMEM((4 * D, D), BF),
            pltpu.SemaphoreType.DMA((A_COPIES,)),
            pltpu.SemaphoreType.DMA,
        ],
        cost_estimate=pl.CostEstimate(
            flops=COST, bytes_accessed=COST, transcendentals=0
        ),
        name="project",
    )(at, tokens, add_three, *pieces)


def grad_ffn_kernel(at_ref, *refs, high):
    wide, slim, outs, (left, right, sems) = refs[:4], refs[4:8], refs[8:11], refs[11:]
    which = (at_ref[0] // 2) ^ high
    for w in range(2):

        @pl.when(which == w)
        def _():
            copies = []
            for i in range(2):
                rows = pl.ds(SEQ * i, SEQ)
                copies.append(
                    pltpu.make_async_copy(wide[2 * w + i], left.at[rows, :], sems.at[2 * i])
                )
                copies.append(
                    pltpu.make_async_copy(slim[2 * w + i], right.at[rows, :], sems.at[2 * i + 1])
                )
            for copy in copies:
                copy.start()
            for copy in copies:
                copy.wait()

    own, kept, sent = outs
    for z in range(2):
        done = mm(left[:, HALF // 2 * z : HALF // 2 * (z + 1)], right[...], TN).astype(BF)
        rows = [done[F_ROWS * q : F_ROWS * q + F_ROWS, :] for q in range(4)]
        own[z] = rows[0]
        kept[z] = rows[1 if high else 2]
        sent[z] = rows[3]
        sent[2 + z] = rows[2 if high else 1]


def grad_ffn(at, wide, slim, high):
    shape = lambda n: jax.ShapeDtypeStruct((n, F_ROWS, D), BF)
    return pl.pallas_call(
        lambda *refs: grad_ffn_kernel(*refs, high=high),
        in_specs=[pl.BlockSpec(memory_space=pltpu.SMEM)] + [ANY] * 8,
        out_specs=[pl.BlockSpec(memory_space=pltpu.VMEM)] * 3,
        out_shape=[shape(2), shape(2), shape(4)],
        scratch_shapes=[
            pltpu.VMEM((2 * SEQ, HALF), BF),
            pltpu.VMEM((2 * SEQ, D), BF),
            pltpu.SemaphoreType.DMA((4,)),
        ],
        cost_estimate=pl.CostEstimate(
            flops=COST, bytes_accessed=COST, transcendentals=0
        ),
        name="grad_ffn",
    )(at, *wide, *slim)


def grad_attn_kernel(at_ref, tok_ref, tok_far, ctx_ref, ctx_far, *refs):
    grads, outs, (flip, left, right, sems) = refs[:8], refs[8:14], refs[14:]
    copies = []
    for t in range(4):
        for i in range(2):
            spot = right.at[t, pl.ds(SEQ * i, SEQ), :]
            copies.append(pltpu.make_async_copy(grads[2 * t + i], spot, sems.at[2 * t + i]))
    for copy in copies:
        copy.start()
    for n, (near, far) in enumerate(((tok_ref, tok_far), (ctx_ref, ctx_far))):
        flip[:, :SEQ] = near[...].astype(F32).T.astype(BF)
        flip[:, SEQ:] = far[...].astype(F32).T.astype(BF)
        for q in range(4):
            block = (((at_ref[1] ^ (q // 2)) * 2 + (at_ref[2] ^ (q % 2))) * 2) + at_ref[3]
            spot = pl.ds(pl.multiple_of(block * A_ROWS, A_ROWS), A_ROWS)
            left[n, A_ROWS * q : A_ROWS * q + A_ROWS, :] = flip[spot, :]
    for copy in copies:
        copy.wait()
    for z in range(4):
        which = at_ref[0] ^ z
        done = mm(left[which // 3], right[which], NN).astype(BF)
        rows = [done[A_ROWS * q : A_ROWS * q + A_ROWS, :] for q in range(4)]
        own, kept, sent = outs[3 * (z // 2) : 3 * (z // 2) + 3]
        own[z % 2] = rows[0]
        kept[z % 2] = rows[1 if z // 2 else 2]
        sent[z % 2] = rows[3]
        sent[2 + z % 2] = rows[2 if z // 2 else 1]


def grad_attn(at, tokens, tokens_far, ctx, ctx_far, grads):
    shape = lambda n: jax.ShapeDtypeStruct((n, A_ROWS, D), BF)
    vmem = pl.BlockSpec(memory_space=pltpu.VMEM)
    return pl.pallas_call(
        grad_attn_kernel,
        in_specs=[pl.BlockSpec(memory_space=pltpu.SMEM)] + [vmem] * 4 + [ANY] * 8,
        out_specs=[vmem] * 6,
        out_shape=[shape(2), shape(2), shape(4)] * 2,
        scratch_shapes=[
            pltpu.VMEM((D, 2 * SEQ), BF),
            pltpu.VMEM((2, D // 2, 2 * SEQ), BF),
            pltpu.VMEM((4, 2 * SEQ, D), BF),
            pltpu.SemaphoreType.DMA((8,)),
        ],
        cost_estimate=pl.CostEstimate(
            flops=COST, bytes_accessed=COST, transcendentals=0
        ),
        name="grad_attn",
    )(at, tokens, tokens_far, ctx, ctx_far, *grads)


def row_mean(values):
    return jnp.mean(values, axis=-1, keepdims=True)


def normal_rows(values):
    center = values - row_mean(values)
    inv = lax.rsqrt(row_mean(center * center) + NORM_EPS)
    return center * inv, inv


def normal_back(normal, inv, grad):
    return inv * (grad - row_mean(grad) - normal * row_mean(grad * normal))


def gelu_parts(u):
    z = jnp.abs(u) * (2.0**-0.5)
    t = 1.0 / (1.0 + 0.3275911 * z)
    tail = jnp.exp(-0.5 * u * u)
    poly = t * (
        0.254829592
        + t * (-0.284496736 + t * (1.421413741 + t * (-1.453152027 + t * 1.061405429)))
    )
    half = 0.5 * poly * tail
    cdf = jnp.where(u < 0, half, 1.0 - half)
    return u * cdf, cdf + u * (tail * (1.0 / math.sqrt(2.0 * math.pi)))


def row_sum(values):
    return jnp.sum(values.astype(F32), axis=0, keepdims=True)


def block_kernel(
    at_ref,
    ctx_ref,
    tok_ref,
    cot_ref,
    vec_ref,
    b1_ref,
    wo_ref,
    *refs,
    wide,
):
    split = len(FFN_PLAN) + len(FFN_FAR)
    pieces, refs = refs[:split], refs[split:]
    out_ref, hid_ref, act_near, act_far, dff_ref, du_near, du_far = refs[:7]
    dr_ref, dab_ref, dctx_ref, sum_ref, db1_ref, slope_ref, ffn_ref, sems = refs[7:]
    copies = []
    for n, (core, z, x, y, offset, rows, ref) in enumerate(piece_list((FFN_PLAN, FFN_FAR), pieces)):
        spot = pl.ds(core * HALF + ((z % 2) * 4 + x * 2 + y) * F_ROWS + offset, rows)
        which = (at_ref[0] // 2) ^ (z // 2)
        copies.append(pltpu.make_async_copy(ref, ffn_ref.at[which, spot, :], sems.at[n]))
    w1_ref, w2_ref = ffn_ref.at[0], ffn_ref.at[1]

    @pl.when(pl.program_id(0) == 0)
    def _():
        for copy in copies:
            copy.start()
        sum_ref[...] = jnp.zeros_like(sum_ref)
        db1_ref[...] = jnp.zeros_like(db1_ref)

    vec = [vec_ref[i : i + 1, :] for i in range(8)]
    resid = tok_ref[...].astype(F32) + (mm(ctx_ref[...], wo_ref[...], NN) + vec[6])
    n_one, inv_one = normal_rows(resid)
    hidden = n_one * vec[0] + vec[1]
    hid_low = hidden.astype(BF)
    hid_ref[...] = hid_low
    total = hidden + vec[7]

    @pl.when(pl.program_id(0) == 0)
    def _():
        for copy in copies:
            copy.wait()

    for f in range(0, FF, wide):
        part = slice(f, f + wide)
        u = mm(hid_low, w1_ref[part, :], NT) + b1_ref[:, part]
        act, slope = gelu_parts(u)
        act = act.astype(BF)
        side = slice(f % HALF, f % HALF + wide)
        (act_near if f < HALF else act_far)[:, side] = act
        slope_ref[:, part] = slope
        total = total + mm(act, w2_ref[part, :], NN)
    n_two, inv_two = normal_rows(total)
    out_ref[...] = (n_two * vec[2] + vec[3]).astype(BF)
    dy = cot_ref[...].astype(F32)
    d_two = normal_back(n_two, inv_two, dy * vec[2])
    dff = d_two.astype(BF)
    dff_ref[...] = dff
    d_hid = d_two
    for f in range(0, FF, wide):
        part = slice(f, f + wide)
        du = (mm(dff, w2_ref[part, :], NT) * slope_ref[:, part]).astype(BF)
        side = slice(f % HALF, f % HALF + wide)
        (du_near if f < HALF else du_far)[:, side] = du
        db1_ref[:, part] += row_sum(du)
        d_hid = d_hid + mm(du, w1_ref[part, :], NN)
    d_one = normal_back(n_one, inv_one, d_hid * vec[0])
    dr_ref[...] = d_one
    dab = d_one.astype(BF)
    dab_ref[...] = dab
    dctx_ref[...] = mm(dab, wo_ref[...], NT).astype(BF)
    sum_ref[...] += jnp.concatenate(
        [
            row_sum(d_hid * n_one),
            row_sum(d_hid),
            row_sum(dy * n_two),
            row_sum(dy),
            jnp.zeros((2, D), F32),
            row_sum(dab),
            row_sum(dff),
        ],
        axis=0,
    )


def block_pass(at, ctx, tokens, cotangent, vectors, b_first, attn_full, pieces):
    rows = 256
    by_row = lambda width: pl.BlockSpec((rows, width), lambda i, *_: (i, 0))
    whole = lambda shape, first=0: pl.BlockSpec(
        shape, lambda i, *_: (first, 0), pipeline_mode=pl.Buffered(1)
    )
    count = tokens.shape[0]
    low = lambda width: jax.ShapeDtypeStruct((count, width), BF)
    return pl.pallas_call(
        lambda *refs: block_kernel(*refs, wide=768),
        grid_spec=pltpu.PrefetchScalarGridSpec(
            num_scalar_prefetch=1,
            grid=(count // rows,),
            in_specs=[
                by_row(D),
                by_row(D),
                by_row(D),
                whole((12, D)),
                whole((1, FF)),
                whole((D, D), 3),
            ]
            + [ANY] * len(pieces),
            out_specs=[
                by_row(D),
                by_row(D),
                by_row(HALF),
                by_row(HALF),
                by_row(D),
                by_row(HALF),
                by_row(HALF),
                by_row(D),
                by_row(D),
                by_row(D),
                pl.BlockSpec((8, D), lambda i, *_: (0, 0)),
                pl.BlockSpec((1, FF), lambda i, *_: (0, 0)),
            ],
            scratch_shapes=[
                pltpu.VMEM((rows, FF), F32),
                pltpu.VMEM((2, FF, D), BF),
                pltpu.SemaphoreType.DMA((F_COPIES,)),
            ],
        ),
        out_shape=[
            low(D),
            low(D),
            low(HALF),
            low(HALF),
            low(D),
            low(HALF),
            low(HALF),
            jax.ShapeDtypeStruct((count, D), F32),
            low(D),
            low(D),
            jax.ShapeDtypeStruct((8, D), F32),
            jax.ShapeDtypeStruct((1, FF), F32),
        ],
        cost_estimate=pl.CostEstimate(
            flops=COST, bytes_accessed=COST, transcendentals=0
        ),
        name="block_pass",
    )(at, ctx, tokens, cotangent, vectors, b_first, attn_full, *pieces)


def swap(array, mask):
    return lax.ppermute(array, ALL, [(i, i ^ mask) for i in range(BLOCKS)])


def together(*groups):
    return lax.optimization_barrier(groups)


def tie(arrays, after):
    return lax.optimization_barrier((arrays, after))[0]


def column(shard, zs):
    return jnp.concatenate([shard if z == 0 else swap(shard, 8 * z) for z in zs])


def gather_full(shard, plans):
    full = lax.all_gather(shard, ALL, axis=0, tiled=True)
    view = full.reshape(*SPLIT, full.shape[0] // BLOCKS, D)
    return tuple(
        jnp.concatenate([view[z, x, y, core, off : off + n] for _, n, z, x, y, off in pieces])
        for core, plan in enumerate(plans)
        for pieces in plan
    )


def wide(array):
    return array.astype(F32)


def scatter_first(low, high):
    return swap(low[2], 2), swap(high[2], 4)


def scatter_sums(low, high, from_y, from_x):
    to_x = (wide(low[1]) + wide(from_y[:2])).astype(BF)
    to_y = (wide(high[1]) + wide(from_x[:2])).astype(BF)
    return to_x, to_y


def scatter_second(to_x, to_y):
    return swap(to_x, 4), swap(to_y, 2)


def scatter_third(low, high, from_y, from_x, last_x, last_y):
    low = wide(low[0]) + wide(from_y[2:]) + wide(last_x)
    high = wide(high[0]) + wide(from_x[2:]) + wide(last_y)
    send = (low[1].astype(BF), high[0].astype(BF), high[1].astype(BF))
    return low[0], tuple(swap(a, 8 * z) for z, a in zip((1, 2, 3), send))


def scatter_full(sides):
    cores = []
    for low, high in sides:
        rows = [(low[0], high[0]), (low[2][2:], high[1]), (low[1], high[2][2:])]
        rows.append((low[2][:2], high[2][:2]))
        cores.append(jnp.stack([jnp.concatenate(pair) for pair in rows], axis=1))
    full = jnp.stack(cores, axis=2).reshape(-1, D)
    return lax.psum_scatter(full, ALL, scatter_dimension=0, tiled=True).astype(F32)


def flip_bits(array, at):
    for axis, bit in enumerate((at[0] % 2, at[1], at[2], at[3])):
        array = jnp.where(bit == 1, jnp.flip(array, axis), array)
    return array


LANES = 256


def pack_table(grad):
    return jnp.pad(grad, ((0, 0), (0, LANES - BUCKETS))).reshape(H * LANES // D, D)


def update_kernel(total_ref, attn_sum, ffn_sum, *refs):
    states, outs = [refs[4 * i : 4 * i + 4] for i in range(4)], refs[16:]
    per = D // LANES
    vec_total = total_ref[:H, :]
    heads = jnp.concatenate(
        [
            total_ref[H + h // per : H + h // per + 1, LANES * (h % per) : LANES * (h % per + 1)]
            for h in range(H)
        ],
        axis=0,
    )
    square = total_ref[H : H + 1, LANES - 1 : LANES]
    lane = lax.broadcasted_iota(jnp.int32, heads.shape, 1)
    tab_total = jnp.where(lane < BUCKETS, heads, 0.0)
    rows = jnp.sum(tab_total * tab_total, axis=0, keepdims=True)
    square = square + jnp.sum(rows, axis=1, keepdims=True)
    rows = jnp.sum(vec_total * vec_total, axis=0, keepdims=True)
    norm = jnp.sqrt(square + jnp.sum(rows, axis=1, keepdims=True))
    scale = 1.0 / jnp.maximum(norm, 1.0)
    outs[0][...] = norm
    outs[1][...] = vec_total * scale
    totals = (attn_sum[...], ffn_sum[...], vec_total, heads[:H, :BUCKETS])
    for i, (state, total) in enumerate(zip(states, totals)):
        rate, decay = (0.06, 0.01) if i < 2 else (0.6, 0.0)
        weight, first, second, average = (ref[...] for ref in state)
        new = adam_update(weight, first, second, total, scale, rate, decay, average)
        for out, value in zip(outs[2 + 4 * i :], new):
            out[...] = value


def update(total, attn_sum, ffn_sum, states):
    like = lambda a: jax.ShapeDtypeStruct(a.shape, F32)
    one = jax.ShapeDtypeStruct((1, 1), F32)
    steps = 1
    whole = lambda shape: pl.BlockSpec(shape, lambda i: (0, 0))
    part = lambda a: pl.BlockSpec((a.shape[0] // steps, D), lambda i: (i, 0))
    states_specs = [part(a) for a in states[:8]] + [whole(a.shape) for a in states[8:]]
    return pl.pallas_call(
        update_kernel,
        grid=(steps,),
        in_specs=[whole(total.shape), part(attn_sum), part(ffn_sum)] + states_specs,
        out_specs=[whole((1, 1)), whole(states[8].shape)] + states_specs,
        out_shape=[one, like(states[8])] + [like(a) for a in states],
        name="update",
    )(total, attn_sum, ffn_sum, *states)


def hidden_bias(vectors, at):
    flipped = flip_bits(vectors[8:].reshape(2, 2, 2, 2, F_ROWS), at)
    return flipped.transpose(3, 0, 1, 2, 4).reshape(1, FF)


def input_grad(start, d_three, attn_full, which=(0, 1, 2)):
    for t in which:
        start = start + mm(d_three[t], attn_full[D * t : D * t + D], NT)
    return start


def shards(
    tokens,
    cotangent,
    lengths,
    rel_1d,
    rel_x,
    rel_y,
    attn_weights,
    attn_m1,
    attn_m2,
    attn_ema,
    ffn_weights,
    ffn_m1,
    ffn_m2,
    ffn_ema,
    vectors,
    vec_m1,
    vec_m2,
    vec_ema,
    table,
    tab_m1,
    tab_m2,
    tab_ema,
    *,
    direct,
):
    attn_low, ffn_low = attn_weights.astype(BF), ffn_weights.astype(BF)
    rel = (rel_1d, rel_x, rel_y)
    tab = bias_lines(table)
    add_three = jnp.concatenate([vectors[4], jnp.zeros((D,), F32), vectors[5]]).reshape(1, 3 * D)
    if direct:
        dp, fsdp = lax.axis_index("dp"), lax.axis_index("fsdp")
        at = jnp.stack([dp // 2, dp % 2, fsdp // 2, fsdp % 2]).astype(jnp.int32)
        far = lambda a: swap(a, 1)
        b_first = hidden_bias(vectors, at)
        attn_column = column(attn_low, range(4))
        ffn_x, ffn_y = swap(ffn_low, 4), swap(ffn_low, 2)
        bias = page_bias(lengths, tab, rel, 0, None)
        attn_column, ffn_x, ffn_y, later, bias, at, b_first, add_three = together(
            attn_column, ffn_x, ffn_y, ffn_low, bias, at, b_first, add_three
        )
        beside, above = swap(attn_column, 4), swap(attn_column, 2)
        ffn_column = column(later, (1, 2, 3))
        bias = page_bias(lengths, tab, rel, 1, bias)
        beside, above, bias = together(beside, above, bias)
        near, ffn_column, bias = together((attn_column, beside, above), ffn_column, bias)
        side = 2 * A_ROWS
        low, high = swap(near[1][:side], 2), swap(near[2][side:], 4)
        beside, above = swap(ffn_column, 4), swap(ffn_column, 2)
        away = swap(jnp.concatenate(near), 1)
        bias = page_bias(lengths, tab, rel, 2, bias)
        last, away, bias, start = together((low, high), away, bias, (ffn_low, ffn_x, ffn_y))
        attn_pieces = near + last + (away,) + tuple(swap(piece, 1) for piece in last)
        first = tuple(swap(piece, 1) for piece in start)
        qkv, attn_full = project(at, tokens, add_three, attn_pieces)
        first, beside, above, qkv = together(first, beside, above, qkv)
        low = swap(jnp.concatenate([start[1], beside[:F_ROWS]]), 2)
        high = swap(above[F_ROWS:], 4)
        middle = (ffn_column, beside, above)
        away = tuple(swap(piece, 1) for piece in middle)
        ctx, soft = attend(qkv, bias)
        last, away, ctx = together((low, high), away, ctx)
        ffn_pieces = start + middle + last + first + away + tuple(swap(a, 1) for a in last)
    else:
        at = jnp.zeros((4,), jnp.int32)
        b_first = hidden_bias(vectors, at)
        far = jnp.zeros_like
        bias = None
        for part in range(len(BIAS_ROWS)):
            bias = page_bias(lengths, tab, rel, part, bias)
        attn_pieces = gather_full(attn_low, (ATTN_PLAN, ATTN_FAR))
        ffn_pieces = gather_full(ffn_low, (FFN_PLAN, FFN_FAR))
        qkv, attn_full = project(at, tokens, add_three, attn_pieces)
        ctx, soft = attend(qkv, bias)
        tokens_far, ctx_far = far(tokens), far(ctx)
    (
        block_out,
        hid,
        act_near,
        act_away,
        d_ffn,
        du_near,
        du_away,
        d_resid_one,
        d_attn,
        d_context,
        sums,
        grad_bias_first,
    ) = block_pass(at, ctx, tokens, cotangent, vectors, b_first, attn_full, ffn_pieces)
    away = (far(du_away), far(act_away), far(hid), far(d_ffn), far(d_attn))
    dq, dk, dv, d_scores, qv_sums = attend_back(qkv, soft, ctx, d_context)
    d_three = (dq, dk, dv)
    if direct:
        away, d_three, d_scores, rows = together(away, d_three, d_scores, (tokens, ctx))
        du_far, act_far, hid_far, d_ffn_far, d_attn_far = away
        wide_ones, slim = (du_near, du_far, act_near, act_far), (hid, hid_far, d_ffn, d_ffn_far)
        low = grad_ffn(at, wide_ones, slim, 0)
        three_far = tuple(far(d) for d in d_three + rows)
        low, three_far, wide_ones = together(low, three_far, wide_ones)
        high = grad_ffn(at, wide_ones, slim, 1)
        grads = [g for pair in zip(d_three, three_far[:3]) for g in pair] + [d_attn, d_attn_far]
        high, grads = together(high, grads)
        ffn_first = scatter_first(low, high)
        parts = grad_attn(at, tokens, three_far[3], ctx, three_far[4], grads)
        parts, d_scores = together(parts, d_scores)
        attn_first = scatter_first(parts[:3], parts[3:])
        tables = [table_grad(*rel, d_scores, 0)]
        ffn_first, d_scores, tables[0] = together(ffn_first, d_scores, tables[0])
        ffn_second = scatter_second(*scatter_sums(low, high, *ffn_first))
        tables.append(table_grad(*rel, d_scores, 1))
        attn_first, ffn_second, d_three, tables[1] = together(
            attn_first, ffn_second, d_three, tables[1]
        )
        ffn_own, ffn_three = scatter_third(low, high, *ffn_first, *ffn_second)
        sent, d_three = together(scatter_sums(parts[:3], parts[3:], *attn_first), d_three)
        attn_second = scatter_second(*sent)
        late = (sums, qv_sums, grad_bias_first, tables, d_three)
        attn_second, late = together(attn_second, late)
        sums, qv_sums, grad_bias_first, tables, d_three = late
        grad_input = input_grad(d_resid_one, d_three, attn_full)
        attn_own, attn_three = scatter_third(parts[:3], parts[3:], *attn_first, *attn_second)
        ffn_shard = sum((wide(a) for a in ffn_three), ffn_own)
        attn_shard = sum((wide(a) for a in attn_three), attn_own)
    else:
        sides, attn_sides = [], []
        grads = [g for d in (*d_three, d_attn) for g in (d, far(d))]
        slim = (hid, far(hid), d_ffn, far(d_ffn))
        for core, (du, act) in enumerate(((du_near, act_near), (du_away, act_away))):
            wide_ones = (du, far(du), act, far(act))
            sides.append([grad_ffn(at, wide_ones, slim, side) for side in range(2)])
            spot = at.at[3].set(core)
            parts = grad_attn(spot, tokens, tokens_far, ctx, ctx_far, grads)
            attn_sides.append((parts[:3], parts[3:]))
        ffn_shard, attn_shard = scatter_full(sides), scatter_full(attn_sides)
        tables = [table_grad(*rel, d_scores, part) for part in range(PARTS)]
        grad_input = input_grad(d_resid_one, d_three, attn_full)
    grad_table = pack_table(sum(tables[1:], tables[0]))
    grad_bias_first = grad_bias_first.reshape(2, 2, 2, 2, F_ROWS).transpose(1, 2, 3, 0, 4)
    grad_bias_first = flip_bits(grad_bias_first, at).reshape(FF // D, D)
    small = jnp.concatenate([sums[:4], qv_sums[:2], sums[6:], grad_bias_first, grad_table], axis=0)
    squares = jnp.sum(attn_shard * attn_shard) + jnp.sum(ffn_shard * ffn_shard)
    row = lax.broadcasted_iota(jnp.int32, small.shape, 0)
    lane = lax.broadcasted_iota(jnp.int32, small.shape, 1)
    small = jnp.where((row == H) & (lane == LANES - 1), squares, small)
    if direct:
        for mask in (1, 2, 4, 8, 16):
            small = small + swap(small, mask)
    else:
        small = lax.psum(small, ALL)
    states = (attn_weights, attn_m1, attn_m2, attn_ema, ffn_weights, ffn_m1, ffn_m2, ffn_ema)
    states += (vectors, vec_m1, vec_m2, vec_ema, table.T, tab_m1.T, tab_m2.T, tab_ema.T)
    grad_norm, vec_grad, *new = update(small, attn_shard, ffn_shard, states)
    new = new[:12] + [array.T for array in new[12:]]
    return (block_out, grad_input, grad_norm.reshape(()), *new, vec_grad)


def solution(mesh):
    direct = mesh.shape["dp"] == SPLIT[0] * SPLIT[1] and mesh.shape["fsdp"] == SPLIT[2] * SPLIT[3]
    return jax.shard_map(
        lambda *arrays: shards(*arrays, direct=direct),
        mesh=mesh,
        in_specs=(
            P(("dp", "fsdp"), None),
            P(("dp", "fsdp"), None),
            P(("dp", "fsdp")),
            P(("dp", "fsdp"), None, None),
            P(("dp", "fsdp"), None, None),
            P(("dp", "fsdp"), None, None),
            P(("dp", "fsdp"), None),
            P(("dp", "fsdp"), None),
            P(("dp", "fsdp"), None),
            P(("dp", "fsdp"), None),
            P(("dp", "fsdp"), None),
            P(("dp", "fsdp"), None),
            P(("dp", "fsdp"), None),
            P(("dp", "fsdp"), None),
            P(),
            P(),
            P(),
            P(),
            P(),
            P(),
            P(),
            P(),
        ),
        out_specs=(
            P(("dp", "fsdp"), None),
            P(("dp", "fsdp"), None),
            P(),
            P(("dp", "fsdp"), None),
            P(("dp", "fsdp"), None),
            P(("dp", "fsdp"), None),
            P(("dp", "fsdp"), None),
            P(("dp", "fsdp"), None),
            P(("dp", "fsdp"), None),
            P(("dp", "fsdp"), None),
            P(("dp", "fsdp"), None),
            P(),
            P(),
            P(),
            P(),
            P(),
            P(),
            P(),
            P(),
            P(),
        ),
        check_vma=False,
    )
```
